128 devices in a mesh: req: 32 (over y, x, core), mdl: 4 (over z).
Axes of the slice: x: 4, y: 4, z: 4, core: 2. Of those that a mesh axis runs over, the one named last changes fastest.
Arguments:
- hidden_in: bfloat16 [256, 16, 2048], P('req'), may hold values from -6 to 6
- mixer_gain: bfloat16 [2048], replicated, may hold values from 0.5 to 1.5
- w_query: bfloat16 [2048, 1024], P(None, 'mdl'), may hold values from -0.125 to 0.125
- w_kv: bfloat16 [2, 2048, 256], replicated, may hold values from -0.125 to 0.125
- w_attn_out: bfloat16 [1024, 2048], P('mdl'), may hold values from -0.1875 to 0.1875
- prompt_kv: bfloat16 [64, 2, 1024, 256], P('req')
- prompt_lengths: int32 [64], P('req'), may hold values from 1 to 1024, as said below
- member: int32 [256], P('req'), may hold values from 0 to 1
- accepted: int32 [256], P('req'), may hold values from 1 to 16, as said below
- w_z: bfloat16 [2048, 1536], P(None, 'mdl'), may hold values from -0.125 to 0.125
- w_x: bfloat16 [2048, 1536], P(None, 'mdl'), may hold values from -0.125 to 0.125
- w_bc: bfloat16 [2048, 512], replicated, may hold values from -0.125 to 0.125
- w_dt: bfloat16 [2048, 24], P(None, 'mdl'), may hold values from -0.125 to 0.125
- conv_x: bfloat16 [4, 1536], P(None, 'mdl'), may hold values from -1.5 to 1.5
- conv_bc: bfloat16 [4, 512], replicated, may hold values from -1.5 to 1.5
- ssm_rate: float32 [24], P('mdl'), may hold values from 1 to 16
- dt_bias: float32 [24], P('mdl'), may hold values from -4 to 0.5
- skip_d: float32 [24], P('mdl'), may hold values from 0.5 to 1.5
- prompt_state: float32 [64, 24, 64, 256], P('req', 'mdl'), may hold values from -0.4 to 0.4
- prompt_conv_x: bfloat16 [64, 3, 1536], P('req', None, 'mdl'), may hold values from -6 to 6
- prompt_conv_bc: bfloat16 [64, 3, 512], P('req'), may hold values from -6 to 6
- w_mamba_out: bfloat16 [1536, 2048], P('mdl'), may hold values from -0.15625 to 0.15625
- mlp_gain: bfloat16 [2048], replicated, may hold values from 0.5 to 1.5
- w_gate: bfloat16 [2048, 4096], P(None, 'req'), may hold values from -0.125 to 0.125
- w_up: bfloat16 [2048, 4096], P(None, 'req'), may hold values from -0.125 to 0.125
- w_down: bfloat16 [4096, 2048], P('req'), may hold values from -0.09375 to 0.09375
- final_gain: bfloat16 [2048], replicated, may hold values from 0.5 to 1.5
- head_weight: bfloat16 [32768, 2048], P('req')
- draft_ids: int32 [256, 16], replicated, may hold values from 0 to 32767
Outputs:
- hidden_out: bfloat16 [256, 16, 2048], P(('req', 'mdl'))
- verify_scores: float32 [256, 16], P(('req', 'mdl'))
- kept_state: float32 [256, 24, 64, 256], P(('req', 'mdl'))
- kept_conv: bfloat16 [256, 3, 2048], P(('req', 'mdl'))
The draws below stay inside these ranges and needn't reach their ends.
Inputs may be any that keep to these rules, and one draw needn't show every extreme that they name: Each request has accepted 1 to 16 drafts; both ends occur in every draw. `prompt_lengths`: a prompt of 1024 tokens occurs in every draw. `member`: index of the request's prompt among the 2 prompts of its block of 8 requests.
All inputs are finite; a program needn't handle non-finite values.
Results may differ from the reference program's by a relative error of at most 0.017.
Values may be sent and summed in bfloat16 or wider, within the bound.
No kernel may reach another device: no remote copies, remote signals or barrier semaphores. Data moves between devices by JAX's collectives and lax.ppermute only.
A program may use at most 128 MiB of HBM per device.

```python
import math
import jax
import jax.numpy as jnp
from jax import lax

D = 2048
FF = 4096
VOCAB = 32768
Q_HEADS = 8
KV_HEADS = 2
HEAD_DIM = 128
SSM_HEADS = 24
SSM_DIM = 64
STATE = 256
CONV = 4
DRAFT = 16
PROMPTS = 2
P_MAX = 1024
ROW_REQ = 8
REQS = 256
NPROMPT = 64
TOKENS = 4096
SSM_INNER = 1536
N_REQ = 32


def draw_prompt_kv(key, part):
    values = jax.random.normal(key, (NPROMPT, KV_HEADS, P_MAX, 2 * HEAD_DIM), jnp.float32)
    return values.astype(jnp.bfloat16)


def draw_head_weight(key, part):
    values = jax.random.normal(key, (VOCAB, D), jnp.float32) * (3.0 / math.sqrt(D))
    return values.astype(jnp.bfloat16)


def draw_accepted(key, part):
    values = jax.random.randint(key, (REQS,), 1, DRAFT + 1)
    return values.at[0].set(DRAFT).at[1].set(1).astype(jnp.int32)


def draw_prompt_lengths(key, part):
    values = jax.random.randint(key, (NPROMPT,), 1, P_MAX + 1)
    return values.at[0].set(P_MAX).astype(jnp.int32)


def with_ends(array, key, least, top_value):
    longest = array.shape.index(max(array.shape))
    spots = []
    for shift in (0, 1):
        where = [jax.random.randint(jax.random.fold_in(key, axis), (), 0, length) for axis, length in enumerate(array.shape)]
        where[longest] = (where[longest] + shift) % array.shape[longest]
        spots.append(tuple(where))
    return array.at[spots[0]].set(least).at[spots[1]].set(top_value)


def steps_of(key, shape, shards, low, largest):
    level = 1.0
    for axis_at, blocks in shards:
        draws = jax.random.uniform(jax.random.fold_in(jax.random.fold_in(key, 6), axis_at), (blocks,), jnp.float32, low / len(shards), largest / len(shards))
        level = level * jnp.repeat(jnp.exp(draws), shape[axis_at] // blocks).reshape((-1,) + (1,) * (len(shape) - 1 - axis_at))
    return level


def scatter_about(rng, shape, scale, reach, split=(), held_as=jnp.bfloat16):
    entries = scale * jax.random.normal(rng, shape, jnp.float32)
    if split:
        entries = entries * steps_of(rng, shape, split, -0.22, 0.18)
    return jnp.clip(entries, -reach, reach).astype(held_as)


def setup_inputs(seed: int = 0) -> dict:
    streams_of = jax.random.split(jax.random.key(seed), 30)
    hidden_in = scatter_about(streams_of[0], (REQS, DRAFT, D), 1.0, 6.0, ((0, 32),))
    mixer_gain = jnp.clip(1.0 + 0.1 * jax.random.normal(streams_of[1], (D,), jnp.float32), 0.5, 1.5).astype(jnp.bfloat16)
    w_query = scatter_about(streams_of[2], (D, Q_HEADS * HEAD_DIM), D ** -0.5, 0.125, ((1, 4),))
    w_kv = scatter_about(streams_of[3], (KV_HEADS, D, 2 * HEAD_DIM), D ** -0.5, 0.125)
    w_attn_out = scatter_about(streams_of[4], (Q_HEADS * HEAD_DIM, D), (Q_HEADS * HEAD_DIM) ** -0.5, 0.1875, ((0, 4),))
    prompt_kv = draw_prompt_kv(jax.random.fold_in(streams_of[29], 71), 0)
    prompt_lengths = draw_prompt_lengths(jax.random.fold_in(streams_of[29], 71), 0)
    member = with_ends(jax.random.randint(streams_of[7], (REQS,), 0, PROMPTS), jax.random.fold_in(streams_of[7], 1), 0, PROMPTS - 1).astype(jnp.int32)
    accepted = draw_accepted(jax.random.fold_in(streams_of[29], 71), 0)
    w_z = scatter_about(streams_of[9], (D, SSM_INNER), D ** -0.5, 0.125, ((1, 4),))
    w_x = scatter_about(streams_of[10], (D, SSM_INNER), D ** -0.5, 0.125, ((1, 4),))
    w_bc = scatter_about(streams_of[11], (D, 2 * STATE), D ** -0.5, 0.125)
    w_dt = scatter_about(streams_of[12], (D, SSM_HEADS), D ** -0.5, 0.125, ((1, 4),))
    conv_x = scatter_about(streams_of[13], (CONV, SSM_INNER), 0.25, 1.5, ((1, 4),))
    conv_bc = scatter_about(streams_of[14], (CONV, 2 * STATE), 0.25, 1.5)
    ssm_rate = jnp.clip(jnp.exp(math.log(16.0) - 2.7725887 * jax.random.uniform(streams_of[15], (SSM_HEADS,), jnp.float32) ** steps_of(streams_of[15], (SSM_HEADS,), ((0, 4),), -0.2, 0.2)), 1.0, 16.0)
    dt_bias = jnp.clip(-4.0 + 4.5 * jax.random.uniform(streams_of[16], (SSM_HEADS,), jnp.float32) ** steps_of(streams_of[16], (SSM_HEADS,), ((0, 4),), -0.2, 0.2), -4.0, 0.5)
    skip_d = jnp.clip(0.5 + 1.0 * jax.random.uniform(streams_of[17], (SSM_HEADS,), jnp.float32) ** steps_of(streams_of[17], (SSM_HEADS,), ((0, 4),), -0.2, 0.2), 0.5, 1.5)
    prompt_state = scatter_about(streams_of[18], (NPROMPT, SSM_HEADS, SSM_DIM, STATE), 0.05, 0.4, ((0, 32), (1, 4)), jnp.float32)
    prompt_conv_x = scatter_about(streams_of[19], (NPROMPT, CONV - 1, SSM_INNER), 1.0, 6.0, ((0, 32), (2, 4)))
    prompt_conv_bc = scatter_about(streams_of[20], (NPROMPT, CONV - 1, 2 * STATE), 1.0, 6.0, ((0, 32),))
    w_mamba_out = scatter_about(streams_of[21], (SSM_INNER, D), SSM_INNER ** -0.5, 0.15625, ((0, 4),))
    mlp_gain = jnp.clip(1.0 + 0.1 * jax.random.normal(streams_of[22], (D,), jnp.float32), 0.5, 1.5).astype(jnp.bfloat16)
    w_gate = scatter_about(streams_of[23], (D, FF), D ** -0.5, 0.125, ((1, 32),))
    w_up = scatter_about(streams_of[24], (D, FF), D ** -0.5, 0.125, ((1, 32),))
    w_down = scatter_about(streams_of[25], (FF, D), FF ** -0.5, 0.09375, ((0, 32),))
    final_gain = jnp.clip(1.0 + 0.1 * jax.random.normal(streams_of[26], (D,), jnp.float32), 0.5, 1.5).astype(jnp.bfloat16)
    head_weight = draw_head_weight(jax.random.fold_in(streams_of[29], 71), 0)
    draft_ids = with_ends(jax.random.randint(streams_of[28], (REQS, DRAFT), 0, VOCAB), jax.random.fold_in(streams_of[28], 1), 0, VOCAB - 1).astype(jnp.int32)
    return dict(hidden_in=hidden_in, mixer_gain=mixer_gain, w_query=w_query, w_kv=w_kv, w_attn_out=w_attn_out, prompt_kv=prompt_kv, prompt_lengths=prompt_lengths, member=member, accepted=accepted, w_z=w_z, w_x=w_x, w_bc=w_bc, w_dt=w_dt, conv_x=conv_x, conv_bc=conv_bc, ssm_rate=ssm_rate, dt_bias=dt_bias, skip_d=skip_d, prompt_state=prompt_state, prompt_conv_x=prompt_conv_x, prompt_conv_bc=prompt_conv_bc, w_mamba_out=w_mamba_out, mlp_gain=mlp_gain, w_gate=w_gate, w_up=w_up, w_down=w_down, final_gain=final_gain, head_weight=head_weight, draft_ids=draft_ids)


eps_norm = 1e-05
far_below = -1e+30

def rms_scale(values, gain):
    widened = values.astype(jnp.float32)
    spread = lax.optimization_barrier(jnp.mean(widened * widened, axis=-1, keepdims=True))
    return widened * lax.rsqrt(spread + eps_norm) * gain.astype(jnp.float32)

def convolve(series, kernel, length):
    summed = jnp.zeros(series.shape[:-2] + (length, series.shape[-1]), jnp.float32)
    for kernel_tap in range(kernel.shape[0]):
        window = lax.slice_in_dim(series, kernel_tap, kernel_tap + length, axis=series.ndim - 2)
        summed = summed + window * kernel[kernel_tap].astype(jnp.float32)
    return jax.nn.silu(summed)

def reference(hidden_in, mixer_gain, w_query, w_kv, w_attn_out, prompt_kv, prompt_lengths, member, accepted, w_z, w_x, w_bc, w_dt, conv_x, conv_bc, ssm_rate, dt_bias, skip_d, prompt_state, prompt_conv_x, prompt_conv_bc, w_mamba_out, mlp_gain, w_gate, w_up, w_down, final_gain, head_weight, draft_ids):
    flat_rows = hidden_in.reshape(TOKENS, D)
    normed = rms_scale(flat_rows, mixer_gain).astype(jnp.bfloat16)
    queries = jnp.dot(normed, w_query, preferred_element_type=jnp.float32).astype(jnp.bfloat16)
    queries = queries.reshape(REQS, DRAFT, Q_HEADS, HEAD_DIM)
    key_value = jnp.stack([jnp.dot(normed, w_kv[group_index], preferred_element_type=jnp.float32) for group_index in range(KV_HEADS)], axis=1).astype(jnp.bfloat16)
    key_value = key_value.reshape(REQS, DRAFT, KV_HEADS, 2 * HEAD_DIM)
    slots = (jnp.arange(REQS) // ROW_REQ * PROMPTS + member).astype(jnp.int32)
    gate_z = jnp.dot(normed, w_z, preferred_element_type=jnp.float32).astype(jnp.bfloat16).reshape(REQS, DRAFT, SSM_INNER)
    ssm_in = jnp.dot(normed, w_x, preferred_element_type=jnp.float32).astype(jnp.bfloat16).reshape(REQS, DRAFT, SSM_INNER)
    bc_in = jnp.dot(normed, w_bc, preferred_element_type=jnp.float32).astype(jnp.bfloat16).reshape(REQS, DRAFT, 2 * STATE)
    dt_in = jnp.dot(normed, w_dt, preferred_element_type=jnp.float32).astype(jnp.bfloat16).reshape(REQS, DRAFT, SSM_HEADS)
    per_group = Q_HEADS // KV_HEADS
    score_scale = HEAD_DIM ** (-0.5)
    causal_pairs = jnp.arange(DRAFT)[None, :] <= jnp.arange(DRAFT)[:, None]

    def one_request(inputs):
        query_r, kv_r, prompt_slot, accepted_r, gate_r, input_r, bc_r, dt_r = inputs
        prompt_slot = prompt_slot.astype(jnp.int32)
        accepted_r = accepted_r.astype(jnp.int32)
        cached = lax.dynamic_index_in_dim(prompt_kv, prompt_slot, 0, keepdims=False)
        length = lax.dynamic_index_in_dim(prompt_lengths, prompt_slot, 0, keepdims=False)
        cached_heads = jnp.repeat(cached, per_group, axis=0).astype(jnp.float32)
        draft_heads = jnp.repeat(kv_r, per_group, axis=1).astype(jnp.float32)
        query_wide = query_r.astype(jnp.float32)
        prompt_scores = jnp.einsum('thd,hkd->htk', query_wide, cached_heads[:, :, :HEAD_DIM]) * score_scale
        prompt_valid = (jnp.arange(P_MAX) < length)[None, None, :]
        draft_scores = jnp.einsum('thd,shd->hts', query_wide, draft_heads[:, :, :HEAD_DIM]) * score_scale
        draft_valid = causal_pairs[None]
        row_top = jnp.maximum(lax.optimization_barrier(jnp.max(jnp.where(prompt_valid, prompt_scores, far_below), axis=-1)), lax.optimization_barrier(jnp.max(jnp.where(draft_valid, draft_scores, far_below), axis=-1)))
        prompt_weights = jnp.exp(jnp.where(prompt_valid, prompt_scores - row_top[..., None], far_below))
        draft_weights = jnp.exp(jnp.where(draft_valid, draft_scores - row_top[..., None], far_below))
        weight_total = lax.optimization_barrier(jnp.sum(prompt_weights, axis=-1)) + lax.optimization_barrier(jnp.sum(draft_weights, axis=-1))
        rounded_prompt = lax.optimization_barrier(prompt_weights.astype(jnp.bfloat16)).astype(jnp.float32)
        rounded_draft = lax.optimization_barrier(draft_weights.astype(jnp.bfloat16)).astype(jnp.float32)
        weighted = jnp.einsum('htk,hke->hte', rounded_prompt, cached_heads[:, :, HEAD_DIM:])
        weighted = weighted + jnp.einsum('hts,she->hte', rounded_draft, draft_heads[:, :, HEAD_DIM:])
        attended = (weighted / weight_total[..., None]).astype(jnp.bfloat16)
        attended = attended.transpose(1, 0, 2).reshape(DRAFT, Q_HEADS * HEAD_DIM)
        start_x = lax.dynamic_index_in_dim(prompt_conv_x, prompt_slot, 0, keepdims=False).astype(jnp.float32)
        start_bc = lax.dynamic_index_in_dim(prompt_conv_bc, prompt_slot, 0, keepdims=False).astype(jnp.float32)
        series_x = jnp.concatenate([start_x, input_r.astype(jnp.float32)], axis=0)
        series_bc = jnp.concatenate([start_bc, bc_r.astype(jnp.float32)], axis=0)
        conv_xs = convolve(series_x, conv_x, DRAFT)
        conv_bcs = convolve(series_bc, conv_bc, DRAFT)
        b_part = conv_bcs[:, :STATE]
        c_part = conv_bcs[:, STATE:]
        step_size = jax.nn.softplus(dt_r.astype(jnp.float32) + dt_bias)
        decay = jnp.exp(-step_size * ssm_rate)
        heads_x = conv_xs.reshape(DRAFT, SSM_HEADS, SSM_DIM)
        initial = lax.dynamic_index_in_dim(prompt_state, prompt_slot, 0, keepdims=False)

        def advance(carried_state, inputs_now):
            decay_now, size_now, input_now, b_now, c_now = inputs_now
            carried_state = decay_now[:, None, None] * carried_state + size_now[:, None, None] * input_now[:, :, None] * b_now[None, None, :]
            output_now = jnp.einsum('hdn,n->hd', carried_state, c_now, precision=lax.Precision.HIGHEST) + skip_d[:, None] * input_now
            return (carried_state, (carried_state, output_now))
        last_state, (all_states, ssm_out) = lax.scan(advance, initial, (decay, step_size, heads_x, b_part, c_part))
        kept_state_r = lax.dynamic_index_in_dim(all_states, accepted_r - 1, 0, keepdims=False)
        gated = (ssm_out.reshape(DRAFT, SSM_INNER) * jax.nn.silu(gate_r.astype(jnp.float32))).astype(jnp.bfloat16)
        edge_rows = jnp.concatenate([series_x, series_bc], axis=1)
        kept_conv_r = lax.dynamic_slice_in_dim(edge_rows, accepted_r, CONV - 1, 0).astype(jnp.bfloat16)
        return (attended, gated, kept_state_r, kept_conv_r)
    attended_all, gated_all, kept_state, kept_conv = lax.map(one_request, (queries, key_value, slots, accepted, gate_z, ssm_in, bc_in, dt_in))
    mixer = jnp.dot(attended_all.reshape(TOKENS, Q_HEADS * HEAD_DIM), w_attn_out, preferred_element_type=jnp.float32)
    mixer = mixer + jnp.dot(gated_all.reshape(TOKENS, SSM_INNER), w_mamba_out, preferred_element_type=jnp.float32)
    after_mixer = (flat_rows.astype(jnp.float32) + mixer).astype(jnp.bfloat16)
    prepared = rms_scale(after_mixer, mlp_gain).astype(jnp.bfloat16)
    gate_val = jnp.dot(prepared, w_gate, preferred_element_type=jnp.float32)
    up_val = jnp.dot(prepared, w_up, preferred_element_type=jnp.float32)
    active = (jax.nn.silu(gate_val) * up_val).astype(jnp.bfloat16)
    block_units = FF // N_REQ

    def add_block(running_sum, block_index):
        first_unit = (block_index * block_units).astype(jnp.int32)
        active_block = lax.dynamic_slice_in_dim(active, first_unit, block_units, 1)
        down_block = lax.dynamic_slice_in_dim(w_down, first_unit, block_units, 0)
        feed_part = jnp.dot(active_block, down_block, preferred_element_type=jnp.float32)
        feed_part = lax.optimization_barrier(feed_part.astype(jnp.bfloat16)).astype(jnp.float32)
        return (running_sum + feed_part, None)
    feed_total, unused_out = lax.scan(add_block, jnp.zeros((TOKENS, D), jnp.float32), jnp.arange(N_REQ, dtype=jnp.int32))
    hidden_out = (after_mixer.astype(jnp.float32) + feed_total).astype(jnp.bfloat16)
    final_rows = rms_scale(hidden_out, final_gain).astype(jnp.bfloat16)
    next_ids = jnp.concatenate([draft_ids[:, 1:], draft_ids[:, :1]], axis=1).reshape(TOKENS).astype(jnp.int32)
    position = (jnp.arange(TOKENS) % DRAFT).astype(jnp.int32)
    block_rows = ROW_REQ * DRAFT

    def score_block(inputs):
        rows_block, ids_block, position_block = inputs
        logits = lax.dot_general(rows_block, head_weight, (((1,), (1,)), ((), ())), preferred_element_type=jnp.float32)
        logit_top = lax.optimization_barrier(jnp.max(logits, axis=1))
        log_total = logit_top + jnp.log(lax.optimization_barrier(jnp.sum(jnp.exp(logits - logit_top[:, None]), axis=1)))
        target = jnp.take_along_axis(logits, ids_block[:, None], axis=1)[:, 0]
        return jnp.where(position_block < DRAFT - 1, target - log_total, logit_top - log_total)
    verify_scores = lax.map(score_block, (final_rows.reshape(TOKENS // block_rows, block_rows, D), next_ids.reshape(TOKENS // block_rows, block_rows), position.reshape(TOKENS // block_rows, block_rows)))
    return (hidden_out.reshape(REQS, DRAFT, D), verify_scores.reshape(REQS, DRAFT), kept_state, kept_conv)
```

```python
import functools

import jax
import jax.numpy as jnp
import numpy as np
from jax import lax
from jax.experimental import pallas as pl
from jax.experimental.pallas import tpu as pltpu
from jax.sharding import PartitionSpec as P

Q_HEADS = 8
KV_HEADS = 2
HEAD_DIM = 128
SSM_DIM = 64
STATE = 256
CONV = 4
PROMPTS = 2
P_MAX = 1024
DRAFT = 16
SIDE = 4
CORES = 2

eps_norm = 1e-05
far_below = -1e30

HOPS = ((0, 1), (0, 3), (1, 0), (3, 0))
ORDERS = tuple(
    tuple(tuple(HOPS[(first + step) % 4] for step in range(4)) for first in firsts)
    for firsts in ((0, 1), (2, 3))
)


def device_at(y, x, core):
    return (y * SIDE + x) * CORES + core


def hop_pairs(fragment, step):
    pairs = []
    for y in range(SIDE):
        for x in range(SIDE):
            for core in range(CORES):
                flip_y, flip_x = ORDERS[core][fragment][step]
                pairs.append((device_at(y, x, core), device_at(y ^ flip_y, x ^ flip_x, core)))
    return pairs


CORE_PAIRS = [(device, device ^ 1) for device in range(SIDE * SIDE * CORES)]


def offsets_of(core, fragment):
    found = [(0, 0)]
    for flip_y, flip_x in ORDERS[core][fragment]:
        found = found + [(y ^ flip_y, x ^ flip_x) for y, x in found]
    return found


def hop(part, fragment, step):
    return lax.ppermute(part, "req", hop_pairs(fragment, step))


def swap_core(part):
    return lax.ppermute(part, "req", CORE_PAIRS)


def gather_rows(fragments):
    held = list(fragments)
    for step in range(4):
        came = [hop(held[f], f, step) for f in range(2)]
        held = [jnp.concatenate([held[f], came[f]], axis=0) for f in range(2)]
    return held, [swap_core(part) for part in held]


def scatter_rows(own, sibling):
    came = [swap_core(part) for part in sibling]
    held = [own[f] + came[f] for f in range(2)]
    for step in reversed(range(4)):
        half = held[0].shape[0] // 2
        came = [hop(held[f][half:], f, step) for f in range(2)]
        held = [held[f][:half] + came[f] for f in range(2)]
    return held


def block_table():
    table = np.zeros((CORES, 4, 16, 4), np.int32)
    for core in range(CORES):
        for half in range(2):
            for fragment in range(2):
                for place, (y, x) in enumerate(offsets_of(core ^ half, fragment)):
                    table[core, half * 2 + fragment, place] = (y, x, half, fragment)
    return table.reshape(CORES, 64, 4)


def rms_scale(values, gain):
    widened = values.astype(jnp.float32)
    spread = jnp.mean(widened * widened, axis=-1, keepdims=True)
    return widened * lax.rsqrt(spread + eps_norm) * gain.astype(jnp.float32)


def convolve(series, kernel, length):
    summed = jnp.zeros(series.shape[:-2] + (length, series.shape[-1]), jnp.float32)
    for kernel_tap in range(kernel.shape[0]):
        window = lax.slice_in_dim(series, kernel_tap, kernel_tap + length, axis=series.ndim - 2)
        summed = summed + window * kernel[kernel_tap].astype(jnp.float32)
    return jax.nn.silu(summed)


def feed_kernel(first_ref, second_ref, both_ref, down_ref, first_out, second_out):
    hidden = down_ref.shape[0]
    for rows_ref, out_ref in ((first_ref, first_out), (second_ref, second_out)):
        pair = jnp.dot(rows_ref[...], both_ref[...], preferred_element_type=jnp.float32)
        gate, up = pair[:, :hidden], pair[:, hidden:]
        active = (gate * jax.nn.sigmoid(gate) * up).astype(jnp.bfloat16)
        out_ref[...] = jnp.dot(
            active, down_ref[...], preferred_element_type=jnp.float32
        ).astype(jnp.bfloat16)


def feed(first, second, w_both, w_down):
    rows, width = first.shape
    whole = pl.BlockSpec(memory_space=pltpu.VMEM)
    return pl.pallas_call(
        feed_kernel,
        out_shape=[jax.ShapeDtypeStruct((rows, width), jnp.bfloat16)] * 2,
        in_specs=[whole] * 4,
        out_specs=[whole] * 2,
        compiler_params=pltpu.CompilerParams(vmem_limit_bytes=32 << 20),
        cost_estimate=pl.CostEstimate(
            flops=2 * rows * width * 2 * 3 * w_down.shape[0],
            bytes_accessed=4 * rows * width * 2 + 3 * w_down.size * 2,
            transcendentals=2 * rows * w_down.shape[0],
        ),
        name="feed",
    )(first, second, w_both, w_down)


def head_kernel(base_ref, targets_ref, owners_ref, *refs):
    rows_refs, head_ref, out_ref = refs[:4], refs[4], refs[5]
    vocab = head_ref.shape[0]
    lanes = rows_refs[0].shape[0]
    lane = lax.broadcasted_iota(jnp.int32, (lanes, 128), 0)
    column = lax.broadcasted_iota(jnp.int32, (lanes, 128), 1)
    packed = jnp.zeros(out_ref.shape, jnp.float32)
    for which in range(4):
        logits = lax.dot_general(
            head_ref[...],
            rows_refs[which][...],
            (((1,), (1,)), ((), ())),
            preferred_element_type=jnp.float32,
        )
        ids = lax.broadcasted_iota(jnp.int32, (vocab, lanes), 0) + base_ref[0]
        target = jnp.sum(
            jnp.where(ids == targets_ref[which : which + 1, :], logits, 0.0), axis=0, keepdims=True
        )
        top = jnp.max(logits, axis=0, keepdims=True)
        total = jnp.sum(jnp.exp(logits - top), axis=0, keepdims=True)
        device = lax.broadcasted_iota(jnp.int32, (out_ref.shape[0], lanes), 0)
        here = device == owners_ref[which : which + 1, :]
        for kind, stat in enumerate((top, total, target)):
            place = (column == (kind * 2 + which % 2) * DRAFT + lane % DRAFT).astype(jnp.float32)
            packed = packed + jnp.dot(
                jnp.where(here, stat, 0.0),
                place,
                precision=lax.Precision.HIGHEST,
                preferred_element_type=jnp.float32,
            )
    out_ref[...] = packed


def head_stats(base, targets, owners, rows, head_weight, devices):
    whole = pl.BlockSpec(memory_space=pltpu.VMEM)
    return pl.pallas_call(
        head_kernel,
        out_shape=jax.ShapeDtypeStruct((devices, 128), jnp.float32),
        in_specs=[pl.BlockSpec(memory_space=pltpu.SMEM)] + [whole] * 7,
        out_specs=whole,
        compiler_params=pltpu.CompilerParams(vmem_limit_bytes=48 << 20),
        cost_estimate=pl.CostEstimate(
            flops=8 * rows[0].size * head_weight.shape[0],
            bytes_accessed=8 * rows[0].size + 2 * head_weight.size,
            transcendentals=4 * rows[0].shape[0] * head_weight.shape[0],
        ),
        name="head_stats",
    )(base, targets, owners, *rows, head_weight)


def shards(
    hidden_in,
    mixer_gain,
    w_query,
    w_kv,
    w_attn_out,
    prompt_kv,
    prompt_lengths,
    member,
    accepted,
    w_z,
    w_x,
    w_bc,
    w_dt,
    conv_x,
    conv_bc,
    ssm_rate,
    dt_bias,
    skip_d,
    prompt_state,
    prompt_conv_x,
    prompt_conv_bc,
    w_mamba_out,
    mlp_gain,
    w_gate,
    w_up,
    w_down,
    final_gain,
    head_weight,
    draft_ids,
):
    row_reqs, draft_len, width = hidden_in.shape
    mdl_count = lax.axis_size("mdl")
    req_count = lax.axis_size("req")
    mdl_rank = lax.axis_index("mdl")
    req_rank = lax.axis_index("req")
    row_tokens = row_reqs * draft_len
    own_reqs = row_reqs // mdl_count
    own_tokens = own_reqs * draft_len
    contract_last = (((1,), (1,)), ((), ()))
    flat_rows = hidden_in.reshape(row_tokens, width)
    normed = rms_scale(flat_rows, mixer_gain).astype(jnp.bfloat16)
    token_request = jnp.arange(row_tokens) // draft_len
    token_position = jnp.arange(row_tokens) % draft_len
    prompt_pick = jax.nn.one_hot(member, PROMPTS, dtype=jnp.float32)
    local_heads = w_query.shape[1] // HEAD_DIM
    per_group = Q_HEADS // KV_HEADS
    kv_index = mdl_rank * local_heads // per_group
    kv_weight = lax.dynamic_index_in_dim(w_kv, kv_index, 0, keepdims=False)
    queries = jnp.dot(normed, w_query, preferred_element_type=jnp.float32).astype(jnp.bfloat16)
    key_value = jnp.dot(normed, kv_weight, preferred_element_type=jnp.float32).astype(jnp.bfloat16)
    draft_keys = key_value[:, :HEAD_DIM]
    draft_values = key_value[:, HEAD_DIM:]
    query_rows = (
        queries.reshape(row_tokens, local_heads, HEAD_DIM)
        .transpose(1, 0, 2)
        .reshape(local_heads * row_tokens, HEAD_DIM)
    )
    row_request = jnp.tile(token_request, local_heads)
    row_position = jnp.tile(token_position, local_heads)
    row_member = jnp.take(member, row_request)
    cached = lax.dynamic_index_in_dim(prompt_kv, kv_index, 1, keepdims=False)
    score_scale = HEAD_DIM ** (-0.5)
    draft_scores = (
        lax.dot_general(query_rows, draft_keys, contract_last, preferred_element_type=jnp.float32)
        * score_scale
    )
    draft_mask = (row_request[:, None] == token_request[None, :]) & (
        token_position[None, :] <= row_position[:, None]
    )
    draft_top = jnp.max(jnp.where(draft_mask, draft_scores, far_below), axis=1)

    def prompt_scores(prompt_slot, row_count):
        key_block = cached[prompt_slot]
        scores = (
            lax.dot_general(
                query_rows,
                key_block[:, :HEAD_DIM],
                contract_last,
                preferred_element_type=jnp.float32,
            )
            * score_scale
        )
        positions = jnp.arange(row_count)
        valid_keys = (row_member[:, None] == prompt_slot) & (
            positions[None, :] < prompt_lengths[prompt_slot]
        )
        return (scores, valid_keys, key_block[:, HEAD_DIM:])

    def add_weights(carry, scores, valid_keys, values_block, row_top):
        weight_total, weighted = carry
        weights = jnp.exp(jnp.where(valid_keys, scores - row_top[:, None], far_below))
        weight_total = weight_total + jnp.sum(weights, axis=1)
        weighted = weighted + jnp.dot(
            weights.astype(jnp.bfloat16), values_block, preferred_element_type=jnp.float32
        )
        return (weight_total, weighted)

    row_top = draft_top
    prompt_parts = []
    for prompt_slot in range(PROMPTS):
        scores, valid_keys, values_block = prompt_scores(prompt_slot, P_MAX)
        row_top = jnp.maximum(row_top, jnp.max(jnp.where(valid_keys, scores, far_below), axis=1))
        prompt_parts.append((scores, valid_keys, values_block))
    carry = (
        jnp.zeros(row_top.shape, jnp.float32),
        jnp.zeros((query_rows.shape[0], HEAD_DIM), jnp.float32),
    )
    for scores, valid_keys, values_block in prompt_parts:
        carry = add_weights(carry, scores, valid_keys, values_block, row_top)
    carry = add_weights(carry, draft_scores, draft_mask, draft_values, row_top)
    attended = (carry[1] / carry[0][:, None]).astype(jnp.bfloat16)
    attention_flat = (
        attended.reshape(local_heads, row_tokens, HEAD_DIM)
        .transpose(1, 0, 2)
        .reshape(row_tokens, local_heads * HEAD_DIM)
    )
    gate_z = jnp.dot(normed, w_z, preferred_element_type=jnp.float32).astype(jnp.bfloat16)
    ssm_in = jnp.dot(normed, w_x, preferred_element_type=jnp.float32).astype(jnp.bfloat16)
    bc_in = jnp.dot(normed, w_bc, preferred_element_type=jnp.float32).astype(jnp.bfloat16)
    dt_in = jnp.dot(normed, w_dt, preferred_element_type=jnp.float32).astype(jnp.bfloat16)
    local_inner = w_x.shape[1]
    local_ssm = local_inner // SSM_DIM
    edge_len = CONV - 1
    start_x = jnp.einsum(
        "rp,pcw->rcw",
        prompt_pick,
        prompt_conv_x.astype(jnp.float32),
        precision=lax.Precision.HIGHEST,
    )
    start_bc = jnp.einsum(
        "rp,pcw->rcw",
        prompt_pick,
        prompt_conv_bc.astype(jnp.float32),
        precision=lax.Precision.HIGHEST,
    )
    series_x = jnp.concatenate(
        [start_x, ssm_in.astype(jnp.float32).reshape(row_reqs, draft_len, local_inner)], axis=1
    )
    series_bc = jnp.concatenate(
        [start_bc, bc_in.astype(jnp.float32).reshape(row_reqs, draft_len, 2 * STATE)], axis=1
    )
    conv_xs = convolve(series_x, conv_x, draft_len)
    conv_bcs = convolve(series_bc, conv_bc, draft_len)
    b_part = conv_bcs[:, :, :STATE]
    c_part = conv_bcs[:, :, STATE:]
    step_size = jax.nn.softplus(
        dt_in.astype(jnp.float32).reshape(row_reqs, draft_len, local_ssm) + dt_bias
    )
    log_decay = jnp.cumsum(-step_size * ssm_rate, axis=1)
    heads_x = conv_xs.reshape(row_reqs, draft_len, local_ssm, SSM_DIM)
    causal_pairs = jnp.arange(draft_len)[:, None] >= jnp.arange(draft_len)[None, :]
    log_gaps = log_decay[:, :, None, :] - log_decay[:, None, :, :]
    mixing = jnp.exp(jnp.where(causal_pairs[None, :, :, None], log_gaps, far_below))
    intersection = jnp.einsum("rtn,rsn->rts", c_part, b_part, precision=lax.Precision.HIGHEST)
    pair_weights = mixing * intersection[..., None] * step_size[:, None, :, :]
    intra = jnp.einsum("rtsh,rshp->rthp", pair_weights, heads_x, precision=lax.Precision.HIGHEST)
    initial = jnp.einsum(
        "rp,phdn->rhdn", prompt_pick, prompt_state, precision=lax.Precision.HIGHEST
    )
    carried = (
        jnp.einsum("rhdn,rtn->rthd", initial, c_part, precision=lax.Precision.HIGHEST)
        * jnp.exp(log_decay)[..., None]
    )
    ssm_out = intra + carried + skip_d[None, None, :, None] * heads_x
    gated = (
        ssm_out.reshape(row_tokens, local_inner) * jax.nn.silu(gate_z.astype(jnp.float32))
    ).astype(jnp.bfloat16)
    last_index = accepted - 1
    pick_step = jax.nn.one_hot(last_index, draft_len, dtype=jnp.float32)
    final_log = jnp.einsum("rt,rth->rh", pick_step, log_decay, precision=lax.Precision.HIGHEST)
    upto_last = jnp.arange(draft_len)[None, :] <= last_index[:, None]
    carry_weights = (
        jnp.exp(jnp.where(upto_last[:, :, None], final_log[:, None, :] - log_decay, far_below))
        * step_size
    )
    kept_states = jnp.exp(final_log)[:, :, None, None] * initial
    kept_states = kept_states + jnp.einsum(
        "rsh,rshd,rsn->rhdn", carry_weights, heads_x, b_part, precision=lax.Precision.HIGHEST
    )
    window_pick = jax.nn.one_hot(
        accepted[:, None] + jnp.arange(edge_len)[None, :], edge_len + draft_len, dtype=jnp.float32
    )
    kept_x = jnp.einsum("rkl,rlc->rkc", window_pick, series_x, precision=lax.Precision.HIGHEST)
    kept_bc = jnp.einsum("rkl,rlc->rkc", window_pick, series_bc, precision=lax.Precision.HIGHEST)
    states_out = lax.all_to_all(
        kept_states.reshape(mdl_count, own_reqs, local_inner, STATE).astype(jnp.bfloat16),
        "mdl",
        split_axis=0,
        concat_axis=0,
        tiled=True,
    )
    edges_out = lax.all_to_all(
        kept_x.reshape(mdl_count, own_reqs * edge_len, local_inner).astype(jnp.bfloat16),
        "mdl",
        split_axis=0,
        concat_axis=0,
        tiled=True,
    )
    all_ssm = mdl_count * local_ssm
    kept_state = (
        states_out.transpose(1, 0, 2, 3)
        .astype(jnp.float32)
        .reshape(own_reqs, all_ssm, SSM_DIM, STATE)
    )
    edge_x = edges_out.transpose(1, 0, 2).reshape(own_reqs, edge_len, all_ssm * SSM_DIM)
    own_bc = lax.dynamic_slice_in_dim(kept_bc, mdl_rank * own_reqs, own_reqs, 0)
    kept_conv = jnp.concatenate([edge_x, own_bc.astype(jnp.bfloat16)], axis=2)

    core = req_rank % CORES
    chip_x = req_rank // CORES % SIDE
    chip_y = req_rank // (CORES * SIDE)
    table = jnp.where(core == 0, jnp.asarray(block_table()[0]), jnp.asarray(block_table()[1]))
    owner = ((chip_y ^ table[:, 0]) * SIDE + (chip_x ^ table[:, 1])) * CORES + (core ^ table[:, 2])
    request = owner * row_reqs + mdl_rank * own_reqs + table[:, 3]
    next_ids = jnp.concatenate([draft_ids[:, 1:], draft_ids[:, :1]], axis=1)
    picked = (request[:, None] == jnp.arange(draft_ids.shape[0])[None, :]).astype(jnp.float32)
    targets = jnp.dot(
        picked, next_ids.astype(jnp.float32), precision=lax.Precision.HIGHEST
    ).astype(jnp.int32)
    targets = targets.reshape(4, 16 * draft_len)
    owners = jnp.broadcast_to(owner[:, None], (64, draft_len)).reshape(4, 16 * draft_len)

    partial = (
        jnp.dot(attention_flat, w_attn_out, preferred_element_type=jnp.float32)
        + jnp.dot(gated, w_mamba_out, preferred_element_type=jnp.float32)
    ).astype(jnp.bfloat16)
    blocks = [
        lax.dynamic_slice_in_dim(partial, (mdl_rank ^ flip) * own_tokens, own_tokens, 0)
        for flip in range(SIDE)
    ]
    came = lax.ppermute(
        jnp.concatenate([blocks[3], blocks[2]], axis=0), "mdl", [(i, i ^ 3) for i in range(SIDE)]
    ).astype(jnp.float32)
    theirs = (blocks[1].astype(jnp.float32) + came[own_tokens:]).astype(jnp.bfloat16)
    last = lax.ppermute(theirs, "mdl", [(i, i ^ 1) for i in range(SIDE)])
    mixed = blocks[0].astype(jnp.float32) + came[:own_tokens] + last.astype(jnp.float32)
    own_rows = lax.dynamic_slice_in_dim(flat_rows, mdl_rank * own_tokens, own_tokens, 0)
    after_mixer = (own_rows.astype(jnp.float32) + mixed).astype(jnp.bfloat16)
    prepared = rms_scale(after_mixer, mlp_gain).astype(jnp.bfloat16)
    own, sibling = gather_rows([prepared[:draft_len], prepared[draft_len:]])
    w_both = jnp.concatenate([w_gate, w_up], axis=1)
    own_parts = feed(*own, w_both, w_down)
    sibling_parts = feed(*sibling, w_both, w_down)
    summed = jnp.concatenate(scatter_rows(own_parts, sibling_parts), axis=0)
    after_feed = (after_mixer.astype(jnp.float32) + summed.astype(jnp.float32)).astype(jnp.bfloat16)
    final_rows = rms_scale(after_feed, final_gain).astype(jnp.bfloat16)
    own, sibling = gather_rows([final_rows[:draft_len], final_rows[draft_len:]])
    base = (req_rank * head_weight.shape[0]).reshape(1).astype(jnp.int32)
    stats = head_stats(base, targets, owners, own + sibling, head_weight, req_count)
    shared = lax.all_to_all(stats, "req", split_axis=0, concat_axis=0, tiled=True)
    tops, totals, hits = (
        shared[:, kind * own_tokens : (kind + 1) * own_tokens] for kind in range(3)
    )
    top = jnp.max(tops, axis=0)
    total = jnp.sum(totals * jnp.exp(tops - top[None, :]), axis=0)
    log_total = top + jnp.log(total)
    position = jnp.arange(own_tokens) % draft_len
    verify_scores = jnp.where(
        position < draft_len - 1, jnp.sum(hits, axis=0) - log_total, top - log_total
    ).reshape(own_reqs, draft_len)
    return (
        after_feed.reshape(own_reqs, draft_len, width),
        verify_scores,
        kept_state,
        kept_conv,
    )


def solution(mesh):
    in_specs = (
        P("req", None, None),
        P(),
        P(None, "mdl"),
        P(),
        P("mdl", None),
        P("req", None, None, None),
        P("req"),
        P("req"),
        P("req"),
        P(None, "mdl"),
        P(None, "mdl"),
        P(),
        P(None, "mdl"),
        P(None, "mdl"),
        P(),
        P("mdl"),
        P("mdl"),
        P("mdl"),
        P("req", "mdl", None, None),
        P("req", None, "mdl"),
        P("req", None, None),
        P("mdl", None),
        P(),
        P(None, "req"),
        P(None, "req"),
        P("req", None),
        P(),
        P("req", None),
        P(),
    )
    out_specs = (
        P(("req", "mdl"), None, None),
        P(("req", "mdl"), None),
        P(("req", "mdl"), None, None, None),
        P(("req", "mdl"), None, None),
    )
    return jax.shard_map(shards, mesh=mesh, in_specs=in_specs, out_specs=out_specs, check_vma=False)
```

```python
import functools

import jax
import jax.numpy as jnp
import numpy as np
from jax import lax
from jax.experimental import pallas as pl
from jax.experimental.pallas import tpu as pltpu
from jax.sharding import PartitionSpec as P

Q_HEADS = 8
KV_HEADS = 2
HEAD_DIM = 128
SSM_DIM = 64
STATE = 256
CONV = 4
PROMPTS = 2
P_MAX = 1024
DRAFT = 16
SIDE = 4
CORES = 2

eps_norm = 1e-05
far_below = -1e30

HOPS = ((0, 1), (0, 3), (1, 0), (3, 0))
ORDERS = tuple(
    tuple(tuple(HOPS[(first + step) % 4] for step in range(4)) for first in firsts)
    for firsts in ((0, 1), (2, 3))
)


def device_at(y, x, core):
    return (y * SIDE + x) * CORES + core


def hop_pairs(fragment, step):
    pairs = []
    for y in range(SIDE):
        for x in range(SIDE):
            for core in range(CORES):
                flip_y, flip_x = ORDERS[core][fragment][step]
                pairs.append((device_at(y, x, core), device_at(y ^ flip_y, x ^ flip_x, core)))
    return pairs


CORE_PAIRS = [(device, device ^ 1) for device in range(SIDE * SIDE * CORES)]


def offsets_of(core, fragment):
    found = [(0, 0)]
    for flip_y, flip_x in ORDERS[core][fragment]:
        found = found + [(y ^ flip_y, x ^ flip_x) for y, x in found]
    return found


def hop(part, fragment, step):
    return lax.ppermute(part, "req", hop_pairs(fragment, step))


def swap_core(part):
    return lax.ppermute(part, "req", CORE_PAIRS)


def gather_rows(fragments):
    held = list(fragments)
    for step in range(4):
        came = [hop(held[f], f, step) for f in range(2)]
        held = [jnp.concatenate([held[f], came[f]], axis=0) for f in range(2)]
    return held, [swap_core(part) for part in held]


def scatter_rows(own, sibling):
    came = [swap_core(part) for part in sibling]
    held = [own[f] + came[f] for f in range(2)]
    for step in reversed(range(4)):
        half = held[0].shape[0] // 2
        came = [hop(held[f][half:], f, step) for f in range(2)]
        held = [held[f][:half] + came[f] for f in range(2)]
    return held


def block_table():
    table = np.zeros((CORES, 4, 16, 4), np.int32)
    for core in range(CORES):
        for half in range(2):
            for fragment in range(2):
                for place, (y, x) in enumerate(offsets_of(core ^ half, fragment)):
                    table[core, half * 2 + fragment, place] = (y, x, half, fragment)
    return table.reshape(CORES, 64, 4)


def rms_scale(values, gain):
    widened = values.astype(jnp.float32)
    spread = jnp.mean(widened * widened, axis=-1, keepdims=True)
    return widened * lax.rsqrt(spread + eps_norm) * gain.astype(jnp.float32)


HIGHEST = lax.Precision.HIGHEST
NEXT_TO = (((1,), (1,)), ((), ()))


def dot32(left, right, dims=None):
    dims = dims or (((1,), (0,)), ((), ()))
    return lax.dot_general(left, right, dims, preferred_element_type=jnp.float32)


def exact_dot(left, right):
    return jnp.dot(left, right, precision=HIGHEST, preferred_element_type=jnp.float32)


def mixer_kernel(
    member_ref,
    accepted_ref,
    lengths_ref,
    place_ref,
    hidden_ref,
    gain_ref,
    w_dt_ref,
    conv_x_ref,
    conv_bc_ref,
    rate_ref,
    bias_ref,
    skip_ref,
    past_x_ref,
    past_bc_ref,
    w_query_hbm,
    w_kv_hbm,
    prompt_hbm,
    w_x_hbm,
    w_bc_hbm,
    w_z_hbm,
    state_hbm,
    w_attn_hbm,
    w_mamba_hbm,
    far_ref,
    near_ref,
    kept_ref,
    kept_x_ref,
    kept_bc_ref,
    w_query,
    w_kv,
    prompt,
    w_x,
    w_bc,
    w_z,
    state,
    w_out,
    mixed_scr,
    lanes_scr,
    sems,
):
    rank, group = place_ref[0], place_ref[1]
    tokens = hidden_ref.shape[0]
    requests = tokens // DRAFT
    inner = w_x.shape[1]
    heads = inner // SSM_DIM
    query_width = w_query.shape[1]
    copies = [
        pltpu.make_async_copy(source, target, sems.at[index])
        for index, (source, target) in enumerate(
            (
                (w_query_hbm, w_query),
                (w_kv_hbm.at[group], w_kv),
                (prompt_hbm.at[0, group], prompt.at[0]),
                (prompt_hbm.at[1, group], prompt.at[1]),
                (w_x_hbm, w_x),
                (w_bc_hbm, w_bc),
                (w_z_hbm, w_z),
                (state_hbm, state),
                (w_attn_hbm, w_out.at[pl.ds(0, query_width), :]),
                (w_mamba_hbm, w_out.at[pl.ds(query_width, inner), :]),
            )
        )
    ]
    for copy in copies:
        copy.start()

    row = lax.broadcasted_iota(jnp.int32, (tokens, 1), 0)
    time, request = row % DRAFT, row // DRAFT
    own_prompt = jnp.zeros((tokens, 1), jnp.int32)
    last = jnp.zeros((tokens, 1), jnp.int32)
    for r in range(requests):
        own_prompt = jnp.where(request == r, member_ref[r], own_prompt)
        last = jnp.where(request == r, accepted_ref[r] - 1, last)
    first_prompt = own_prompt == 0

    widened = hidden_ref[...].astype(jnp.float32)
    spread = jnp.mean(widened * widened, axis=-1, keepdims=True)
    normed = (
        widened * lax.rsqrt(spread + eps_norm) * gain_ref[...].astype(jnp.float32)
    ).astype(jnp.bfloat16)

    copies[0].wait()
    queries = dot32(normed, w_query[...]).astype(jnp.bfloat16)
    copies[1].wait()
    drafts = dot32(normed, w_kv[...]).astype(jnp.bfloat16)
    local_heads = query_width // HEAD_DIM
    query_rows = jnp.concatenate(
        [queries[:, h * HEAD_DIM : (h + 1) * HEAD_DIM] for h in range(local_heads)], axis=0
    )
    scale = HEAD_DIM**-0.5
    row_first = jnp.concatenate([own_prompt] * local_heads, axis=0) == 0
    draft_scores = dot32(query_rows, drafts[:, :HEAD_DIM], NEXT_TO) * scale
    same = (row // DRAFT == lax.broadcasted_iota(jnp.int32, (tokens, tokens), 1) // DRAFT) & (
        lax.broadcasted_iota(jnp.int32, (tokens, tokens), 1) <= row
    )
    draft_mask = jnp.concatenate([same] * local_heads, axis=0)
    draft_scores = jnp.where(draft_mask, draft_scores, far_below)
    copies[2].wait()
    copies[3].wait()
    scores = jnp.where(
        row_first,
        dot32(query_rows, prompt[0, :, :HEAD_DIM], NEXT_TO),
        dot32(query_rows, prompt[1, :, :HEAD_DIM], NEXT_TO),
    )
    length = jnp.where(row_first, lengths_ref[0], lengths_ref[1])
    position = lax.broadcasted_iota(jnp.int32, scores.shape, 1)
    scores = jnp.where(position < length, scores * scale, far_below)
    top = jnp.maximum(
        jnp.max(scores, axis=1, keepdims=True), jnp.max(draft_scores, axis=1, keepdims=True)
    )
    weights = jnp.exp(scores - top)
    draft_weights = jnp.exp(draft_scores - top)
    total = jnp.sum(weights, axis=1, keepdims=True) + jnp.sum(draft_weights, axis=1, keepdims=True)
    weighted = (
        dot32(jnp.where(row_first, weights, 0.0).astype(jnp.bfloat16), prompt[0, :, HEAD_DIM:])
        + dot32(jnp.where(row_first, 0.0, weights).astype(jnp.bfloat16), prompt[1, :, HEAD_DIM:])
        + dot32(draft_weights.astype(jnp.bfloat16), drafts[:, HEAD_DIM:])
    )
    attended = (weighted / total).astype(jnp.bfloat16)
    for h in range(local_heads):
        mixed_scr[:, h * HEAD_DIM : (h + 1) * HEAD_DIM] = attended[h * tokens : (h + 1) * tokens]

    def convolve_rows(series, past_ref, taps_ref):
        past = [
            jnp.where(
                first_prompt,
                past_ref[0, j : j + 1, :].astype(jnp.float32),
                past_ref[1, j : j + 1, :].astype(jnp.float32),
            )
            for j in range(CONV - 1)
        ]
        taps = taps_ref[...].astype(jnp.float32)
        summed = series * taps[CONV - 1 : CONV, :]
        for shift in range(1, CONV):
            window = pltpu.roll(series, shift, 0)
            for t in range(shift):
                window = jnp.where(time == t, past[CONV - 1 - shift + t], window)
            summed = summed + window * taps[CONV - 1 - shift : CONV - shift, :]
        return summed * jax.nn.sigmoid(summed)

    copies[4].wait()
    in_x = dot32(normed, w_x[...]).astype(jnp.bfloat16)
    heads_x = convolve_rows(in_x.astype(jnp.float32), past_x_ref, conv_x_ref)
    copies[5].wait()
    in_bc = dot32(normed, w_bc[...]).astype(jnp.bfloat16)
    conv_bcs = convolve_rows(in_bc.astype(jnp.float32), past_bc_ref, conv_bc_ref)
    b_part = conv_bcs[:, :STATE].astype(jnp.bfloat16)
    c_part = conv_bcs[:, STATE:].astype(jnp.bfloat16)

    def widen(values):
        lanes_scr[...] = jnp.zeros(lanes_scr.shape, jnp.float32)
        lanes_scr[:, :heads] = values
        return lanes_scr[...]

    spread_lanes = (
        lax.broadcasted_iota(jnp.int32, (tokens, inner), 0)
        == lax.broadcasted_iota(jnp.int32, (tokens, inner), 1) // SSM_DIM
    ).astype(jnp.float32)
    dt_in = dot32(normed, w_dt_ref[...]).astype(jnp.bfloat16).astype(jnp.float32) + bias_ref[...]
    step = jnp.maximum(dt_in, 0.0) + jnp.log1p(jnp.exp(-jnp.abs(dt_in)))
    log_decay = exact_dot(same.astype(jnp.float32), widen(-step * rate_ref[...]))
    step_x = exact_dot(widen(step), spread_lanes)
    skip_x = exact_dot(widen(jnp.broadcast_to(skip_ref[...], (tokens, heads))), spread_lanes)
    decay_x = exact_dot(log_decay, spread_lanes)
    turned = log_decay.T
    intersection = dot32(c_part, b_part, NEXT_TO)
    scaled_x = heads_x * step_x
    low = lax.broadcasted_iota(jnp.int32, (tokens, 2 * SSM_DIM), 1) < SSM_DIM
    groups = []
    for pair in range(heads // 2):
        mixing = []
        for h in (2 * pair, 2 * pair + 1):
            gaps = log_decay[:, h : h + 1] - turned[h : h + 1, :]
            mixing.append(
                (jnp.exp(jnp.where(same, gaps, far_below)) * intersection).astype(jnp.bfloat16)
            )
        lanes = scaled_x[:, pair * 2 * SSM_DIM : (pair + 1) * 2 * SSM_DIM]
        both = jnp.concatenate([jnp.where(low, lanes, 0.0), jnp.where(low, 0.0, lanes)], axis=0)
        groups.append(dot32(jnp.concatenate(mixing, axis=1), both.astype(jnp.bfloat16)))
    copies[7].wait()
    carried = jnp.where(
        first_prompt,
        dot32(c_part, state[0].astype(jnp.bfloat16), NEXT_TO),
        dot32(c_part, state[1].astype(jnp.bfloat16), NEXT_TO),
    )
    ssm_out = jnp.concatenate(groups, axis=1) + carried * jnp.exp(decay_x) + skip_x * heads_x
    copies[6].wait()
    gate_z = dot32(normed, w_z[...]).astype(jnp.bfloat16).astype(jnp.float32)
    mixed_scr[:, query_width:] = (ssm_out * (gate_z * jax.nn.sigmoid(gate_z))).astype(jnp.bfloat16)

    own_rows = tokens // SIDE
    copies[8].wait()
    copies[9].wait()
    for out_ref, flips in ((far_ref, (3, 2)), (near_ref, (0, 1))):
        rows = jnp.concatenate(
            [
                mixed_scr[pl.ds(pl.multiple_of((rank ^ flip) * own_rows, own_rows), own_rows), :]
                for flip in flips
            ],
            axis=0,
        )
        out_ref[...] = dot32(rows, w_out[...]).astype(jnp.bfloat16)

    other = lax.broadcasted_iota(jnp.int32, (tokens, tokens), 1)
    pick = (other == request * DRAFT + last).astype(jnp.float32)
    final_log = exact_dot(pick, log_decay)
    final_x = exact_dot(final_log, spread_lanes)
    carry_x = jnp.exp(jnp.where(time <= last, final_x - decay_x, far_below))
    carried_x = (scaled_x * carry_x).T.astype(jnp.bfloat16)
    shrink = jnp.exp(final_x).T
    for r in range(requests):
        b_here = jnp.where(request == r, b_part, jnp.zeros_like(b_part))
        kept = shrink[:, r * DRAFT : r * DRAFT + 1] * state[member_ref[r]] + dot32(
            carried_x, b_here
        )
        kept_ref[r] = kept.astype(jnp.bfloat16)

    def kept_rows(first_request, count, series, past_ref):
        at = lax.broadcasted_iota(jnp.int32, (count, 1), 0)
        here, edge = at // (CONV - 1), at % (CONV - 1)
        start = jnp.zeros((count, 1), jnp.int32)
        owner = jnp.zeros((count, 1), jnp.int32)
        for r in range(count // (CONV - 1)):
            start = jnp.where(here == r, accepted_ref[first_request + r], start)
            owner = jnp.where(here == r, member_ref[first_request + r], owner)
        index = start + edge
        token = (here + first_request) * DRAFT + index - (CONV - 1)
        chosen = (lax.broadcasted_iota(jnp.int32, (count, tokens), 1) == token) & (
            index >= CONV - 1
        )
        rows = dot32(chosen.astype(jnp.bfloat16), series)
        for p in range(PROMPTS):
            for j in range(CONV - 1):
                rows = jnp.where(
                    (owner == p) & (index == j), past_ref[p, j : j + 1, :].astype(jnp.float32), rows
                )
        return rows.astype(jnp.bfloat16)

    kept_x_ref[...] = kept_rows(0, kept_x_ref.shape[0], in_x, past_x_ref)
    kept_bc_ref[...] = kept_rows(
        rank * (requests // SIDE), kept_bc_ref.shape[0], in_bc, past_bc_ref
    )


def mixer(
    hidden, mixer_gain, w_query, w_kv, w_attn_out, prompt_kv, prompt_lengths, member, accepted, w_z, w_x, w_bc,
    w_dt, conv_x, conv_bc, ssm_rate, dt_bias, skip_d, prompt_state, prompt_conv_x, prompt_conv_bc, w_mamba_out, rank,
):
    tokens, width = hidden.shape
    requests = tokens // DRAFT
    inner = w_x.shape[1]
    query_width = w_query.shape[1]
    group = rank * (query_width // HEAD_DIM) // (Q_HEADS // KV_HEADS)
    place = jnp.stack([rank, group]).astype(jnp.int32)
    scalars = pl.BlockSpec(memory_space=pltpu.SMEM)
    whole = pl.BlockSpec(memory_space=pltpu.VMEM)
    left = pl.BlockSpec(memory_space=pl.ANY)
    edges = CONV - 1
    bf16 = jnp.bfloat16
    state = prompt_state.reshape(PROMPTS, inner, STATE)
    return pl.pallas_call(
        mixer_kernel,
        out_shape=[
            jax.ShapeDtypeStruct((tokens // 2, width), bf16),
            jax.ShapeDtypeStruct((tokens // 2, width), bf16),
            jax.ShapeDtypeStruct((requests, inner, STATE), bf16),
            jax.ShapeDtypeStruct((requests * edges, inner), bf16),
            jax.ShapeDtypeStruct((requests // SIDE * edges, 2 * STATE), bf16),
        ],
        in_specs=[scalars] * 4 + [whole] * 10 + [left] * 9,
        out_specs=[whole] * 5,
        scratch_shapes=[
            pltpu.VMEM(w_query.shape, bf16),
            pltpu.VMEM(w_kv.shape[1:], bf16),
            pltpu.VMEM((PROMPTS, *prompt_kv.shape[2:]), bf16),
            pltpu.VMEM(w_x.shape, bf16),
            pltpu.VMEM(w_bc.shape, bf16),
            pltpu.VMEM(w_z.shape, bf16),
            pltpu.VMEM(state.shape, jnp.float32),
            pltpu.VMEM((query_width + inner, width), bf16),
            pltpu.VMEM((tokens, query_width + inner), bf16),
            pltpu.VMEM((tokens, 128), jnp.float32),
            pltpu.SemaphoreType.DMA((10,)),
        ],
        compiler_params=pltpu.CompilerParams(vmem_limit_bytes=48 << 20),
        cost_estimate=pl.CostEstimate(
            flops=3_000_000_000, bytes_accessed=20_000_000, transcendentals=1_000_000
        ),
        name="mixer",
    )(
        member, accepted, prompt_lengths, place, hidden, mixer_gain.reshape(1, width), w_dt, conv_x, conv_bc,
        ssm_rate.reshape(1, -1), dt_bias.reshape(1, -1), skip_d.reshape(1, -1), prompt_conv_x, prompt_conv_bc,
        w_query, w_kv, prompt_kv, w_x, w_bc, w_z, state, w_attn_out, w_mamba_out,
    )


def feed_kernel(first_ref, second_ref, both_ref, down_ref, first_out, second_out):
    hidden = down_ref.shape[0]
    for rows_ref, out_ref in ((first_ref, first_out), (second_ref, second_out)):
        pair = jnp.dot(rows_ref[...], both_ref[...], preferred_element_type=jnp.float32)
        gate, up = pair[:, :hidden], pair[:, hidden:]
        active = (gate * jax.nn.sigmoid(gate) * up).astype(jnp.bfloat16)
        out_ref[...] = jnp.dot(
            active, down_ref[...], preferred_element_type=jnp.float32
        ).astype(jnp.bfloat16)


def feed(first, second, w_both, w_down):
    rows, width = first.shape
    whole = pl.BlockSpec(memory_space=pltpu.VMEM)
    return pl.pallas_call(
        feed_kernel,
        out_shape=[jax.ShapeDtypeStruct((rows, width), jnp.bfloat16)] * 2,
        in_specs=[whole] * 4,
        out_specs=[whole] * 2,
        compiler_params=pltpu.CompilerParams(vmem_limit_bytes=32 << 20),
        cost_estimate=pl.CostEstimate(
            flops=2 * rows * width * 2 * 3 * w_down.shape[0],
            bytes_accessed=4 * rows * width * 2 + 3 * w_down.size * 2,
            transcendentals=2 * rows * w_down.shape[0],
        ),
        name="feed",
    )(first, second, w_both, w_down)


def head_kernel(base_ref, targets_ref, owners_ref, *refs):
    rows_refs, head_ref, out_ref = refs[:4], refs[4], refs[5]
    vocab = head_ref.shape[0]
    lanes = rows_refs[0].shape[0]
    lane = lax.broadcasted_iota(jnp.int32, (lanes, 128), 0)
    column = lax.broadcasted_iota(jnp.int32, (lanes, 128), 1)
    packed = jnp.zeros(out_ref.shape, jnp.float32)
    for which in range(4):
        logits = lax.dot_general(
            head_ref[...],
            rows_refs[which][...],
            (((1,), (1,)), ((), ())),
            preferred_element_type=jnp.float32,
        )
        ids = lax.broadcasted_iota(jnp.int32, (vocab, lanes), 0) + base_ref[0]
        target = jnp.sum(
            jnp.where(ids == targets_ref[which : which + 1, :], logits, 0.0), axis=0, keepdims=True
        )
        top = jnp.max(logits, axis=0, keepdims=True)
        total = jnp.sum(jnp.exp(logits - top), axis=0, keepdims=True)
        device = lax.broadcasted_iota(jnp.int32, (out_ref.shape[0], lanes), 0)
        here = device == owners_ref[which : which + 1, :]
        for kind, stat in enumerate((top, total, target)):
            place = (column == (kind * 2 + which % 2) * DRAFT + lane % DRAFT).astype(jnp.float32)
            packed = packed + jnp.dot(
                jnp.where(here, stat, 0.0),
                place,
                precision=lax.Precision.HIGHEST,
                preferred_element_type=jnp.float32,
            )
    out_ref[...] = packed


def head_stats(base, targets, owners, rows, head_weight, devices):
    whole = pl.BlockSpec(memory_space=pltpu.VMEM)
    return pl.pallas_call(
        head_kernel,
        out_shape=jax.ShapeDtypeStruct((devices, 128), jnp.float32),
        in_specs=[pl.BlockSpec(memory_space=pltpu.SMEM)] + [whole] * 7,
        out_specs=whole,
        compiler_params=pltpu.CompilerParams(vmem_limit_bytes=48 << 20),
        cost_estimate=pl.CostEstimate(
            flops=8 * rows[0].size * head_weight.shape[0],
            bytes_accessed=8 * rows[0].size + 2 * head_weight.size,
            transcendentals=4 * rows[0].shape[0] * head_weight.shape[0],
        ),
        name="head_stats",
    )(base, targets, owners, *rows, head_weight)


def shards(
    hidden_in,
    mixer_gain,
    w_query,
    w_kv,
    w_attn_out,
    prompt_kv,
    prompt_lengths,
    member,
    accepted,
    w_z,
    w_x,
    w_bc,
    w_dt,
    conv_x,
    conv_bc,
    ssm_rate,
    dt_bias,
    skip_d,
    prompt_state,
    prompt_conv_x,
    prompt_conv_bc,
    w_mamba_out,
    mlp_gain,
    w_gate,
    w_up,
    w_down,
    final_gain,
    head_weight,
    draft_ids,
):
    row_reqs, draft_len, width = hidden_in.shape
    mdl_count = lax.axis_size("mdl")
    req_count = lax.axis_size("req")
    mdl_rank = lax.axis_index("mdl")
    req_rank = lax.axis_index("req")
    row_tokens = row_reqs * draft_len
    own_reqs = row_reqs // mdl_count
    own_tokens = own_reqs * draft_len
    flat_rows = hidden_in.reshape(row_tokens, width)
    local_inner = w_x.shape[1]
    local_ssm = local_inner // SSM_DIM
    edge_len = CONV - 1
    far, near, kept_states, kept_x, own_bc = mixer(
        flat_rows, mixer_gain, w_query, w_kv, w_attn_out, prompt_kv, prompt_lengths, member, accepted, w_z, w_x, w_bc,
        w_dt, conv_x, conv_bc, ssm_rate, dt_bias, skip_d, prompt_state, prompt_conv_x, prompt_conv_bc, w_mamba_out, mdl_rank,
    )
    states_out = lax.all_to_all(
        kept_states.reshape(mdl_count, own_reqs, local_inner, STATE),
        "mdl",
        split_axis=0,
        concat_axis=0,
        tiled=True,
    )
    edges_out = lax.all_to_all(
        kept_x.reshape(mdl_count, own_reqs * edge_len, local_inner),
        "mdl",
        split_axis=0,
        concat_axis=0,
        tiled=True,
    )
    all_ssm = mdl_count * local_ssm
    kept_state = (
        states_out.transpose(1, 0, 2, 3)
        .astype(jnp.float32)
        .reshape(own_reqs, all_ssm, SSM_DIM, STATE)
    )
    edge_x = edges_out.transpose(1, 0, 2).reshape(own_reqs, edge_len, all_ssm * SSM_DIM)
    kept_conv = jnp.concatenate([edge_x, own_bc.reshape(own_reqs, edge_len, 2 * STATE)], axis=2)

    core = req_rank % CORES
    chip_x = req_rank // CORES % SIDE
    chip_y = req_rank // (CORES * SIDE)
    table = jnp.where(core == 0, jnp.asarray(block_table()[0]), jnp.asarray(block_table()[1]))
    owner = ((chip_y ^ table[:, 0]) * SIDE + (chip_x ^ table[:, 1])) * CORES + (core ^ table[:, 2])
    request = owner * row_reqs + mdl_rank * own_reqs + table[:, 3]
    next_ids = jnp.concatenate([draft_ids[:, 1:], draft_ids[:, :1]], axis=1)
    picked = (request[:, None] == jnp.arange(draft_ids.shape[0])[None, :]).astype(jnp.float32)
    targets = jnp.dot(
        picked, next_ids.astype(jnp.float32), precision=lax.Precision.HIGHEST
    ).astype(jnp.int32)
    targets = targets.reshape(4, 16 * draft_len)
    owners = jnp.broadcast_to(owner[:, None], (64, draft_len)).reshape(4, 16 * draft_len)

    came = lax.ppermute(far, "mdl", [(i, i ^ 3) for i in range(SIDE)])
    theirs = near[own_tokens:] + came[own_tokens:]
    last = lax.ppermute(theirs, "mdl", [(i, i ^ 1) for i in range(SIDE)])
    mixed = (
        near[:own_tokens].astype(jnp.float32)
        + came[:own_tokens].astype(jnp.float32)
        + last.astype(jnp.float32)
    )
    own_rows = lax.dynamic_slice_in_dim(flat_rows, mdl_rank * own_tokens, own_tokens, 0)
    after_mixer = (own_rows.astype(jnp.float32) + mixed).astype(jnp.bfloat16)
    prepared = rms_scale(after_mixer, mlp_gain).astype(jnp.bfloat16)
    own, sibling = gather_rows([prepared[:draft_len], prepared[draft_len:]])
    w_both = jnp.concatenate([w_gate, w_up], axis=1)
    own_parts = feed(*own, w_both, w_down)
    sibling_parts = feed(*sibling, w_both, w_down)
    summed = jnp.concatenate(scatter_rows(own_parts, sibling_parts), axis=0)
    after_feed = (after_mixer.astype(jnp.float32) + summed.astype(jnp.float32)).astype(jnp.bfloat16)
    final_rows = rms_scale(after_feed, final_gain).astype(jnp.bfloat16)
    own, sibling = gather_rows([final_rows[:draft_len], final_rows[draft_len:]])
    base = (req_rank * head_weight.shape[0]).reshape(1).astype(jnp.int32)
    stats = head_stats(base, targets, owners, own + sibling, head_weight, req_count)
    shared = lax.all_to_all(stats, "req", split_axis=0, concat_axis=0, tiled=True)
    tops, totals, hits = (
        shared[:, kind * own_tokens : (kind + 1) * own_tokens] for kind in range(3)
    )
    top = jnp.max(tops, axis=0)
    total = jnp.sum(totals * jnp.exp(tops - top[None, :]), axis=0)
    log_total = top + jnp.log(total)
    position = jnp.arange(own_tokens) % draft_len
    verify_scores = jnp.where(
        position < draft_len - 1, jnp.sum(hits, axis=0) - log_total, top - log_total
    ).reshape(own_reqs, draft_len)
    return (
        after_feed.reshape(own_reqs, draft_len, width),
        verify_scores,
        kept_state,
        kept_conv,
    )


def solution(mesh):
    in_specs = (
        P("req", None, None),
        P(),
        P(None, "mdl"),
        P(),
        P("mdl", None),
        P("req", None, None, None),
        P("req"),
        P("req"),
        P("req"),
        P(None, "mdl"),
        P(None, "mdl"),
        P(),
        P(None, "mdl"),
        P(None, "mdl"),
        P(),
        P("mdl"),
        P("mdl"),
        P("mdl"),
        P("req", "mdl", None, None),
        P("req", None, "mdl"),
        P("req", None, None),
        P("mdl", None),
        P(),
        P(None, "req"),
        P(None, "req"),
        P("req", None),
        P(),
        P("req", None),
        P(),
    )
    out_specs = (
        P(("req", "mdl"), None, None),
        P(("req", "mdl"), None),
        P(("req", "mdl"), None, None, None),
        P(("req", "mdl"), None, None),
    )
    return jax.shard_map(shards, mesh=mesh, in_specs=in_specs, out_specs=out_specs, check_vma=False)
```

```python
import functools

import jax
import jax.numpy as jnp
import numpy as np
from jax import lax
from jax.experimental import pallas as pl
from jax.experimental.pallas import tpu as pltpu
from jax.sharding import PartitionSpec as P

Q_HEADS = 8
KV_HEADS = 2
HEAD_DIM = 128
SSM_DIM = 64
STATE = 256
CONV = 4
PROMPTS = 2
P_MAX = 1024
DRAFT = 16
SIDE = 4
CORES = 2

eps_norm = 1e-05
far_below = -1e30

HOPS = ((0, 1), (0, 3), (1, 0), (3, 0))
ORDERS = tuple(
    tuple(tuple(HOPS[(first + step) % 4] for step in range(4)) for first in firsts)
    for firsts in ((0, 1), (2, 3))
)


def device_at(y, x, core):
    return (y * SIDE + x) * CORES + core


def hop_pairs(fragment, step):
    pairs = []
    for y in range(SIDE):
        for x in range(SIDE):
            for core in range(CORES):
                flip_y, flip_x = ORDERS[core][fragment][step]
                pairs.append((device_at(y, x, core), device_at(y ^ flip_y, x ^ flip_x, core)))
    return pairs


CORE_PAIRS = [(device, device ^ 1) for device in range(SIDE * SIDE * CORES)]


def offsets_of(core, fragment):
    found = [(0, 0)]
    for flip_y, flip_x in ORDERS[core][fragment]:
        found = found + [(y ^ flip_y, x ^ flip_x) for y, x in found]
    return found


def hop(part, fragment, step):
    return lax.ppermute(part, "req", hop_pairs(fragment, step))


def swap_core(part):
    return lax.ppermute(part, "req", CORE_PAIRS)


def gather_rows(fragments):
    held = list(fragments)
    for step in range(3):
        came = [hop(held[f], f, step) for f in range(2)]
        held = [jnp.concatenate([held[f], came[f]], axis=0) for f in range(2)]
    late = [hop(held[f], f, 3) for f in range(2)]
    return (held, [swap_core(part) for part in held]), (late, [swap_core(part) for part in late])


def added(left, right):
    return (left.astype(jnp.float32) + right.astype(jnp.float32)).astype(jnp.bfloat16)


def scatter_rows(early, late):
    came = [swap_core(part) for part in late[1]]
    late = [hop(added(late[0][f], came[f]), f, 3) for f in range(2)]
    came = [swap_core(part) for part in early[1]]
    held = [added(early[0][f], came[f]) for f in range(2)]
    held = [added(held[f], late[f]) for f in range(2)]
    for step in reversed(range(3)):
        half = held[0].shape[0] // 2
        came = [hop(held[f][half:], f, step) for f in range(2)]
        held = [added(held[f][:half], came[f]) for f in range(2)]
    return held


def block_table():
    table = np.zeros((CORES, 2, 2, 2, 8, 4), np.int32)
    for core in range(CORES):
        for half in range(2):
            for fragment in range(2):
                for place, (y, x) in enumerate(offsets_of(core ^ half, fragment)):
                    table[core, place // 8, half, fragment, place % 8] = (y, x, half, fragment)
    return table.reshape(CORES, 64, 4)


def rms_scale(values, gain):
    widened = values.astype(jnp.float32)
    spread = jnp.mean(widened * widened, axis=-1, keepdims=True)
    return widened * lax.rsqrt(spread + eps_norm) * gain.astype(jnp.float32)


HIGHEST = lax.Precision.HIGHEST
NEXT_TO = (((1,), (1,)), ((), ()))


def dot32(left, right, dims=None):
    dims = dims or (((1,), (0,)), ((), ()))
    return lax.dot_general(left, right, dims, preferred_element_type=jnp.float32)


def exact_dot(left, right):
    return jnp.dot(left, right, precision=HIGHEST, preferred_element_type=jnp.float32)


def mixer_kernel(*refs):
    sources, refs = refs[:22], refs[22:]
    far_ref, near_ref, kept_ref, kept_bc_ref = refs[:4]
    held, (mixed_scr, lanes_scr, sems) = refs[4:-3], refs[-3:]
    member_ref, accepted_ref, lengths_ref, rate_ref, bias_ref, skip_ref = held[:6]
    hidden_ref, gain_ref, w_dt_ref, conv_x_ref, conv_bc_ref, past_x_ref, past_bc_ref = held[6:13]
    w_query, w_kv, prompt, w_x, w_bc, w_z, state, w_out = held[13:]
    tokens = hidden_ref.shape[0]
    requests = tokens // DRAFT
    inner = w_x.shape[1]
    heads = inner // SSM_DIM
    query_width = w_query.shape[1]
    rank = lax.axis_index("mdl")
    core = lax.axis_index("req") % CORES
    group = rank * (query_width // HEAD_DIM) // (Q_HEADS // KV_HEADS)
    query_hbm, kv_hbm, prompt_hbm, x_hbm, bc_hbm, z_hbm, state_hbm, attn_hbm, mamba_hbm = sources[13:]
    moves = [(source, target) for source, target in zip(sources[:13], held[:13], strict=True)]
    moves += [
        (query_hbm, w_query),
        (kv_hbm.at[group], w_kv),
        (prompt_hbm.at[0, group], prompt.at[0]),
        (prompt_hbm.at[1, group], prompt.at[1]),
        (x_hbm, w_x),
        (bc_hbm, w_bc),
        (z_hbm, w_z),
        (state_hbm, state),
        (attn_hbm, w_out.at[pl.ds(0, query_width), :]),
        (mamba_hbm, w_out.at[pl.ds(query_width, inner), :]),
    ]
    started = [
        pltpu.make_async_copy(source, target, sems.at[index])
        for index, (source, target) in enumerate(moves)
    ]
    for copy in started:
        copy.start()
    for copy in started[:13]:
        copy.wait()
    copies = started[13:]

    def head_row(ref):
        lane = lax.broadcasted_iota(jnp.int32, (1, heads), 1)
        values = jnp.zeros((1, heads), jnp.float32)
        for h in range(heads):
            values = jnp.where(lane == h, ref[h], values)
        return values

    row = lax.broadcasted_iota(jnp.int32, (tokens, 1), 0)
    time, request = row % DRAFT, row // DRAFT
    own_prompt = jnp.zeros((tokens, 1), jnp.int32)
    last = jnp.zeros((tokens, 1), jnp.int32)
    for r in range(requests):
        own_prompt = jnp.where(request == r, member_ref[r], own_prompt)
        last = jnp.where(request == r, accepted_ref[r] - 1, last)
    first_prompt = own_prompt == 0

    gain = jnp.concatenate(
        [gain_ref[j : j + 1, :].astype(jnp.float32) for j in range(gain_ref.shape[0])], axis=1
    )
    widened = hidden_ref[...].astype(jnp.float32)
    spread = jnp.mean(widened * widened, axis=-1, keepdims=True)
    normed = (
        widened * lax.rsqrt(spread + eps_norm) * gain
    ).astype(jnp.bfloat16)

    copies[0].wait()
    queries = dot32(normed, w_query[...]).astype(jnp.bfloat16)
    copies[1].wait()
    drafts = dot32(normed, w_kv[...]).astype(jnp.bfloat16)
    local_heads = query_width // HEAD_DIM
    query_rows = jnp.concatenate(
        [queries[:, h * HEAD_DIM : (h + 1) * HEAD_DIM] for h in range(local_heads)], axis=0
    )
    scale = HEAD_DIM**-0.5
    row_first = jnp.concatenate([own_prompt] * local_heads, axis=0) == 0
    draft_scores = dot32(query_rows, drafts[:, :HEAD_DIM], NEXT_TO) * scale
    same = (row // DRAFT == lax.broadcasted_iota(jnp.int32, (tokens, tokens), 1) // DRAFT) & (
        lax.broadcasted_iota(jnp.int32, (tokens, tokens), 1) <= row
    )
    draft_mask = jnp.concatenate([same] * local_heads, axis=0)
    draft_scores = jnp.where(draft_mask, draft_scores, far_below)
    copies[2].wait()
    copies[3].wait()
    scores = jnp.where(
        row_first,
        dot32(query_rows, prompt[0, :, :HEAD_DIM], NEXT_TO),
        dot32(query_rows, prompt[1, :, :HEAD_DIM], NEXT_TO),
    )
    length = jnp.where(row_first, lengths_ref[0], lengths_ref[1])
    position = lax.broadcasted_iota(jnp.int32, scores.shape, 1)
    scores = jnp.where(position < length, scores * scale, far_below)
    top = jnp.maximum(
        jnp.max(scores, axis=1, keepdims=True), jnp.max(draft_scores, axis=1, keepdims=True)
    )
    weights = jnp.exp(scores - top)
    draft_weights = jnp.exp(draft_scores - top)
    total = jnp.sum(weights, axis=1, keepdims=True) + jnp.sum(draft_weights, axis=1, keepdims=True)
    weighted = (
        dot32(jnp.where(row_first, weights, 0.0).astype(jnp.bfloat16), prompt[0, :, HEAD_DIM:])
        + dot32(jnp.where(row_first, 0.0, weights).astype(jnp.bfloat16), prompt[1, :, HEAD_DIM:])
        + dot32(draft_weights.astype(jnp.bfloat16), drafts[:, HEAD_DIM:])
    )
    attended = (weighted / total).astype(jnp.bfloat16)
    for h in range(local_heads):
        mixed_scr[:, h * HEAD_DIM : (h + 1) * HEAD_DIM] = attended[h * tokens : (h + 1) * tokens]

    def convolve_rows(series, past_ref, taps_ref):
        past = [
            jnp.where(
                first_prompt,
                past_ref[j, 0:1, :].astype(jnp.float32),
                past_ref[j, 1:2, :].astype(jnp.float32),
            )
            for j in range(CONV - 1)
        ]
        taps = taps_ref[...].astype(jnp.float32)
        summed = series * taps[CONV - 1 : CONV, :]
        for shift in range(1, CONV):
            window = pltpu.roll(series, shift, 0)
            for t in range(shift):
                window = jnp.where(time == t, past[CONV - 1 - shift + t], window)
            summed = summed + window * taps[CONV - 1 - shift : CONV - shift, :]
        return summed * jax.nn.sigmoid(summed)

    copies[4].wait()
    in_x = dot32(normed, w_x[...]).astype(jnp.bfloat16)
    heads_x = convolve_rows(in_x.astype(jnp.float32), past_x_ref, conv_x_ref)
    copies[5].wait()
    in_bc = dot32(normed, w_bc[...]).astype(jnp.bfloat16)
    conv_bcs = convolve_rows(in_bc.astype(jnp.float32), past_bc_ref, conv_bc_ref)
    b_part = conv_bcs[:, :STATE].astype(jnp.bfloat16)
    c_part = conv_bcs[:, STATE:].astype(jnp.bfloat16)

    def widen(values):
        lanes_scr[...] = jnp.zeros(lanes_scr.shape, jnp.float32)
        lanes_scr[:, :heads] = values
        return lanes_scr[...]

    spread_lanes = (
        lax.broadcasted_iota(jnp.int32, (tokens, inner), 0)
        == lax.broadcasted_iota(jnp.int32, (tokens, inner), 1) // SSM_DIM
    ).astype(jnp.float32)
    dt_in = dot32(normed, w_dt_ref[...], NEXT_TO).astype(jnp.bfloat16).astype(jnp.float32) + head_row(bias_ref)
    step = jnp.maximum(dt_in, 0.0) + jnp.log1p(jnp.exp(-jnp.abs(dt_in)))
    log_decay = exact_dot(same.astype(jnp.float32), widen(-step * head_row(rate_ref)))
    step_x = exact_dot(widen(step), spread_lanes)
    skip_x = exact_dot(widen(jnp.broadcast_to(head_row(skip_ref), (tokens, heads))), spread_lanes)
    decay_x = exact_dot(log_decay, spread_lanes)
    turned = log_decay.T
    intersection = dot32(c_part, b_part, NEXT_TO)
    scaled_x = heads_x * step_x
    low = lax.broadcasted_iota(jnp.int32, (tokens, 2 * SSM_DIM), 1) < SSM_DIM
    groups = []
    for pair in range(heads // 2):
        mixing = []
        for h in (2 * pair, 2 * pair + 1):
            gaps = log_decay[:, h : h + 1] - turned[h : h + 1, :]
            mixing.append(
                (jnp.exp(jnp.where(same, gaps, far_below)) * intersection).astype(jnp.bfloat16)
            )
        lanes = scaled_x[:, pair * 2 * SSM_DIM : (pair + 1) * 2 * SSM_DIM]
        both = jnp.concatenate([jnp.where(low, lanes, 0.0), jnp.where(low, 0.0, lanes)], axis=0)
        groups.append(dot32(jnp.concatenate(mixing, axis=1), both.astype(jnp.bfloat16)))
    copies[7].wait()
    carried = jnp.where(
        first_prompt,
        dot32(c_part, state[0].astype(jnp.bfloat16), NEXT_TO),
        dot32(c_part, state[1].astype(jnp.bfloat16), NEXT_TO),
    )
    ssm_out = jnp.concatenate(groups, axis=1) + carried * jnp.exp(decay_x) + skip_x * heads_x
    copies[6].wait()
    gate_z = dot32(normed, w_z[...]).astype(jnp.bfloat16).astype(jnp.float32)
    mixed_scr[:, query_width:] = (ssm_out * (gate_z * jax.nn.sigmoid(gate_z))).astype(jnp.bfloat16)

    own_rows = tokens // SIDE
    copies[8].wait()
    copies[9].wait()
    first_flip = jnp.where(core == 0, 3, 1)
    for out_ref, flips in ((far_ref, (first_flip, 2)), (near_ref, (0, first_flip ^ 2))):
        rows = jnp.concatenate(
            [
                mixed_scr[pl.ds(pl.multiple_of((rank ^ flip) * own_rows, own_rows), own_rows), :]
                for flip in flips
            ],
            axis=0,
        )
        out_ref[...] = dot32(rows, w_out[...]).astype(jnp.bfloat16)

    other = lax.broadcasted_iota(jnp.int32, (tokens, tokens), 1)
    pick = (other == request * DRAFT + last).astype(jnp.float32)
    final_log = exact_dot(pick, log_decay)
    final_x = exact_dot(final_log, spread_lanes)
    carry_x = jnp.exp(jnp.where(time <= last, final_x - decay_x, far_below))
    carried_x = (scaled_x * carry_x).T.astype(jnp.bfloat16)
    shrink = jnp.exp(final_x).T
    for r in range(requests):
        b_here = jnp.where(request == r, b_part, jnp.zeros_like(b_part))
        kept = shrink[:, r * DRAFT : r * DRAFT + 1] * state[member_ref[r]] + dot32(
            carried_x, b_here
        )
        kept_ref[r, :inner, :] = kept.astype(jnp.bfloat16)

    def kept_rows(first_request, count, slots, series, past_of):
        at = lax.broadcasted_iota(jnp.int32, (count * slots, 1), 0)
        here, edge = at // slots, at % slots
        start = jnp.zeros((count * slots, 1), jnp.int32)
        owner = jnp.zeros((count * slots, 1), jnp.int32)
        for r in range(count):
            start = jnp.where(here == r, accepted_ref[first_request + r], start)
            owner = jnp.where(here == r, member_ref[first_request + r], owner)
        index = start + edge
        token = (here + first_request) * DRAFT + index - (CONV - 1)
        chosen = (lax.broadcasted_iota(jnp.int32, (count * slots, tokens), 1) == token) & (
            index >= CONV - 1
        )
        rows = dot32(chosen.astype(jnp.bfloat16), series)
        for p in range(PROMPTS):
            for j in range(CONV - 1):
                rows = jnp.where((owner == p) & (index == j), past_of(j, p), rows)
        return rows.astype(jnp.bfloat16)

    for lanes in range(2):
        cut = slice(lanes * STATE, min((lanes + 1) * STATE, inner))
        rows = kept_rows(
            0, requests, 8, in_x[:, cut], lambda j, p: past_x_ref[j, p : p + 1, cut].astype(jnp.float32)
        )
        for r in range(requests):
            kept_ref[r, inner + 8 * lanes : inner + 8 * (lanes + 1), : rows.shape[1]] = rows[
                r * 8 : (r + 1) * 8
            ]
    kept_ref[:, inner + 8 :, inner - STATE :] = jnp.zeros(
        (requests, 8, 2 * STATE - inner), jnp.bfloat16
    )
    kept_bc_ref[...] = kept_rows(
        rank * (requests // SIDE),
        requests // SIDE,
        8,
        in_bc,
        lambda j, p: past_bc_ref[j, p : p + 1, :].astype(jnp.float32),
    )


def mixer(
    hidden, mixer_gain, w_query, w_kv, w_attn_out, prompt_kv, prompt_lengths, member, accepted, w_z, w_x, w_bc,
    w_dt, conv_x, conv_bc, ssm_rate, dt_bias, skip_d, prompt_state, prompt_conv_x, prompt_conv_bc, w_mamba_out,
):
    tokens, width = hidden.shape
    requests = tokens // DRAFT
    inner = w_x.shape[1]
    query_width = w_query.shape[1]
    bf16 = jnp.bfloat16
    state = prompt_state.reshape(PROMPTS, inner, STATE)
    small = [
        hidden, mixer_gain.reshape(-1, 128), w_dt.T, conv_x, conv_bc,
        prompt_conv_x.transpose(1, 0, 2), prompt_conv_bc.transpose(1, 0, 2),
    ]
    scalars = [member, accepted, prompt_lengths, ssm_rate, dt_bias, skip_d]
    whole = pl.BlockSpec(memory_space=pltpu.VMEM)
    return pl.pallas_call(
        mixer_kernel,
        out_shape=[
            jax.ShapeDtypeStruct((tokens // 2, width), bf16),
            jax.ShapeDtypeStruct((tokens // 2, width), bf16),
            jax.ShapeDtypeStruct((requests, inner + 16, STATE), bf16),
            jax.ShapeDtypeStruct((requests // SIDE * 8, 2 * STATE), bf16),
        ],
        in_specs=[pl.BlockSpec(memory_space=pltpu.HBM)] * 22,
        out_specs=[whole] * 4,
        scratch_shapes=[
            *(pltpu.SMEM(a.shape, a.dtype) for a in scalars),
            *(pltpu.VMEM(a.shape, a.dtype) for a in small),
            pltpu.VMEM(w_query.shape, bf16),
            pltpu.VMEM(w_kv.shape[1:], bf16),
            pltpu.VMEM((PROMPTS, *prompt_kv.shape[2:]), bf16),
            pltpu.VMEM(w_x.shape, bf16),
            pltpu.VMEM(w_bc.shape, bf16),
            pltpu.VMEM(w_z.shape, bf16),
            pltpu.VMEM(state.shape, jnp.float32),
            pltpu.VMEM((query_width + inner, width), bf16),
            pltpu.VMEM((tokens, query_width + inner), bf16),
            pltpu.VMEM((tokens, 128), jnp.float32),
            pltpu.SemaphoreType.DMA((23,)),
        ],
        compiler_params=pltpu.CompilerParams(vmem_limit_bytes=59 << 20),
        cost_estimate=pl.CostEstimate(
            flops=3_000_000_000, bytes_accessed=20_000_000, transcendentals=1_000_000
        ),
        name="mixer",
    )(
        *scalars, *small, w_query, w_kv, prompt_kv, w_x, w_bc, w_z, state, w_attn_out, w_mamba_out
    )


def feed_kernel(first_ref, second_ref, both_ref, down_ref, _, first_out, second_out):
    hidden = down_ref.shape[0]
    rows = first_ref.shape[0]
    joined = jnp.concatenate([first_ref[...], second_ref[...]], axis=0)
    pair = dot32(joined, both_ref[...])
    gate, up = pair[:, :hidden], pair[:, hidden:]
    active = (gate * jax.nn.sigmoid(gate) * up).astype(jnp.bfloat16)
    parts = dot32(active, down_ref[...]).astype(jnp.bfloat16)
    first_out[...] = parts[:rows]
    second_out[...] = parts[rows:]


def feed(first, second, w_both, w_down, token):
    rows, width = first.shape
    whole = pl.BlockSpec(memory_space=pltpu.VMEM)
    return pl.pallas_call(
        feed_kernel,
        out_shape=[jax.ShapeDtypeStruct((rows, width), jnp.bfloat16)] * 2,
        in_specs=[whole] * 4 + [pl.BlockSpec(memory_space=pl.ANY)],
        out_specs=[whole] * 2,
        compiler_params=pltpu.CompilerParams(vmem_limit_bytes=16 << 20),
        cost_estimate=pl.CostEstimate(
            flops=20 * 2 * rows * width * 2 * 3 * w_down.shape[0],
            bytes_accessed=4 * rows * width * 2 + 3 * w_down.size * 2,
            transcendentals=2 * rows * w_down.shape[0],
        ),
        name="feed",
    )(first, second, w_both, w_down, token)


def head_kernel(targets_ref, owners_ref, *refs):
    count = targets_ref.shape[0]
    rows_refs, head_ref, others, out_ref = refs[:count], refs[count], refs[count + 1 : -1], refs[-1]
    vocab = head_ref.shape[0]
    lanes = 2 * rows_refs[0].shape[0]
    slots = out_ref.shape[0]
    base = lax.axis_index("req") * vocab
    lane = lax.broadcasted_iota(jnp.int32, (lanes, 128), 0)
    column = lax.broadcasted_iota(jnp.int32, (lanes, 128), 1)
    fragment = (lane >= lanes // 2).astype(jnp.int32)
    place = (column == fragment * DRAFT + lane % DRAFT).astype(jnp.bfloat16)
    ids = lax.broadcasted_iota(jnp.int32, (vocab, lanes), 0) + base
    slot = lax.broadcasted_iota(jnp.int32, (slots, lanes), 0)
    packed = jnp.zeros(out_ref.shape, jnp.float32)
    for other in others:
        packed = packed + other[...]
    for pair in range(count // 2):
        joined = jnp.concatenate([rows_refs[2 * pair][...], rows_refs[2 * pair + 1][...]], axis=0)
        wanted = jnp.concatenate(
            [targets_ref[2 * pair : 2 * pair + 1, :], targets_ref[2 * pair + 1 : 2 * pair + 2, :]],
            axis=1,
        )
        owner = jnp.concatenate(
            [owners_ref[2 * pair : 2 * pair + 1, :], owners_ref[2 * pair + 1 : 2 * pair + 2, :]],
            axis=1,
        )
        logits = dot32(head_ref[...], joined, NEXT_TO)
        target = jnp.sum(jnp.where(ids == wanted, logits, 0.0), axis=0, keepdims=True)
        top = jnp.max(logits, axis=0, keepdims=True)
        total = jnp.sum(jnp.exp(logits - top), axis=0, keepdims=True)
        stats = jnp.where(slot % 8 == 0, top, jnp.where(slot % 8 == 1, total, target))
        rest = jnp.where((slot // 8 == owner) & (slot % 8 < 3), stats, 0.0)
        for _ in range(3):
            part = rest.astype(jnp.bfloat16)
            packed = packed + dot32(part, place)
            rest = rest - part.astype(jnp.float32)
    out_ref[...] = packed


def head_stats(targets, owners, rows, head_weight, devices, others=()):
    whole = pl.BlockSpec(memory_space=pltpu.VMEM)
    return pl.pallas_call(
        head_kernel,
        out_shape=jax.ShapeDtypeStruct((devices * 8, 128), jnp.float32),
        in_specs=[whole] * (3 + len(rows) + len(others)),
        out_specs=whole,
        compiler_params=pltpu.CompilerParams(vmem_limit_bytes=32 << 20),
        cost_estimate=pl.CostEstimate(
            flops=10 * 2 * len(rows) * rows[0].size * head_weight.shape[0],
            bytes_accessed=2 * len(rows) * rows[0].size + 2 * head_weight.size,
            transcendentals=len(rows) * rows[0].shape[0] * head_weight.shape[0],
        ),
        name="head_stats",
    )(targets, owners, *rows, head_weight, *others)


def mdl_pairs(step):
    pairs = []
    for device in range(SIDE * SIDE * CORES):
        flip = (3, 1)[(device + step) % 2]
        pairs += [(device * SIDE + z, device * SIDE + (z ^ flip)) for z in range(SIDE)]
    return pairs


def shards(
    hidden_in,
    mixer_gain,
    w_query,
    w_kv,
    w_attn_out,
    prompt_kv,
    prompt_lengths,
    member,
    accepted,
    w_z,
    w_x,
    w_bc,
    w_dt,
    conv_x,
    conv_bc,
    ssm_rate,
    dt_bias,
    skip_d,
    prompt_state,
    prompt_conv_x,
    prompt_conv_bc,
    w_mamba_out,
    mlp_gain,
    w_gate,
    w_up,
    w_down,
    final_gain,
    head_weight,
    draft_ids,
):
    row_reqs, draft_len, width = hidden_in.shape
    mdl_count = lax.axis_size("mdl")
    req_count = lax.axis_size("req")
    mdl_rank = lax.axis_index("mdl")
    req_rank = lax.axis_index("req")
    row_tokens = row_reqs * draft_len
    own_reqs = row_reqs // mdl_count
    own_tokens = own_reqs * draft_len
    flat_rows = hidden_in.reshape(row_tokens, width)
    local_inner = w_x.shape[1]
    edge_len = CONV - 1
    far, near, kept, own_bc = mixer(
        flat_rows, mixer_gain, w_query, w_kv, w_attn_out, prompt_kv, prompt_lengths, member, accepted, w_z, w_x, w_bc,
        w_dt, conv_x, conv_bc, ssm_rate, dt_bias, skip_d, prompt_state, prompt_conv_x, prompt_conv_bc, w_mamba_out,
    )
    kept_out = lax.all_to_all(
        kept.reshape(mdl_count, own_reqs, local_inner + 16, STATE),
        "mdl",
        split_axis=0,
        concat_axis=0,
        tiled=True,
    )

    came = lax.ppermute(far, ("req", "mdl"), mdl_pairs(0))
    last = lax.ppermute(added(near[own_tokens:], came[own_tokens:]), ("req", "mdl"), mdl_pairs(1))
    mixed = (
        near[:own_tokens].astype(jnp.float32)
        + came[:own_tokens].astype(jnp.float32)
        + last.astype(jnp.float32)
    )
    own_rows = lax.dynamic_slice_in_dim(flat_rows, mdl_rank * own_tokens, own_tokens, 0)
    after_mixer = (own_rows.astype(jnp.float32) + mixed).astype(jnp.bfloat16)
    prepared = rms_scale(after_mixer, mlp_gain).astype(jnp.bfloat16)
    w_both = jnp.concatenate([w_gate, w_up], axis=1)
    early, late = gather_rows([prepared[:draft_len], prepared[draft_len:]])

    core = req_rank % CORES
    chip_x = req_rank // CORES % SIDE
    chip_y = req_rank // (CORES * SIDE)
    table = jnp.where(core == 0, jnp.asarray(block_table()[0]), jnp.asarray(block_table()[1]))
    owner = ((chip_y ^ table[:, 0]) * SIDE + (chip_x ^ table[:, 1])) * CORES + (core ^ table[:, 2])
    request = owner * row_reqs + mdl_rank * own_reqs + table[:, 3]
    next_ids = jnp.concatenate([draft_ids[:, 1:], draft_ids[:, :1]], axis=1)
    picked = (request[:, None] == jnp.arange(draft_ids.shape[0])[None, :]).astype(jnp.float32)
    targets = jnp.dot(picked, next_ids.astype(jnp.float32), precision=HIGHEST).astype(jnp.int32)
    targets = targets.reshape(8, 8 * draft_len)
    owners = jnp.broadcast_to(owner[:, None], (64, draft_len)).reshape(8, 8 * draft_len)

    token = jnp.zeros((8, 128), jnp.float32)
    early_parts = [feed(*rows, w_both, w_down, token) for rows in early]
    later_token, kept_out = lax.optimization_barrier((token, kept_out))
    late_parts = [
        feed(*late[0], w_both, w_down, token),
        feed(*late[1], w_both, w_down, later_token),
    ]
    summed = jnp.concatenate(scatter_rows(early_parts, late_parts), axis=0)
    kept_state = (
        kept_out[:, :, :local_inner, :]
        .transpose(1, 0, 2, 3)
        .astype(jnp.float32)
        .reshape(own_reqs, mdl_count * local_inner // SSM_DIM, SSM_DIM, STATE)
    )
    edges = kept_out[:, :, local_inner:, :]
    edges = jnp.concatenate(
        [edges[:, :, :edge_len, :], edges[:, :, 8 : 8 + edge_len, : local_inner - STATE]], axis=3
    )
    kept_conv = jnp.concatenate(
        [
            edges.transpose(1, 2, 0, 3).reshape(own_reqs, edge_len, mdl_count * local_inner),
            own_bc.reshape(own_reqs, 8, 2 * STATE)[:, :edge_len, :],
        ],
        axis=2,
    )
    final_gain, kept_state, kept_conv, targets, owners = lax.optimization_barrier(
        (final_gain, kept_state, kept_conv, targets, owners)
    )
    after_feed = added(after_mixer, summed)
    final_rows = rms_scale(after_feed, final_gain).astype(jnp.bfloat16)
    early, late = gather_rows([final_rows[:draft_len], final_rows[draft_len:]])
    stats = [
        head_stats(targets[:4], owners[:4], early[0] + early[1], head_weight, req_count),
        head_stats(targets[4:6], owners[4:6], late[0], head_weight, req_count),
    ]
    stats = head_stats(targets[6:], owners[6:], late[1], head_weight, req_count, stats)
    shared = lax.all_to_all(stats, "req", split_axis=0, concat_axis=0, tiled=True)
    shared = shared.reshape(req_count, 8, 128)[:, :, :own_tokens]
    tops, totals, hits = shared[:, 0], shared[:, 1], shared[:, 2]
    top = jnp.max(tops, axis=0)
    total = jnp.sum(totals * jnp.exp(tops - top[None, :]), axis=0)
    log_total = top + jnp.log(total)
    position = jnp.arange(own_tokens) % draft_len
    verify_scores = jnp.where(
        position < draft_len - 1, jnp.sum(hits, axis=0) - log_total, top - log_total
    ).reshape(own_reqs, draft_len)
    return (
        after_feed.reshape(own_reqs, draft_len, width),
        verify_scores,
        kept_state,
        kept_conv,
    )


def solution(mesh):
    in_specs = (
        P("req", None, None),
        P(),
        P(None, "mdl"),
        P(),
        P("mdl", None),
        P("req", None, None, None),
        P("req"),
        P("req"),
        P("req"),
        P(None, "mdl"),
        P(None, "mdl"),
        P(),
        P(None, "mdl"),
        P(None, "mdl"),
        P(),
        P("mdl"),
        P("mdl"),
        P("mdl"),
        P("req", "mdl", None, None),
        P("req", None, "mdl"),
        P("req", None, None),
        P("mdl", None),
        P(),
        P(None, "req"),
        P(None, "req"),
        P("req", None),
        P(),
        P("req", None),
        P(),
    )
    out_specs = (
        P(("req", "mdl"), None, None),
        P(("req", "mdl"), None),
        P(("req", "mdl"), None, None, None),
        P(("req", "mdl"), None, None),
    )
    return jax.shard_map(shards, mesh=mesh, in_specs=in_specs, out_specs=out_specs, check_vma=False)
```

```python
import functools

import jax
import jax.numpy as jnp
import numpy as np
from jax import lax
from jax.experimental import pallas as pl
from jax.experimental.pallas import tpu as pltpu
from jax.sharding import PartitionSpec as P

Q_HEADS = 8
KV_HEADS = 2
HEAD_DIM = 128
SSM_DIM = 64
STATE = 256
CONV = 4
PROMPTS = 2
P_MAX = 1024
DRAFT = 16
SIDE = 4
CORES = 2

eps_norm = 1e-05
far_below = -1e30

DIRECT = (1, 3, 2)
EDGES = ((1, 3), (3, 1))


def device_at(y, x, core):
    return (y * SIDE + x) * CORES + core


def flip_pairs(ring, flip):
    pairs = []
    for y in range(SIDE):
        for x in range(SIDE):
            for core in range(CORES):
                on_x = ring == core
                target = device_at(y if on_x else y ^ flip, x ^ flip if on_x else x, core)
                pairs.append((device_at(y, x, core), target))
    return pairs


CORE_PAIRS = [(device, device ^ 1) for device in range(SIDE * SIDE * CORES)]


def hop(part, ring, flip):
    return lax.ppermute(part, "req", flip_pairs(ring, flip))


def swap_core(part):
    return lax.ppermute(part, "req", CORE_PAIRS)


def gather_rows(rows):
    came = [hop(rows, 0, flip) for flip in DIRECT]
    held = [jnp.concatenate([rows, came[0]], axis=0), jnp.concatenate(came[1:], axis=0)]
    came = [hop(held[s], 1, EDGES[s][0]) for s in range(2)]
    held = [jnp.concatenate([held[s], came[s]], axis=0) for s in range(2)]
    late = [hop(held[s], 1, EDGES[s][1]) for s in range(2)]
    return held, late


def added(left, right):
    return (left.astype(jnp.float32) + right.astype(jnp.float32)).astype(jnp.bfloat16)


def scatter_rows(early, late):
    came = [swap_core(part) for part in late[1]]
    late = [hop(added(late[0][s], came[s]), 1, EDGES[s][1]) for s in range(2)]
    came = [swap_core(part) for part in early[1]]
    held = [added(early[0][s], came[s]) for s in range(2)]
    held = [added(held[s], late[s]) for s in range(2)]
    half = held[0].shape[0] // 2
    came = [hop(held[s][half:], 1, EDGES[s][0]) for s in range(2)]
    held = [added(held[s][:half], came[s]) for s in range(2)]
    half = half // 2
    blocks = (held[0][half:], held[1][:half], held[1][half:])
    came = [hop(block, 0, flip) for block, flip in zip(blocks, DIRECT, strict=True)]
    return sum((part.astype(jnp.float32) for part in came), held[0][:half].astype(jnp.float32))


def block_table():
    table = np.zeros((CORES, 2, 2, 2, 2, 2, 2, 4), np.int32)
    for core, late, half, stream, second, block, request in np.ndindex(table.shape[:-1]):
        first = ((0, 1), (3, 2))[stream][block]
        other = (EDGES[stream][1] if late else 0) ^ (EDGES[stream][0] if second else 0)
        y, x = (other, first) if core == half else (first, other)
        table[core, late, half, stream, second, block, request] = (y, x, half, request)
    return table.reshape(CORES, 64, 4)


def rms_scale(values, gain):
    widened = values.astype(jnp.float32)
    spread = jnp.mean(widened * widened, axis=-1, keepdims=True)
    return widened * lax.rsqrt(spread + eps_norm) * gain.astype(jnp.float32)


HIGHEST = lax.Precision.HIGHEST
NEXT_TO = (((1,), (1,)), ((), ()))


def dot32(left, right, dims=None):
    dims = dims or (((1,), (0,)), ((), ()))
    return lax.dot_general(left, right, dims, preferred_element_type=jnp.float32)


def exact_dot(left, right):
    return jnp.dot(left, right, precision=HIGHEST, preferred_element_type=jnp.float32)


def mixer_kernel(*refs):
    sources, refs = refs[:22], refs[22:]
    far_ref, near_ref, kept_ref, kept_bc_ref = refs[:4]
    held, (mixed_scr, lanes_scr, sems) = refs[4:-3], refs[-3:]
    member_ref, accepted_ref, lengths_ref, rate_ref, bias_ref, skip_ref = held[:6]
    hidden_ref, gain_ref, w_dt_ref, conv_x_ref, conv_bc_ref, past_x_ref, past_bc_ref = held[6:13]
    w_query, w_kv, prompt, w_x, w_bc, w_z, state, w_out = held[13:]
    tokens = hidden_ref.shape[0]
    requests = tokens // DRAFT
    inner = w_x.shape[1]
    heads = inner // SSM_DIM
    query_width = w_query.shape[1]
    rank = lax.axis_index("mdl")
    core = lax.axis_index("req") % CORES
    group = rank * (query_width // HEAD_DIM) // (Q_HEADS // KV_HEADS)
    query_hbm, kv_hbm, prompt_hbm, x_hbm, bc_hbm, z_hbm, state_hbm, attn_hbm, mamba_hbm = sources[13:]
    moves = [(source, target) for source, target in zip(sources[:13], held[:13], strict=True)]
    moves += [
        (query_hbm, w_query),
        (kv_hbm.at[group], w_kv),
        (prompt_hbm.at[0, group], prompt.at[0]),
        (prompt_hbm.at[1, group], prompt.at[1]),
        (x_hbm, w_x),
        (bc_hbm, w_bc),
        (z_hbm, w_z),
        (state_hbm, state),
        (attn_hbm, w_out.at[pl.ds(0, query_width), :]),
        (mamba_hbm, w_out.at[pl.ds(query_width, inner), :]),
    ]
    started = [
        pltpu.make_async_copy(source, target, sems.at[index])
        for index, (source, target) in enumerate(moves)
    ]
    for copy in started:
        copy.start()
    for copy in started[:13]:
        copy.wait()
    copies = started[13:]

    def head_row(ref):
        lane = lax.broadcasted_iota(jnp.int32, (1, heads), 1)
        values = jnp.zeros((1, heads), jnp.float32)
        for h in range(heads):
            values = jnp.where(lane == h, ref[h], values)
        return values

    row = lax.broadcasted_iota(jnp.int32, (tokens, 1), 0)
    time, request = row % DRAFT, row // DRAFT
    own_prompt = jnp.zeros((tokens, 1), jnp.int32)
    last = jnp.zeros((tokens, 1), jnp.int32)
    for r in range(requests):
        own_prompt = jnp.where(request == r, member_ref[r], own_prompt)
        last = jnp.where(request == r, accepted_ref[r] - 1, last)
    first_prompt = own_prompt == 0

    gain = jnp.concatenate(
        [gain_ref[j : j + 1, :].astype(jnp.float32) for j in range(gain_ref.shape[0])], axis=1
    )
    widened = hidden_ref[...].astype(jnp.float32)
    spread = jnp.mean(widened * widened, axis=-1, keepdims=True)
    normed = (
        widened * lax.rsqrt(spread + eps_norm) * gain
    ).astype(jnp.bfloat16)

    copies[0].wait()
    queries = dot32(normed, w_query[...]).astype(jnp.bfloat16)
    copies[1].wait()
    drafts = dot32(normed, w_kv[...]).astype(jnp.bfloat16)
    local_heads = query_width // HEAD_DIM
    query_rows = jnp.concatenate(
        [queries[:, h * HEAD_DIM : (h + 1) * HEAD_DIM] for h in range(local_heads)], axis=0
    )
    scale = HEAD_DIM**-0.5
    row_first = jnp.concatenate([own_prompt] * local_heads, axis=0) == 0
    draft_scores = dot32(query_rows, drafts[:, :HEAD_DIM], NEXT_TO) * scale
    same = (row // DRAFT == lax.broadcasted_iota(jnp.int32, (tokens, tokens), 1) // DRAFT) & (
        lax.broadcasted_iota(jnp.int32, (tokens, tokens), 1) <= row
    )
    draft_mask = jnp.concatenate([same] * local_heads, axis=0)
    draft_scores = jnp.where(draft_mask, draft_scores, far_below)
    copies[2].wait()
    copies[3].wait()
    scores = jnp.where(
        row_first,
        dot32(query_rows, prompt[0, :, :HEAD_DIM], NEXT_TO),
        dot32(query_rows, prompt[1, :, :HEAD_DIM], NEXT_TO),
    )
    length = jnp.where(row_first, lengths_ref[0], lengths_ref[1])
    position = lax.broadcasted_iota(jnp.int32, scores.shape, 1)
    scores = jnp.where(position < length, scores * scale, far_below)
    top = jnp.maximum(
        jnp.max(scores, axis=1, keepdims=True), jnp.max(draft_scores, axis=1, keepdims=True)
    )
    weights = jnp.exp(scores - top)
    draft_weights = jnp.exp(draft_scores - top)
    total = jnp.sum(weights, axis=1, keepdims=True) + jnp.sum(draft_weights, axis=1, keepdims=True)
    weighted = (
        dot32(jnp.where(row_first, weights, 0.0).astype(jnp.bfloat16), prompt[0, :, HEAD_DIM:])
        + dot32(jnp.where(row_first, 0.0, weights).astype(jnp.bfloat16), prompt[1, :, HEAD_DIM:])
        + dot32(draft_weights.astype(jnp.bfloat16), drafts[:, HEAD_DIM:])
    )
    attended = (weighted / total).astype(jnp.bfloat16)
    for h in range(local_heads):
        mixed_scr[:, h * HEAD_DIM : (h + 1) * HEAD_DIM] = attended[h * tokens : (h + 1) * tokens]

    def convolve_rows(series, past_ref, taps_ref):
        past = [
            jnp.where(
                first_prompt,
                past_ref[j, 0:1, :].astype(jnp.float32),
                past_ref[j, 1:2, :].astype(jnp.float32),
            )
            for j in range(CONV - 1)
        ]
        taps = taps_ref[...].astype(jnp.float32)
        summed = series * taps[CONV - 1 : CONV, :]
        for shift in range(1, CONV):
            window = pltpu.roll(series, shift, 0)
            for t in range(shift):
                window = jnp.where(time == t, past[CONV - 1 - shift + t], window)
            summed = summed + window * taps[CONV - 1 - shift : CONV - shift, :]
        return summed * jax.nn.sigmoid(summed)

    copies[4].wait()
    in_x = dot32(normed, w_x[...]).astype(jnp.bfloat16)
    heads_x = convolve_rows(in_x.astype(jnp.float32), past_x_ref, conv_x_ref)
    copies[5].wait()
    in_bc = dot32(normed, w_bc[...]).astype(jnp.bfloat16)
    conv_bcs = convolve_rows(in_bc.astype(jnp.float32), past_bc_ref, conv_bc_ref)
    b_part = conv_bcs[:, :STATE].astype(jnp.bfloat16)
    c_part = conv_bcs[:, STATE:].astype(jnp.bfloat16)

    def widen(values):
        lanes_scr[...] = jnp.zeros(lanes_scr.shape, jnp.float32)
        lanes_scr[:, :heads] = values
        return lanes_scr[...]

    spread_lanes = (
        lax.broadcasted_iota(jnp.int32, (tokens, inner), 0)
        == lax.broadcasted_iota(jnp.int32, (tokens, inner), 1) // SSM_DIM
    ).astype(jnp.float32)
    dt_in = dot32(normed, w_dt_ref[...], NEXT_TO).astype(jnp.bfloat16).astype(jnp.float32) + head_row(bias_ref)
    step = jnp.maximum(dt_in, 0.0) + jnp.log1p(jnp.exp(-jnp.abs(dt_in)))
    log_decay = exact_dot(same.astype(jnp.float32), widen(-step * head_row(rate_ref)))
    step_x = exact_dot(widen(step), spread_lanes)
    skip_x = exact_dot(widen(jnp.broadcast_to(head_row(skip_ref), (tokens, heads))), spread_lanes)
    decay_x = exact_dot(log_decay, spread_lanes)
    turned = log_decay.T
    intersection = dot32(c_part, b_part, NEXT_TO)
    scaled_x = heads_x * step_x
    low = lax.broadcasted_iota(jnp.int32, (tokens, 2 * SSM_DIM), 1) < SSM_DIM
    groups = []
    for pair in range(heads // 2):
        mixing = []
        for h in (2 * pair, 2 * pair + 1):
            gaps = log_decay[:, h : h + 1] - turned[h : h + 1, :]
            mixing.append(
                (jnp.exp(jnp.where(same, gaps, far_below)) * intersection).astype(jnp.bfloat16)
            )
        lanes = scaled_x[:, pair * 2 * SSM_DIM : (pair + 1) * 2 * SSM_DIM]
        both = jnp.concatenate([jnp.where(low, lanes, 0.0), jnp.where(low, 0.0, lanes)], axis=0)
        groups.append(dot32(jnp.concatenate(mixing, axis=1), both.astype(jnp.bfloat16)))
    copies[7].wait()
    carried = jnp.where(
        first_prompt,
        dot32(c_part, state[0].astype(jnp.bfloat16), NEXT_TO),
        dot32(c_part, state[1].astype(jnp.bfloat16), NEXT_TO),
    )
    ssm_out = jnp.concatenate(groups, axis=1) + carried * jnp.exp(decay_x) + skip_x * heads_x
    copies[6].wait()
    gate_z = dot32(normed, w_z[...]).astype(jnp.bfloat16).astype(jnp.float32)
    mixed_scr[:, query_width:] = (ssm_out * (gate_z * jax.nn.sigmoid(gate_z))).astype(jnp.bfloat16)

    own_rows = tokens // SIDE
    copies[8].wait()
    copies[9].wait()
    first_flip = jnp.where(core == 0, 3, 1)
    for out_ref, flips in ((far_ref, (first_flip, 2)), (near_ref, (0, first_flip ^ 2))):
        rows = jnp.concatenate(
            [
                mixed_scr[pl.ds(pl.multiple_of((rank ^ flip) * own_rows, own_rows), own_rows), :]
                for flip in flips
            ],
            axis=0,
        )
        out_ref[...] = dot32(rows, w_out[...]).astype(jnp.bfloat16)

    other = lax.broadcasted_iota(jnp.int32, (tokens, tokens), 1)
    pick = (other == request * DRAFT + last).astype(jnp.float32)
    final_log = exact_dot(pick, log_decay)
    final_x = exact_dot(final_log, spread_lanes)
    carry_x = jnp.exp(jnp.where(time <= last, final_x - decay_x, far_below))
    carried_x = (scaled_x * carry_x).T.astype(jnp.bfloat16)
    shrink = jnp.exp(final_x).T
    for r in range(requests):
        b_here = jnp.where(request == r, b_part, jnp.zeros_like(b_part))
        kept = shrink[:, r * DRAFT : r * DRAFT + 1] * state[member_ref[r]] + dot32(
            carried_x, b_here
        )
        kept_ref[r, :inner, :] = kept.astype(jnp.bfloat16)

    def kept_rows(first_request, count, slots, series, past_of):
        at = lax.broadcasted_iota(jnp.int32, (count * slots, 1), 0)
        here, edge = at // slots, at % slots
        start = jnp.zeros((count * slots, 1), jnp.int32)
        owner = jnp.zeros((count * slots, 1), jnp.int32)
        for r in range(count):
            start = jnp.where(here == r, accepted_ref[first_request + r], start)
            owner = jnp.where(here == r, member_ref[first_request + r], owner)
        index = start + edge
        token = (here + first_request) * DRAFT + index - (CONV - 1)
        chosen = (lax.broadcasted_iota(jnp.int32, (count * slots, tokens), 1) == token) & (
            index >= CONV - 1
        )
        rows = dot32(chosen.astype(jnp.bfloat16), series)
        for p in range(PROMPTS):
            for j in range(CONV - 1):
                rows = jnp.where((owner == p) & (index == j), past_of(j, p), rows)
        return rows.astype(jnp.bfloat16)

    for lanes in range(2):
        cut = slice(lanes * STATE, min((lanes + 1) * STATE, inner))
        rows = kept_rows(
            0, requests, 8, in_x[:, cut], lambda j, p: past_x_ref[j, p : p + 1, cut].astype(jnp.float32)
        )
        for r in range(requests):
            kept_ref[r, inner + 8 * lanes : inner + 8 * (lanes + 1), : rows.shape[1]] = rows[
                r * 8 : (r + 1) * 8
            ]
    kept_ref[:, inner + 8 :, inner - STATE :] = jnp.zeros(
        (requests, 8, 2 * STATE - inner), jnp.bfloat16
    )
    kept_bc_ref[...] = kept_rows(
        rank * (requests // SIDE),
        requests // SIDE,
        8,
        in_bc,
        lambda j, p: past_bc_ref[j, p : p + 1, :].astype(jnp.float32),
    )


def mixer(
    hidden, mixer_gain, w_query, w_kv, w_attn_out, prompt_kv, prompt_lengths, member, accepted, w_z, w_x, w_bc,
    w_dt, conv_x, conv_bc, ssm_rate, dt_bias, skip_d, prompt_state, prompt_conv_x, prompt_conv_bc, w_mamba_out,
):
    tokens, width = hidden.shape
    requests = tokens // DRAFT
    inner = w_x.shape[1]
    query_width = w_query.shape[1]
    bf16 = jnp.bfloat16
    state = prompt_state.reshape(PROMPTS, inner, STATE)
    small = [
        hidden, mixer_gain.reshape(-1, 128), w_dt.T, conv_x, conv_bc,
        prompt_conv_x.transpose(1, 0, 2), prompt_conv_bc.transpose(1, 0, 2),
    ]
    scalars = [member, accepted, prompt_lengths, ssm_rate, dt_bias, skip_d]
    whole = pl.BlockSpec(memory_space=pltpu.VMEM)
    return pl.pallas_call(
        mixer_kernel,
        out_shape=[
            jax.ShapeDtypeStruct((tokens // 2, width), bf16),
            jax.ShapeDtypeStruct((tokens // 2, width), bf16),
            jax.ShapeDtypeStruct((requests, inner + 16, STATE), bf16),
            jax.ShapeDtypeStruct((requests // SIDE * 8, 2 * STATE), bf16),
        ],
        in_specs=[pl.BlockSpec(memory_space=pltpu.HBM)] * 22,
        out_specs=[whole] * 4,
        scratch_shapes=[
            *(pltpu.SMEM(a.shape, a.dtype) for a in scalars),
            *(pltpu.VMEM(a.shape, a.dtype) for a in small),
            pltpu.VMEM(w_query.shape, bf16),
            pltpu.VMEM(w_kv.shape[1:], bf16),
            pltpu.VMEM((PROMPTS, *prompt_kv.shape[2:]), bf16),
            pltpu.VMEM(w_x.shape, bf16),
            pltpu.VMEM(w_bc.shape, bf16),
            pltpu.VMEM(w_z.shape, bf16),
            pltpu.VMEM(state.shape, jnp.float32),
            pltpu.VMEM((query_width + inner, width), bf16),
            pltpu.VMEM((tokens, query_width + inner), bf16),
            pltpu.VMEM((tokens, 128), jnp.float32),
            pltpu.SemaphoreType.DMA((23,)),
        ],
        compiler_params=pltpu.CompilerParams(vmem_limit_bytes=59 << 20),
        cost_estimate=pl.CostEstimate(
            flops=3_000_000_000, bytes_accessed=20_000_000, transcendentals=1_000_000
        ),
        name="mixer",
    )(
        *scalars, *small, w_query, w_kv, prompt_kv, w_x, w_bc, w_z, state, w_attn_out, w_mamba_out
    )


def feed_kernel(first_ref, second_ref, both_ref, down_ref, _, first_out, second_out):
    hidden = down_ref.shape[0]
    rows = first_ref.shape[0]
    joined = jnp.concatenate([first_ref[...], second_ref[...]], axis=0)
    pair = dot32(joined, both_ref[...])
    gate, up = pair[:, :hidden], pair[:, hidden:]
    active = (gate * jax.nn.sigmoid(gate) * up).astype(jnp.bfloat16)
    parts = dot32(active, down_ref[...]).astype(jnp.bfloat16)
    first_out[...] = parts[:rows]
    second_out[...] = parts[rows:]


def feed(first, second, w_both, w_down, token):
    rows, width = first.shape
    whole = pl.BlockSpec(memory_space=pltpu.VMEM)
    return pl.pallas_call(
        feed_kernel,
        out_shape=[jax.ShapeDtypeStruct((rows, width), jnp.bfloat16)] * 2,
        in_specs=[whole] * 4 + [pl.BlockSpec(memory_space=pl.ANY)],
        out_specs=[whole] * 2,
        compiler_params=pltpu.CompilerParams(vmem_limit_bytes=16 << 20),
        cost_estimate=pl.CostEstimate(
            flops=20 * 2 * rows * width * 2 * 3 * w_down.shape[0],
            bytes_accessed=4 * rows * width * 2 + 3 * w_down.size * 2,
            transcendentals=2 * rows * w_down.shape[0],
        ),
        name="feed",
    )(first, second, w_both, w_down, token)


def head_kernel(targets_ref, owners_ref, *refs):
    count = targets_ref.shape[0]
    rows_refs, head_ref, others, out_ref = refs[:count], refs[count], refs[count + 1 : -1], refs[-1]
    vocab = head_ref.shape[0]
    lanes = 2 * rows_refs[0].shape[0]
    slots = out_ref.shape[0]
    base = lax.axis_index("req") * vocab
    lane = lax.broadcasted_iota(jnp.int32, (lanes, 128), 0)
    column = lax.broadcasted_iota(jnp.int32, (lanes, 128), 1)
    place = (column == lane % (2 * DRAFT)).astype(jnp.bfloat16)
    ids = lax.broadcasted_iota(jnp.int32, (vocab, lanes), 0) + base
    slot = lax.broadcasted_iota(jnp.int32, (slots, lanes), 0)
    packed = jnp.zeros(out_ref.shape, jnp.float32)
    for other in others:
        packed = packed + other[...]
    for pair in range(count // 2):
        joined = jnp.concatenate([rows_refs[2 * pair][...], rows_refs[2 * pair + 1][...]], axis=0)
        wanted = jnp.concatenate(
            [targets_ref[2 * pair : 2 * pair + 1, :], targets_ref[2 * pair + 1 : 2 * pair + 2, :]],
            axis=1,
        )
        owner = jnp.concatenate(
            [owners_ref[2 * pair : 2 * pair + 1, :], owners_ref[2 * pair + 1 : 2 * pair + 2, :]],
            axis=1,
        )
        logits = dot32(head_ref[...], joined, NEXT_TO)
        target = jnp.sum(jnp.where(ids == wanted, logits, 0.0), axis=0, keepdims=True)
        top = jnp.max(logits, axis=0, keepdims=True)
        total = jnp.sum(jnp.exp(logits - top), axis=0, keepdims=True)
        stats = jnp.where(slot % 8 == 0, top, jnp.where(slot % 8 == 1, total, target))
        rest = jnp.where((slot // 8 == owner) & (slot % 8 < 3), stats, 0.0)
        for _ in range(3):
            part = rest.astype(jnp.bfloat16)
            packed = packed + dot32(part, place)
            rest = rest - part.astype(jnp.float32)
    out_ref[...] = packed


def head_stats(targets, owners, rows, head_weight, devices, others=()):
    whole = pl.BlockSpec(memory_space=pltpu.VMEM)
    return pl.pallas_call(
        head_kernel,
        out_shape=jax.ShapeDtypeStruct((devices * 8, 128), jnp.float32),
        in_specs=[whole] * (3 + len(rows) + len(others)),
        out_specs=whole,
        compiler_params=pltpu.CompilerParams(vmem_limit_bytes=32 << 20),
        cost_estimate=pl.CostEstimate(
            flops=10 * 2 * len(rows) * rows[0].size * head_weight.shape[0],
            bytes_accessed=2 * len(rows) * rows[0].size + 2 * head_weight.size,
            transcendentals=len(rows) * rows[0].shape[0] * head_weight.shape[0],
        ),
        name="head_stats",
    )(targets, owners, *rows, head_weight, *others)


def mdl_pairs(step):
    pairs = []
    for device in range(SIDE * SIDE * CORES):
        flip = (3, 1)[(device + step) % 2]
        pairs += [(device * SIDE + z, device * SIDE + (z ^ flip)) for z in range(SIDE)]
    return pairs


def shards(
    hidden_in,
    mixer_gain,
    w_query,
    w_kv,
    w_attn_out,
    prompt_kv,
    prompt_lengths,
    member,
    accepted,
    w_z,
    w_x,
    w_bc,
    w_dt,
    conv_x,
    conv_bc,
    ssm_rate,
    dt_bias,
    skip_d,
    prompt_state,
    prompt_conv_x,
    prompt_conv_bc,
    w_mamba_out,
    mlp_gain,
    w_gate,
    w_up,
    w_down,
    final_gain,
    head_weight,
    draft_ids,
):
    row_reqs, draft_len, width = hidden_in.shape
    mdl_count = lax.axis_size("mdl")
    req_count = lax.axis_size("req")
    mdl_rank = lax.axis_index("mdl")
    req_rank = lax.axis_index("req")
    row_tokens = row_reqs * draft_len
    own_reqs = row_reqs // mdl_count
    own_tokens = own_reqs * draft_len
    flat_rows = hidden_in.reshape(row_tokens, width)
    local_inner = w_x.shape[1]
    edge_len = CONV - 1
    far, near, kept, own_bc = mixer(
        flat_rows, mixer_gain, w_query, w_kv, w_attn_out, prompt_kv, prompt_lengths, member, accepted, w_z, w_x, w_bc,
        w_dt, conv_x, conv_bc, ssm_rate, dt_bias, skip_d, prompt_state, prompt_conv_x, prompt_conv_bc, w_mamba_out,
    )
    came = lax.ppermute(far, ("req", "mdl"), mdl_pairs(0))
    last = lax.ppermute(added(near[own_tokens:], came[own_tokens:]), ("req", "mdl"), mdl_pairs(1))
    mixed = (
        near[:own_tokens].astype(jnp.float32)
        + came[:own_tokens].astype(jnp.float32)
        + last.astype(jnp.float32)
    )
    own_rows = lax.dynamic_slice_in_dim(flat_rows, mdl_rank * own_tokens, own_tokens, 0)
    after_mixer = (own_rows.astype(jnp.float32) + mixed).astype(jnp.bfloat16)
    kept, token = lax.optimization_barrier((kept, after_mixer[:8, :128]))
    kept_out = lax.all_to_all(
        kept.reshape(mdl_count, own_reqs, local_inner + 16, STATE),
        "mdl",
        split_axis=0,
        concat_axis=0,
        tiled=True,
    )
    prepared = rms_scale(after_mixer, mlp_gain).astype(jnp.bfloat16)
    w_both = jnp.concatenate([w_gate, w_up], axis=1)
    held, late = gather_rows(prepared)
    early = (held, [swap_core(part) for part in held])
    late = (late, [swap_core(part) for part in late])

    core = req_rank % CORES
    chip_x = req_rank // CORES % SIDE
    chip_y = req_rank // (CORES * SIDE)
    table = jnp.where(core == 0, jnp.asarray(block_table()[0]), jnp.asarray(block_table()[1]))
    owner = ((chip_y ^ table[:, 0]) * SIDE + (chip_x ^ table[:, 1])) * CORES + (core ^ table[:, 2])
    request = owner * row_reqs + mdl_rank * own_reqs + table[:, 3]
    next_ids = jnp.concatenate([draft_ids[:, 1:], draft_ids[:, :1]], axis=1)
    picked = (request[:, None] == jnp.arange(draft_ids.shape[0])[None, :]).astype(jnp.float32)
    targets = jnp.dot(picked, next_ids.astype(jnp.float32), precision=HIGHEST).astype(jnp.int32)
    targets = targets.reshape(8, 8 * draft_len)
    owners = jnp.broadcast_to(owner[:, None], (64, draft_len)).reshape(8, 8 * draft_len)

    early_parts = [feed(*rows, w_both, w_down, token) for rows in early]
    later_token, kept_out = lax.optimization_barrier((token, kept_out))
    late_parts = [
        feed(*late[0], w_both, w_down, token),
        feed(*late[1], w_both, w_down, later_token),
    ]
    summed = scatter_rows(early_parts, late_parts)
    kept_state = (
        kept_out[:, :, :local_inner, :]
        .transpose(1, 0, 2, 3)
        .astype(jnp.float32)
        .reshape(own_reqs, mdl_count * local_inner // SSM_DIM, SSM_DIM, STATE)
    )
    edges = kept_out[:, :, local_inner:, :]
    edges = jnp.concatenate(
        [edges[:, :, :edge_len, :], edges[:, :, 8 : 8 + edge_len, : local_inner - STATE]], axis=3
    )
    kept_conv = jnp.concatenate(
        [
            edges.transpose(1, 2, 0, 3).reshape(own_reqs, edge_len, mdl_count * local_inner),
            own_bc.reshape(own_reqs, 8, 2 * STATE)[:, :edge_len, :],
        ],
        axis=2,
    )
    final_gain, kept_state, kept_conv, targets, owners = lax.optimization_barrier(
        (final_gain, kept_state, kept_conv, targets, owners)
    )
    after_feed = (after_mixer.astype(jnp.float32) + summed).astype(jnp.bfloat16)
    final_rows = rms_scale(after_feed, final_gain).astype(jnp.bfloat16)
    held, late = gather_rows(final_rows)
    early = held + [swap_core(part) for part in held]
    first_stats = head_stats(targets[:4], owners[:4], early, head_weight, req_count)
    late, first_stats = lax.optimization_barrier((late, first_stats))
    sibling = [swap_core(part) for part in late]
    stats = [first_stats, head_stats(targets[4:6], owners[4:6], late, head_weight, req_count)]
    stats = head_stats(targets[6:], owners[6:], sibling, head_weight, req_count, stats)
    shared = lax.all_to_all(stats, "req", split_axis=0, concat_axis=0, tiled=True)
    shared = shared.reshape(req_count, 8, 128)[:, :, :own_tokens]
    tops, totals, hits = shared[:, 0], shared[:, 1], shared[:, 2]
    top = jnp.max(tops, axis=0)
    total = jnp.sum(totals * jnp.exp(tops - top[None, :]), axis=0)
    log_total = top + jnp.log(total)
    position = jnp.arange(own_tokens) % draft_len
    verify_scores = jnp.where(
        position < draft_len - 1, jnp.sum(hits, axis=0) - log_total, top - log_total
    ).reshape(own_reqs, draft_len)
    return (
        after_feed.reshape(own_reqs, draft_len, width),
        verify_scores,
        kept_state,
        kept_conv,
    )


def solution(mesh):
    in_specs = (
        P("req", None, None),
        P(),
        P(None, "mdl"),
        P(),
        P("mdl", None),
        P("req", None, None, None),
        P("req"),
        P("req"),
        P("req"),
        P(None, "mdl"),
        P(None, "mdl"),
        P(),
        P(None, "mdl"),
        P(None, "mdl"),
        P(),
        P("mdl"),
        P("mdl"),
        P("mdl"),
        P("req", "mdl", None, None),
        P("req", None, "mdl"),
        P("req", None, None),
        P("mdl", None),
        P(),
        P(None, "req"),
        P(None, "req"),
        P("req", None),
        P(),
        P("req", None),
        P(),
    )
    out_specs = (
        P(("req", "mdl"), None, None),
        P(("req", "mdl"), None),
        P(("req", "mdl"), None, None, None),
        P(("req", "mdl"), None, None),
    )
    return jax.shard_map(shards, mesh=mesh, in_specs=in_specs, out_specs=out_specs, check_vma=False)
```

```python
import functools

import jax
import jax.numpy as jnp
import numpy as np
from jax import lax
from jax.experimental import pallas as pl
from jax.experimental.pallas import tpu as pltpu
from jax.sharding import PartitionSpec as P

Q_HEADS = 8
KV_HEADS = 2
HEAD_DIM = 128
SSM_DIM = 64
STATE = 256
CONV = 4
PROMPTS = 2
P_MAX = 1024
DRAFT = 16
SIDE = 4
CORES = 2

eps_norm = 1e-05
far_below = -1e30

DIRECT = (1, 3, 2)
EDGES = ((1, 3), (3, 1))


def device_at(y, x, core):
    return (y * SIDE + x) * CORES + core


def flip_pairs(ring, flip):
    pairs = []
    for y in range(SIDE):
        for x in range(SIDE):
            for core in range(CORES):
                on_x = ring == core
                target = device_at(y if on_x else y ^ flip, x ^ flip if on_x else x, core)
                pairs.append((device_at(y, x, core), target))
    return pairs


CORE_PAIRS = [(device, device ^ 1) for device in range(SIDE * SIDE * CORES)]


def hop(part, ring, flip):
    return lax.ppermute(part, "req", flip_pairs(ring, flip))


def swap_core(part):
    return lax.ppermute(part, "req", CORE_PAIRS)


def gather_rows(rows):
    came = [hop(rows, 0, flip) for flip in DIRECT]
    held = [jnp.concatenate([rows, came[0]], axis=0), jnp.concatenate(came[1:], axis=0)]
    came = [hop(held[s], 1, EDGES[s][0]) for s in range(2)]
    held = [jnp.concatenate([held[s], came[s]], axis=0) for s in range(2)]
    late = [hop(held[s], 1, EDGES[s][1]) for s in range(2)]
    return held, late


def added(left, right):
    return (left.astype(jnp.float32) + right.astype(jnp.float32)).astype(jnp.bfloat16)


def scatter_rows(early, late):
    came = [swap_core(part) for part in late[1]]
    late = [hop(added(late[0][s], came[s]), 1, EDGES[s][1]) for s in range(2)]
    came = [swap_core(part) for part in early[1]]
    held = [added(early[0][s], came[s]) for s in range(2)]
    held = [added(held[s], late[s]) for s in range(2)]
    tip = held[1][:8, :128]
    half = held[0].shape[0] // 2
    came = [hop(held[s][half:], 1, EDGES[s][0]) for s in range(2)]
    held = [added(held[s][:half], came[s]) for s in range(2)]
    half = half // 2
    blocks = (held[0][half:], held[1][:half], held[1][half:])
    came = [hop(block, 0, flip) for block, flip in zip(blocks, DIRECT, strict=True)]
    total = held[0][:half].astype(jnp.float32)
    return sum((part.astype(jnp.float32) for part in came), total), tip


def block_table():
    table = np.zeros((CORES, 2, 2, 2, 2, 2, 2, 4), np.int32)
    for core, late, half, stream, second, block, request in np.ndindex(table.shape[:-1]):
        first = ((0, 1), (3, 2))[stream][block]
        other = (EDGES[stream][1] if late else 0) ^ (EDGES[stream][0] if second else 0)
        y, x = (other, first) if core == half else (first, other)
        table[core, late, half, stream, second, block, request] = (y, x, half, request)
    return table.reshape(CORES, 64, 4)


def rms_scale(values, gain):
    widened = values.astype(jnp.float32)
    spread = jnp.mean(widened * widened, axis=-1, keepdims=True)
    return widened * lax.rsqrt(spread + eps_norm) * gain.astype(jnp.float32)


HIGHEST = lax.Precision.HIGHEST
NEXT_TO = (((1,), (1,)), ((), ()))


def dot32(left, right, dims=None):
    dims = dims or (((1,), (0,)), ((), ()))
    return lax.dot_general(left, right, dims, preferred_element_type=jnp.float32)


def exact_dot(left, right):
    return jnp.dot(left, right, precision=HIGHEST, preferred_element_type=jnp.float32)


def lane_spread(rows, lanes):
    return (
        lax.broadcasted_iota(jnp.int32, (rows, lanes), 0)
        == lax.broadcasted_iota(jnp.int32, (rows, lanes), 1) // SSM_DIM
    ).astype(jnp.float32)


def keeper_kernel(*refs):
    sources, (kept_ref, kept_bc_ref), held, sems = refs[:10], refs[10:12], refs[12:22], refs[22]
    copies = [
        pltpu.make_async_copy(source, target, sems.at[index])
        for index, (source, target) in enumerate(zip(sources, held, strict=True))
    ]
    for copy in copies:
        copy.start()
    for copy in copies:
        copy.wait()
    member_ref, accepted_ref, decay_ref, scaled_ref, b_ref, in_x_ref, in_bc_ref = held[:7]
    past_x_ref, past_bc_ref, state = held[7:]
    tokens, inner = scaled_ref.shape
    requests = tokens // DRAFT
    rank = lax.axis_index("mdl")

    row = lax.broadcasted_iota(jnp.int32, (tokens, 1), 0)
    time, request = row % DRAFT, row // DRAFT
    last = jnp.zeros((tokens, 1), jnp.int32)
    for r in range(requests):
        last = jnp.where(request == r, accepted_ref[r] - 1, last)
    spread_lanes = lane_spread(tokens, inner)
    log_decay, scaled_x, b_part = decay_ref[...], scaled_ref[...], b_ref[...]
    in_x, in_bc = in_x_ref[...], in_bc_ref[...]
    decay_x = exact_dot(log_decay, spread_lanes)
    other = lax.broadcasted_iota(jnp.int32, (tokens, tokens), 1)
    pick = (other == request * DRAFT + last).astype(jnp.float32)
    final_log = exact_dot(pick, log_decay)
    final_x = exact_dot(final_log, spread_lanes)
    carry_x = jnp.exp(jnp.where(time <= last, final_x - decay_x, far_below))
    carried_x = (scaled_x * carry_x).T.astype(jnp.bfloat16)
    shrink = jnp.exp(final_x).T
    for r in range(requests):
        b_here = jnp.where(request == r, b_part, jnp.zeros_like(b_part))
        kept = shrink[:, r * DRAFT : r * DRAFT + 1] * state[member_ref[r]] + dot32(
            carried_x, b_here
        )
        kept_ref[r, :inner, :] = kept.astype(jnp.bfloat16)

    def kept_rows(first_request, count, slots, series, past_of):
        at = lax.broadcasted_iota(jnp.int32, (count * slots, 1), 0)
        here, edge = at // slots, at % slots
        start = jnp.zeros((count * slots, 1), jnp.int32)
        owner = jnp.zeros((count * slots, 1), jnp.int32)
        for r in range(count):
            start = jnp.where(here == r, accepted_ref[first_request + r], start)
            owner = jnp.where(here == r, member_ref[first_request + r], owner)
        index = start + edge
        token = (here + first_request) * DRAFT + index - (CONV - 1)
        chosen = (lax.broadcasted_iota(jnp.int32, (count * slots, tokens), 1) == token) & (
            index >= CONV - 1
        )
        rows = dot32(chosen.astype(jnp.bfloat16), series)
        for p in range(PROMPTS):
            for j in range(CONV - 1):
                rows = jnp.where((owner == p) & (index == j), past_of(j, p), rows)
        return rows.astype(jnp.bfloat16)

    for lanes in range(2):
        cut = slice(lanes * STATE, min((lanes + 1) * STATE, inner))
        rows = kept_rows(
            0, requests, 8, in_x[:, cut], lambda j, p: past_x_ref[j, p : p + 1, cut].astype(jnp.float32)
        )
        for r in range(requests):
            kept_ref[r, inner + 8 * lanes : inner + 8 * (lanes + 1), : rows.shape[1]] = rows[
                r * 8 : (r + 1) * 8
            ]
    kept_ref[:, inner + 8 :, inner - STATE :] = jnp.zeros(
        (requests, 8, 2 * STATE - inner), jnp.bfloat16
    )
    kept_bc_ref[...] = kept_rows(
        rank * (requests // SIDE),
        requests // SIDE,
        8,
        in_bc,
        lambda j, p: past_bc_ref[j, p : p + 1, :].astype(jnp.float32),
    )


def keeper(member, accepted, log_decay, scaled_x, b_part, in_x, in_bc, past_x, past_bc, state):
    tokens, inner = scaled_x.shape
    requests = tokens // DRAFT
    operands = (member, accepted, log_decay, scaled_x, b_part, in_x, in_bc, past_x, past_bc, state)
    whole = pl.BlockSpec(memory_space=pltpu.VMEM)
    return pl.pallas_call(
        keeper_kernel,
        out_shape=[
            jax.ShapeDtypeStruct((requests, inner + 16, STATE), jnp.bfloat16),
            jax.ShapeDtypeStruct((requests // SIDE * 8, 2 * STATE), jnp.bfloat16),
        ],
        in_specs=[pl.BlockSpec(memory_space=pltpu.HBM)] * len(operands),
        out_specs=[whole] * 2,
        scratch_shapes=[
            *(pltpu.SMEM(a.shape, a.dtype) for a in operands[:2]),
            *(pltpu.VMEM(a.shape, a.dtype) for a in operands[2:]),
            pltpu.SemaphoreType.DMA((len(operands),)),
        ],
        compiler_params=pltpu.CompilerParams(vmem_limit_bytes=32 << 20),
        cost_estimate=pl.CostEstimate(
            flops=2_000_000_000, bytes_accessed=5_000_000, transcendentals=200_000
        ),
        name="keeper",
    )(*operands)


def unpack_kernel(kept_hbm, bc_ref, _stats, _tip, state_ref, conv_ref, kept_ref, sem):
    copy = pltpu.make_async_copy(kept_hbm, kept_ref, sem)
    copy.start()
    copy.wait()
    inner = kept_ref.shape[2] - 16
    for r in range(state_ref.shape[0]):
        for z in range(kept_ref.shape[0]):
            state_ref[r, z * inner : (z + 1) * inner, :] = kept_ref[z, r, :inner, :].astype(
                jnp.float32
            )
    for j in range(CONV - 1):
        rows = []
        for r in range(state_ref.shape[0]):
            pieces = []
            for z in range(kept_ref.shape[0]):
                tail = kept_ref[z, r, inner:, :].astype(jnp.float32)
                pieces += [tail[j : j + 1, :], tail[8 + j : 9 + j, : inner - STATE]]
            pieces.append(bc_ref[...].astype(jnp.float32)[r * 8 + j : r * 8 + j + 1, :])
            rows.append(jnp.concatenate(pieces, axis=1))
        conv_ref[j] = jnp.concatenate(rows, axis=0).astype(jnp.bfloat16)


def unpack(kept_out, own_bc, *tokens):
    sources, requests, rows, _ = kept_out.shape
    inner = rows - 16
    whole = pl.BlockSpec(memory_space=pltpu.VMEM)
    state, conv = pl.pallas_call(
        unpack_kernel,
        out_shape=[
            jax.ShapeDtypeStruct((requests, sources * inner, STATE), jnp.float32),
            jax.ShapeDtypeStruct((CONV - 1, requests, sources * inner + 2 * STATE), jnp.bfloat16),
        ],
        in_specs=[pl.BlockSpec(memory_space=pltpu.HBM), whole]
        + [pl.BlockSpec(memory_space=pl.ANY)] * len(tokens),
        out_specs=[whole] * 2,
        scratch_shapes=[pltpu.VMEM(kept_out.shape, kept_out.dtype), pltpu.SemaphoreType.DMA],
        compiler_params=pltpu.CompilerParams(vmem_limit_bytes=48 << 20),
        cost_estimate=pl.CostEstimate(flops=1_000_000, bytes_accessed=20_000_000, transcendentals=0),
        name="unpack",
    )(kept_out, own_bc, *tokens)
    return state, conv.transpose(1, 0, 2)


def mixer_kernel(*refs):
    sources, refs = refs[:22], refs[22:]
    far_ref, near_ref, decay_ref, scaled_ref, b_ref, in_x_ref, in_bc_ref = refs[:7]
    held, (mixed_scr, lanes_scr, sems) = refs[7:-3], refs[-3:]
    member_ref, accepted_ref, lengths_ref, rate_ref, bias_ref, skip_ref = held[:6]
    hidden_ref, gain_ref, w_dt_ref, conv_x_ref, conv_bc_ref, past_x_ref, past_bc_ref = held[6:13]
    w_query, w_kv, prompt, w_x, w_bc, w_z, state, w_out = held[13:]
    tokens = hidden_ref.shape[0]
    requests = tokens // DRAFT
    inner = w_x.shape[1]
    heads = inner // SSM_DIM
    query_width = w_query.shape[1]
    rank = lax.axis_index("mdl")
    core = lax.axis_index("req") % CORES
    group = rank * (query_width // HEAD_DIM) // (Q_HEADS // KV_HEADS)
    query_hbm, kv_hbm, prompt_hbm, x_hbm, bc_hbm, z_hbm, state_hbm, attn_hbm, mamba_hbm = sources[13:]
    moves = [(source, target) for source, target in zip(sources[:13], held[:13], strict=True)]
    moves += [
        (query_hbm, w_query),
        (kv_hbm.at[group], w_kv),
        (prompt_hbm.at[0, group], prompt.at[0]),
        (prompt_hbm.at[1, group], prompt.at[1]),
        (x_hbm, w_x),
        (bc_hbm, w_bc),
        (z_hbm, w_z),
        (state_hbm, state),
        (attn_hbm, w_out.at[pl.ds(0, query_width), :]),
        (mamba_hbm, w_out.at[pl.ds(query_width, inner), :]),
    ]
    started = [
        pltpu.make_async_copy(source, target, sems.at[index])
        for index, (source, target) in enumerate(moves)
    ]
    for copy in started:
        copy.start()
    for copy in started[:13]:
        copy.wait()
    copies = started[13:]

    def head_row(ref):
        lane = lax.broadcasted_iota(jnp.int32, (1, heads), 1)
        values = jnp.zeros((1, heads), jnp.float32)
        for h in range(heads):
            values = jnp.where(lane == h, ref[h], values)
        return values

    row = lax.broadcasted_iota(jnp.int32, (tokens, 1), 0)
    time, request = row % DRAFT, row // DRAFT
    own_prompt = jnp.zeros((tokens, 1), jnp.int32)
    last = jnp.zeros((tokens, 1), jnp.int32)
    for r in range(requests):
        own_prompt = jnp.where(request == r, member_ref[r], own_prompt)
        last = jnp.where(request == r, accepted_ref[r] - 1, last)
    first_prompt = own_prompt == 0

    gain = jnp.concatenate(
        [gain_ref[j : j + 1, :].astype(jnp.float32) for j in range(gain_ref.shape[0])], axis=1
    )
    widened = hidden_ref[...].astype(jnp.float32)
    spread = jnp.mean(widened * widened, axis=-1, keepdims=True)
    normed = (
        widened * lax.rsqrt(spread + eps_norm) * gain
    ).astype(jnp.bfloat16)

    copies[0].wait()
    queries = dot32(normed, w_query[...]).astype(jnp.bfloat16)
    copies[1].wait()
    drafts = dot32(normed, w_kv[...]).astype(jnp.bfloat16)
    local_heads = query_width // HEAD_DIM
    query_rows = jnp.concatenate(
        [queries[:, h * HEAD_DIM : (h + 1) * HEAD_DIM] for h in range(local_heads)], axis=0
    )
    scale = HEAD_DIM**-0.5
    row_first = jnp.concatenate([own_prompt] * local_heads, axis=0) == 0
    draft_scores = dot32(query_rows, drafts[:, :HEAD_DIM], NEXT_TO) * scale
    same = (row // DRAFT == lax.broadcasted_iota(jnp.int32, (tokens, tokens), 1) // DRAFT) & (
        lax.broadcasted_iota(jnp.int32, (tokens, tokens), 1) <= row
    )
    draft_mask = jnp.concatenate([same] * local_heads, axis=0)
    draft_scores = jnp.where(draft_mask, draft_scores, far_below)
    copies[2].wait()
    copies[3].wait()
    scores = jnp.where(
        row_first,
        dot32(query_rows, prompt[0, :, :HEAD_DIM], NEXT_TO),
        dot32(query_rows, prompt[1, :, :HEAD_DIM], NEXT_TO),
    )
    length = jnp.where(row_first, lengths_ref[0], lengths_ref[1])
    position = lax.broadcasted_iota(jnp.int32, scores.shape, 1)
    scores = jnp.where(position < length, scores * scale, far_below)
    top = jnp.maximum(
        jnp.max(scores, axis=1, keepdims=True), jnp.max(draft_scores, axis=1, keepdims=True)
    )
    weights = jnp.exp(scores - top)
    draft_weights = jnp.exp(draft_scores - top)
    total = jnp.sum(weights, axis=1, keepdims=True) + jnp.sum(draft_weights, axis=1, keepdims=True)
    weighted = (
        dot32(jnp.where(row_first, weights, 0.0).astype(jnp.bfloat16), prompt[0, :, HEAD_DIM:])
        + dot32(jnp.where(row_first, 0.0, weights).astype(jnp.bfloat16), prompt[1, :, HEAD_DIM:])
        + dot32(draft_weights.astype(jnp.bfloat16), drafts[:, HEAD_DIM:])
    )
    attended = (weighted / total).astype(jnp.bfloat16)
    for h in range(local_heads):
        mixed_scr[:, h * HEAD_DIM : (h + 1) * HEAD_DIM] = attended[h * tokens : (h + 1) * tokens]

    def convolve_rows(series, past_ref, taps_ref):
        past = [
            jnp.where(
                first_prompt,
                past_ref[j, 0:1, :].astype(jnp.float32),
                past_ref[j, 1:2, :].astype(jnp.float32),
            )
            for j in range(CONV - 1)
        ]
        taps = taps_ref[...].astype(jnp.float32)
        summed = series * taps[CONV - 1 : CONV, :]
        for shift in range(1, CONV):
            window = pltpu.roll(series, shift, 0)
            for t in range(shift):
                window = jnp.where(time == t, past[CONV - 1 - shift + t], window)
            summed = summed + window * taps[CONV - 1 - shift : CONV - shift, :]
        return summed * jax.nn.sigmoid(summed)

    copies[4].wait()
    in_x = dot32(normed, w_x[...]).astype(jnp.bfloat16)
    heads_x = convolve_rows(in_x.astype(jnp.float32), past_x_ref, conv_x_ref)
    copies[5].wait()
    in_bc = dot32(normed, w_bc[...]).astype(jnp.bfloat16)
    conv_bcs = convolve_rows(in_bc.astype(jnp.float32), past_bc_ref, conv_bc_ref)
    b_part = conv_bcs[:, :STATE].astype(jnp.bfloat16)
    c_part = conv_bcs[:, STATE:].astype(jnp.bfloat16)

    def widen(values):
        lanes_scr[...] = jnp.zeros(lanes_scr.shape, jnp.float32)
        lanes_scr[:, :heads] = values
        return lanes_scr[...]

    spread_lanes = lane_spread(tokens, inner)
    dt_in = dot32(normed, w_dt_ref[...], NEXT_TO).astype(jnp.bfloat16).astype(jnp.float32) + head_row(bias_ref)
    step = jnp.maximum(dt_in, 0.0) + jnp.log1p(jnp.exp(-jnp.abs(dt_in)))
    log_decay = exact_dot(same.astype(jnp.float32), widen(-step * head_row(rate_ref)))
    step_x = exact_dot(widen(step), spread_lanes)
    skip_x = exact_dot(widen(jnp.broadcast_to(head_row(skip_ref), (tokens, heads))), spread_lanes)
    decay_x = exact_dot(log_decay, spread_lanes)
    turned = log_decay.T
    intersection = dot32(c_part, b_part, NEXT_TO)
    scaled_x = heads_x * step_x
    low = lax.broadcasted_iota(jnp.int32, (tokens, 2 * SSM_DIM), 1) < SSM_DIM
    groups = []
    for pair in range(heads // 2):
        mixing = []
        for h in (2 * pair, 2 * pair + 1):
            gaps = log_decay[:, h : h + 1] - turned[h : h + 1, :]
            mixing.append(
                (jnp.exp(jnp.where(same, gaps, far_below)) * intersection).astype(jnp.bfloat16)
            )
        lanes = scaled_x[:, pair * 2 * SSM_DIM : (pair + 1) * 2 * SSM_DIM]
        both = jnp.concatenate([jnp.where(low, lanes, 0.0), jnp.where(low, 0.0, lanes)], axis=0)
        groups.append(dot32(jnp.concatenate(mixing, axis=1), both.astype(jnp.bfloat16)))
    copies[7].wait()
    carried = jnp.where(
        first_prompt,
        dot32(c_part, state[0].astype(jnp.bfloat16), NEXT_TO),
        dot32(c_part, state[1].astype(jnp.bfloat16), NEXT_TO),
    )
    ssm_out = jnp.concatenate(groups, axis=1) + carried * jnp.exp(decay_x) + skip_x * heads_x
    copies[6].wait()
    gate_z = dot32(normed, w_z[...]).astype(jnp.bfloat16).astype(jnp.float32)
    mixed_scr[:, query_width:] = (ssm_out * (gate_z * jax.nn.sigmoid(gate_z))).astype(jnp.bfloat16)

    own_rows = tokens // SIDE
    copies[8].wait()
    copies[9].wait()
    first_flip = jnp.where(core == 0, 3, 1)
    for out_ref, flips in ((far_ref, (first_flip, 2)), (near_ref, (0, first_flip ^ 2))):
        rows = jnp.concatenate(
            [
                mixed_scr[pl.ds(pl.multiple_of((rank ^ flip) * own_rows, own_rows), own_rows), :]
                for flip in flips
            ],
            axis=0,
        )
        out_ref[...] = dot32(rows, w_out[...]).astype(jnp.bfloat16)

    decay_ref[...] = log_decay
    scaled_ref[...] = scaled_x
    b_ref[...] = b_part
    in_x_ref[...] = in_x
    in_bc_ref[...] = in_bc


def mixer(
    hidden, mixer_gain, w_query, w_kv, w_attn_out, prompt_kv, prompt_lengths, member, accepted, w_z, w_x, w_bc,
    w_dt, conv_x, conv_bc, ssm_rate, dt_bias, skip_d, prompt_state, prompt_conv_x, prompt_conv_bc, w_mamba_out,
):
    tokens, width = hidden.shape
    inner = w_x.shape[1]
    query_width = w_query.shape[1]
    bf16 = jnp.bfloat16
    state = prompt_state.reshape(PROMPTS, inner, STATE)
    small = [
        hidden, mixer_gain.reshape(-1, 128), w_dt.T, conv_x, conv_bc,
        prompt_conv_x.transpose(1, 0, 2), prompt_conv_bc.transpose(1, 0, 2),
    ]
    scalars = [member, accepted, prompt_lengths, ssm_rate, dt_bias, skip_d]
    whole = pl.BlockSpec(memory_space=pltpu.VMEM)
    far, near, *series = pl.pallas_call(
        mixer_kernel,
        out_shape=[
            jax.ShapeDtypeStruct((tokens // 2, width), bf16),
            jax.ShapeDtypeStruct((tokens // 2, width), bf16),
            jax.ShapeDtypeStruct((tokens, 128), jnp.float32),
            jax.ShapeDtypeStruct((tokens, inner), jnp.float32),
            jax.ShapeDtypeStruct((tokens, STATE), bf16),
            jax.ShapeDtypeStruct((tokens, inner), bf16),
            jax.ShapeDtypeStruct((tokens, 2 * STATE), bf16),
        ],
        in_specs=[pl.BlockSpec(memory_space=pltpu.HBM)] * 22,
        out_specs=[whole] * 7,
        scratch_shapes=[
            *(pltpu.SMEM(a.shape, a.dtype) for a in scalars),
            *(pltpu.VMEM(a.shape, a.dtype) for a in small),
            pltpu.VMEM(w_query.shape, bf16),
            pltpu.VMEM(w_kv.shape[1:], bf16),
            pltpu.VMEM((PROMPTS, *prompt_kv.shape[2:]), bf16),
            pltpu.VMEM(w_x.shape, bf16),
            pltpu.VMEM(w_bc.shape, bf16),
            pltpu.VMEM(w_z.shape, bf16),
            pltpu.VMEM(state.shape, jnp.float32),
            pltpu.VMEM((query_width + inner, width), bf16),
            pltpu.VMEM((tokens, query_width + inner), bf16),
            pltpu.VMEM((tokens, 128), jnp.float32),
            pltpu.SemaphoreType.DMA((23,)),
        ],
        compiler_params=pltpu.CompilerParams(vmem_limit_bytes=59 << 20),
        cost_estimate=pl.CostEstimate(
            flops=3_000_000_000, bytes_accessed=20_000_000, transcendentals=1_000_000
        ),
        name="mixer",
    )(
        *scalars, *small, w_query, w_kv, prompt_kv, w_x, w_bc, w_z, state, w_attn_out, w_mamba_out
    )
    return far, near, *keeper(member, accepted, *series, *small[-2:], state)


def feed_kernel(first_ref, second_ref, both_ref, down_ref, first_out, second_out):
    hidden = down_ref.shape[0]
    rows = first_ref.shape[0]
    joined = jnp.concatenate([first_ref[...], second_ref[...]], axis=0)
    pair = dot32(joined, both_ref[...])
    gate, up = pair[:, :hidden], pair[:, hidden:]
    active = (gate * jax.nn.sigmoid(gate) * up).astype(jnp.bfloat16)
    parts = dot32(active, down_ref[...]).astype(jnp.bfloat16)
    first_out[...] = parts[:rows]
    second_out[...] = parts[rows:]


def feed(first, second, w_both, w_down):
    rows, width = first.shape
    whole = pl.BlockSpec(memory_space=pltpu.VMEM)
    return pl.pallas_call(
        feed_kernel,
        out_shape=[jax.ShapeDtypeStruct((rows, width), jnp.bfloat16)] * 2,
        in_specs=[whole] * 4,
        out_specs=[whole] * 2,
        compiler_params=pltpu.CompilerParams(vmem_limit_bytes=16 << 20),
        cost_estimate=pl.CostEstimate(
            flops=20 * 2 * rows * width * 2 * 3 * w_down.shape[0],
            bytes_accessed=4 * rows * width * 2 + 3 * w_down.size * 2,
            transcendentals=2 * rows * w_down.shape[0],
        ),
        name="feed",
    )(first, second, w_both, w_down)


def head_kernel(targets_ref, owners_ref, *refs):
    count = targets_ref.shape[0]
    rows_refs, head_ref, others, out_ref = refs[:count], refs[count], refs[count + 1 : -1], refs[-1]
    vocab = head_ref.shape[0]
    lanes = 2 * rows_refs[0].shape[0]
    slots = out_ref.shape[0]
    base = lax.axis_index("req") * vocab
    lane = lax.broadcasted_iota(jnp.int32, (lanes, 128), 0)
    column = lax.broadcasted_iota(jnp.int32, (lanes, 128), 1)
    place = (column == lane % (2 * DRAFT)).astype(jnp.bfloat16)
    ids = lax.broadcasted_iota(jnp.int32, (vocab, lanes), 0) + base
    slot = lax.broadcasted_iota(jnp.int32, (slots, lanes), 0)
    packed = jnp.zeros(out_ref.shape, jnp.float32)
    for other in others:
        packed = packed + other[...]
    for pair in range(count // 2):
        joined = jnp.concatenate([rows_refs[2 * pair][...], rows_refs[2 * pair + 1][...]], axis=0)
        wanted = jnp.concatenate(
            [targets_ref[2 * pair : 2 * pair + 1, :], targets_ref[2 * pair + 1 : 2 * pair + 2, :]],
            axis=1,
        )
        owner = jnp.concatenate(
            [owners_ref[2 * pair : 2 * pair + 1, :], owners_ref[2 * pair + 1 : 2 * pair + 2, :]],
            axis=1,
        )
        logits = dot32(head_ref[...], joined, NEXT_TO)
        target = jnp.sum(jnp.where(ids == wanted, logits, 0.0), axis=0, keepdims=True)
        top = jnp.max(logits, axis=0, keepdims=True)
        total = jnp.sum(jnp.exp(logits - top), axis=0, keepdims=True)
        stats = jnp.where(slot % 8 == 0, top, jnp.where(slot % 8 == 1, total, target))
        rest = jnp.where((slot // 8 == owner) & (slot % 8 < 3), stats, 0.0)
        for _ in range(3):
            part = rest.astype(jnp.bfloat16)
            packed = packed + dot32(part, place)
            rest = rest - part.astype(jnp.float32)
    out_ref[...] = packed


def head_stats(targets, owners, rows, head_weight, devices, others=()):
    whole = pl.BlockSpec(memory_space=pltpu.VMEM)
    return pl.pallas_call(
        head_kernel,
        out_shape=jax.ShapeDtypeStruct((devices * 8, 128), jnp.float32),
        in_specs=[whole] * (3 + len(rows) + len(others)),
        out_specs=whole,
        compiler_params=pltpu.CompilerParams(vmem_limit_bytes=32 << 20),
        cost_estimate=pl.CostEstimate(
            flops=10 * 2 * len(rows) * rows[0].size * head_weight.shape[0],
            bytes_accessed=2 * len(rows) * rows[0].size + 2 * head_weight.size,
            transcendentals=len(rows) * rows[0].shape[0] * head_weight.shape[0],
        ),
        name="head_stats",
    )(targets, owners, *rows, head_weight, *others)


def mdl_pairs(step):
    pairs = []
    for device in range(SIDE * SIDE * CORES):
        flip = (3, 1)[(device + step) % 2]
        pairs += [(device * SIDE + z, device * SIDE + (z ^ flip)) for z in range(SIDE)]
    return pairs


def shards(
    hidden_in,
    mixer_gain,
    w_query,
    w_kv,
    w_attn_out,
    prompt_kv,
    prompt_lengths,
    member,
    accepted,
    w_z,
    w_x,
    w_bc,
    w_dt,
    conv_x,
    conv_bc,
    ssm_rate,
    dt_bias,
    skip_d,
    prompt_state,
    prompt_conv_x,
    prompt_conv_bc,
    w_mamba_out,
    mlp_gain,
    w_gate,
    w_up,
    w_down,
    final_gain,
    head_weight,
    draft_ids,
):
    row_reqs, draft_len, width = hidden_in.shape
    mdl_count = lax.axis_size("mdl")
    req_count = lax.axis_size("req")
    mdl_rank = lax.axis_index("mdl")
    req_rank = lax.axis_index("req")
    row_tokens = row_reqs * draft_len
    own_reqs = row_reqs // mdl_count
    own_tokens = own_reqs * draft_len
    flat_rows = hidden_in.reshape(row_tokens, width)
    local_inner = w_x.shape[1]
    far, near, kept, own_bc = mixer(
        flat_rows, mixer_gain, w_query, w_kv, w_attn_out, prompt_kv, prompt_lengths, member, accepted, w_z, w_x, w_bc,
        w_dt, conv_x, conv_bc, ssm_rate, dt_bias, skip_d, prompt_state, prompt_conv_x, prompt_conv_bc, w_mamba_out,
    )
    came = lax.ppermute(far, ("req", "mdl"), mdl_pairs(0))
    last = lax.ppermute(added(near[own_tokens:], came[own_tokens:]), ("req", "mdl"), mdl_pairs(1))
    mixed = (
        near[:own_tokens].astype(jnp.float32)
        + came[:own_tokens].astype(jnp.float32)
        + last.astype(jnp.float32)
    )
    own_rows = lax.dynamic_slice_in_dim(flat_rows, mdl_rank * own_tokens, own_tokens, 0)
    after_mixer = (own_rows.astype(jnp.float32) + mixed).astype(jnp.bfloat16)
    prepared = rms_scale(after_mixer, mlp_gain).astype(jnp.bfloat16)
    w_both = jnp.concatenate([w_gate, w_up], axis=1)
    held, late = gather_rows(prepared)
    early = (held, [swap_core(part) for part in held])
    late = (late, [swap_core(part) for part in late])

    core = req_rank % CORES
    chip_x = req_rank // CORES % SIDE
    chip_y = req_rank // (CORES * SIDE)
    table = jnp.where(core == 0, jnp.asarray(block_table()[0]), jnp.asarray(block_table()[1]))
    owner = ((chip_y ^ table[:, 0]) * SIDE + (chip_x ^ table[:, 1])) * CORES + (core ^ table[:, 2])
    request = owner * row_reqs + mdl_rank * own_reqs + table[:, 3]
    next_ids = jnp.concatenate([draft_ids[:, 1:], draft_ids[:, :1]], axis=1)
    picked = (request[:, None] == jnp.arange(draft_ids.shape[0])[None, :]).astype(jnp.float32)
    targets = jnp.dot(picked, next_ids.astype(jnp.float32), precision=HIGHEST).astype(jnp.int32)
    targets = targets.reshape(8, 8 * draft_len)
    owners = jnp.broadcast_to(owner[:, None], (64, draft_len)).reshape(8, 8 * draft_len)

    early_parts = [feed(*rows, w_both, w_down) for rows in early]
    late_parts = [feed(*rows, w_both, w_down) for rows in late]
    summed, tip = scatter_rows(early_parts, late_parts)
    kept, tip = lax.optimization_barrier((kept, tip))
    kept_out = lax.all_to_all(
        kept.reshape(mdl_count, own_reqs, local_inner + 16, STATE),
        "mdl",
        split_axis=0,
        concat_axis=0,
        tiled=True,
    )
    final_gain, kept_out, targets, owners = lax.optimization_barrier(
        (final_gain, kept_out, targets, owners)
    )
    after_feed = (after_mixer.astype(jnp.float32) + summed).astype(jnp.bfloat16)
    final_rows = rms_scale(after_feed, final_gain).astype(jnp.bfloat16)
    held, late = gather_rows(final_rows)
    early = held + [swap_core(part) for part in held]
    first_stats = head_stats(targets[:4], owners[:4], early, head_weight, req_count)
    late, first_stats = lax.optimization_barrier((late, first_stats))
    sibling = [swap_core(part) for part in late]
    stats = [first_stats, head_stats(targets[4:6], owners[4:6], late, head_weight, req_count)]
    stats = head_stats(targets[6:], owners[6:], sibling, head_weight, req_count, stats)
    kept_state, kept_conv = unpack(kept_out, own_bc, stats, tip)
    kept_state = kept_state.reshape(own_reqs, -1, SSM_DIM, STATE)
    shared = lax.all_to_all(stats, "req", split_axis=0, concat_axis=0, tiled=True)
    shared = shared.reshape(req_count, 8, 128)[:, :, :own_tokens]
    tops, totals, hits = shared[:, 0], shared[:, 1], shared[:, 2]
    top = jnp.max(tops, axis=0)
    total = jnp.sum(totals * jnp.exp(tops - top[None, :]), axis=0)
    log_total = top + jnp.log(total)
    position = jnp.arange(own_tokens) % draft_len
    verify_scores = jnp.where(
        position < draft_len - 1, jnp.sum(hits, axis=0) - log_total, top - log_total
    ).reshape(own_reqs, draft_len)
    return (
        after_feed.reshape(own_reqs, draft_len, width),
        verify_scores,
        kept_state,
        kept_conv,
    )


def solution(mesh):
    in_specs = (
        P("req", None, None),
        P(),
        P(None, "mdl"),
        P(),
        P("mdl", None),
        P("req", None, None, None),
        P("req"),
        P("req"),
        P("req"),
        P(None, "mdl"),
        P(None, "mdl"),
        P(),
        P(None, "mdl"),
        P(None, "mdl"),
        P(),
        P("mdl"),
        P("mdl"),
        P("mdl"),
        P("req", "mdl", None, None),
        P("req", None, "mdl"),
        P("req", None, None),
        P("mdl", None),
        P(),
        P(None, "req"),
        P(None, "req"),
        P("req", None),
        P(),
        P("req", None),
        P(),
    )
    out_specs = (
        P(("req", "mdl"), None, None),
        P(("req", "mdl"), None),
        P(("req", "mdl"), None, None, None),
        P(("req", "mdl"), None, None),
    )
    return jax.shard_map(shards, mesh=mesh, in_specs=in_specs, out_specs=out_specs, check_vma=False)
```

```python
import functools

import jax
import jax.numpy as jnp
import numpy as np
from jax import lax
from jax.experimental import pallas as pl
from jax.experimental.pallas import tpu as pltpu
from jax.sharding import PartitionSpec as P

Q_HEADS = 8
KV_HEADS = 2
HEAD_DIM = 128
SSM_DIM = 64
STATE = 256
CONV = 4
PROMPTS = 2
P_MAX = 1024
DRAFT = 16
SIDE = 4
CORES = 2

eps_norm = 1e-05
far_below = -1e30

DIRECT = (1, 3, 2)
EDGES = ((1, 3), (3, 1))


def device_at(y, x, core):
    return (y * SIDE + x) * CORES + core


def flip_pairs(ring, flip):
    pairs = []
    for y in range(SIDE):
        for x in range(SIDE):
            for core in range(CORES):
                on_x = ring == core
                target = device_at(y if on_x else y ^ flip, x ^ flip if on_x else x, core)
                pairs.append((device_at(y, x, core), target))
    return pairs


CORE_PAIRS = [(device, device ^ 1) for device in range(SIDE * SIDE * CORES)]


def hop(part, ring, flip):
    return lax.ppermute(part, "req", flip_pairs(ring, flip))


def swap_core(part):
    return lax.ppermute(part, "req", CORE_PAIRS)


def gather_rows(rows):
    came = [hop(rows, 0, flip) for flip in DIRECT]
    held = [jnp.concatenate([rows, came[0]], axis=0), jnp.concatenate(came[1:], axis=0)]
    came = [hop(held[s], 1, EDGES[s][0]) for s in range(2)]
    held = [jnp.concatenate([held[s], came[s]], axis=0) for s in range(2)]
    late = [hop(held[s], 1, EDGES[s][1]) for s in range(2)]
    return held, late


def added(left, right):
    return (left.astype(jnp.float32) + right.astype(jnp.float32)).astype(jnp.bfloat16)


def scatter_rows(early, late):
    came = [swap_core(part) for part in late[1]]
    late = [hop(added(late[0][s], came[s]), 1, EDGES[s][1]) for s in range(2)]
    came = [swap_core(part) for part in early[1]]
    held = [added(early[0][s], came[s]) for s in range(2)]
    held = [added(held[s], late[s]) for s in range(2)]
    half = held[0].shape[0] // 2
    came = [hop(held[s][half:], 1, EDGES[s][0]) for s in range(2)]
    held = [added(held[s][:half], came[s]) for s in range(2)]
    half = half // 2
    blocks = (held[0][half:], held[1][:half], held[1][half:])
    came = [hop(block, 0, flip) for block, flip in zip(blocks, DIRECT, strict=True)]
    total = held[0][:half].astype(jnp.float32)
    return sum((part.astype(jnp.float32) for part in came), total)


def block_table():
    table = np.zeros((CORES, 2, 2, 2, 2, 2, 2, 4), np.int32)
    for core, late, half, stream, second, block, request in np.ndindex(table.shape[:-1]):
        first = ((0, 1), (3, 2))[stream][block]
        other = (EDGES[stream][1] if late else 0) ^ (EDGES[stream][0] if second else 0)
        y, x = (other, first) if core == half else (first, other)
        table[core, late, half, stream, second, block, request] = (y, x, half, request)
    return table.reshape(CORES, 64, 4)


def rms_scale(values, gain):
    widened = values.astype(jnp.float32)
    spread = jnp.mean(widened * widened, axis=-1, keepdims=True)
    return widened * lax.rsqrt(spread + eps_norm) * gain.astype(jnp.float32)


HIGHEST = lax.Precision.HIGHEST
NEXT_TO = (((1,), (1,)), ((), ()))


def dot32(left, right, dims=None):
    dims = dims or (((1,), (0,)), ((), ()))
    return lax.dot_general(left, right, dims, preferred_element_type=jnp.float32)


def exact_dot(left, right):
    return jnp.dot(left, right, precision=HIGHEST, preferred_element_type=jnp.float32)


def lane_spread(rows, lanes):
    return (
        lax.broadcasted_iota(jnp.int32, (rows, lanes), 0)
        == lax.broadcasted_iota(jnp.int32, (rows, lanes), 1) // SSM_DIM
    ).astype(jnp.float32)


def keeper_kernel(*refs):
    sources, (kept_ref, kept_bc_ref), held, sems = refs[:10], refs[10:12], refs[12:22], refs[22]
    copies = [
        pltpu.make_async_copy(source, target, sems.at[index])
        for index, (source, target) in enumerate(zip(sources, held, strict=True))
    ]
    for copy in copies:
        copy.start()
    for copy in copies:
        copy.wait()
    member_ref, accepted_ref, decay_ref, scaled_ref, b_ref, in_x_ref, in_bc_ref = held[:7]
    past_x_ref, past_bc_ref, state = held[7:]
    tokens, inner = scaled_ref.shape
    requests = tokens // DRAFT
    rank = lax.axis_index("mdl")

    row = lax.broadcasted_iota(jnp.int32, (tokens, 1), 0)
    time, request = row % DRAFT, row // DRAFT
    last = jnp.zeros((tokens, 1), jnp.int32)
    for r in range(requests):
        last = jnp.where(request == r, accepted_ref[r] - 1, last)
    spread_lanes = lane_spread(tokens, inner)
    log_decay, scaled_x, b_part = decay_ref[...], scaled_ref[...], b_ref[...]
    in_x, in_bc = in_x_ref[...], in_bc_ref[...]
    decay_x = exact_dot(log_decay, spread_lanes)
    other = lax.broadcasted_iota(jnp.int32, (tokens, tokens), 1)
    pick = (other == request * DRAFT + last).astype(jnp.float32)
    final_log = exact_dot(pick, log_decay)
    final_x = exact_dot(final_log, spread_lanes)
    carry_x = jnp.exp(jnp.where(time <= last, final_x - decay_x, far_below))
    carried_x = (scaled_x * carry_x).T.astype(jnp.bfloat16)
    shrink = jnp.exp(final_x).T
    for r in range(requests):
        b_here = jnp.where(request == r, b_part, jnp.zeros_like(b_part))
        kept = shrink[:, r * DRAFT : r * DRAFT + 1] * state[member_ref[r]] + dot32(
            carried_x, b_here
        )
        kept_ref[r, :inner, :] = kept.astype(jnp.bfloat16)

    def kept_rows(first_request, count, slots, series, past_of):
        at = lax.broadcasted_iota(jnp.int32, (count * slots, 1), 0)
        here, edge = at // slots, at % slots
        start = jnp.zeros((count * slots, 1), jnp.int32)
        owner = jnp.zeros((count * slots, 1), jnp.int32)
        for r in range(count):
            start = jnp.where(here == r, accepted_ref[first_request + r], start)
            owner = jnp.where(here == r, member_ref[first_request + r], owner)
        index = start + edge
        token = (here + first_request) * DRAFT + index - (CONV - 1)
        chosen = (lax.broadcasted_iota(jnp.int32, (count * slots, tokens), 1) == token) & (
            index >= CONV - 1
        )
        rows = dot32(chosen.astype(jnp.bfloat16), series)
        for p in range(PROMPTS):
            for j in range(CONV - 1):
                rows = jnp.where((owner == p) & (index == j), past_of(j, p), rows)
        return rows.astype(jnp.bfloat16)

    for lanes in range(2):
        cut = slice(lanes * STATE, min((lanes + 1) * STATE, inner))
        rows = kept_rows(
            0, requests, 8, in_x[:, cut], lambda j, p: past_x_ref[j, p : p + 1, cut].astype(jnp.float32)
        )
        for r in range(requests):
            kept_ref[r, inner + 8 * lanes : inner + 8 * (lanes + 1), : rows.shape[1]] = rows[
                r * 8 : (r + 1) * 8
            ]
    kept_ref[:, inner + 8 :, inner - STATE :] = jnp.zeros(
        (requests, 8, 2 * STATE - inner), jnp.bfloat16
    )
    kept_bc_ref[...] = kept_rows(
        rank * (requests // SIDE),
        requests // SIDE,
        8,
        in_bc,
        lambda j, p: past_bc_ref[j, p : p + 1, :].astype(jnp.float32),
    )


def keeper(member, accepted, log_decay, scaled_x, b_part, in_x, in_bc, past_x, past_bc, state):
    tokens, inner = scaled_x.shape
    requests = tokens // DRAFT
    operands = (member, accepted, log_decay, scaled_x, b_part, in_x, in_bc, past_x, past_bc, state)
    whole = pl.BlockSpec(memory_space=pltpu.VMEM)
    return pl.pallas_call(
        keeper_kernel,
        out_shape=[
            jax.ShapeDtypeStruct((requests, inner + 16, STATE), jnp.bfloat16),
            jax.ShapeDtypeStruct((requests // SIDE * 8, 2 * STATE), jnp.bfloat16),
        ],
        in_specs=[pl.BlockSpec(memory_space=pltpu.HBM)] * len(operands),
        out_specs=[whole] * 2,
        scratch_shapes=[
            *(pltpu.SMEM(a.shape, a.dtype) for a in operands[:2]),
            *(pltpu.VMEM(a.shape, a.dtype) for a in operands[2:]),
            pltpu.SemaphoreType.DMA((len(operands),)),
        ],
        compiler_params=pltpu.CompilerParams(vmem_limit_bytes=32 << 20),
        cost_estimate=pl.CostEstimate(
            flops=2_000_000_000, bytes_accessed=5_000_000, transcendentals=200_000
        ),
        name="keeper",
    )(*operands)


def unpack_kernel(kept_hbm, bc_ref, _stats, _tip, state_ref, conv_ref, kept_ref, sem):
    copy = pltpu.make_async_copy(kept_hbm, kept_ref, sem)
    copy.start()
    copy.wait()
    inner = kept_ref.shape[2] - 16
    for r in range(state_ref.shape[0]):
        for z in range(kept_ref.shape[0]):
            state_ref[r, z * inner : (z + 1) * inner, :] = kept_ref[z, r, :inner, :].astype(
                jnp.float32
            )
    for j in range(CONV - 1):
        rows = []
        for r in range(state_ref.shape[0]):
            pieces = []
            for z in range(kept_ref.shape[0]):
                tail = kept_ref[z, r, inner:, :].astype(jnp.float32)
                pieces += [tail[j : j + 1, :], tail[8 + j : 9 + j, : inner - STATE]]
            pieces.append(bc_ref[...].astype(jnp.float32)[r * 8 + j : r * 8 + j + 1, :])
            rows.append(jnp.concatenate(pieces, axis=1))
        conv_ref[j] = jnp.concatenate(rows, axis=0).astype(jnp.bfloat16)


def unpack(kept_out, own_bc, *tokens):
    sources, requests, rows, _ = kept_out.shape
    inner = rows - 16
    whole = pl.BlockSpec(memory_space=pltpu.VMEM)
    state, conv = pl.pallas_call(
        unpack_kernel,
        out_shape=[
            jax.ShapeDtypeStruct((requests, sources * inner, STATE), jnp.float32),
            jax.ShapeDtypeStruct((CONV - 1, requests, sources * inner + 2 * STATE), jnp.bfloat16),
        ],
        in_specs=[pl.BlockSpec(memory_space=pltpu.HBM), whole]
        + [pl.BlockSpec(memory_space=pl.ANY)] * len(tokens),
        out_specs=[whole] * 2,
        scratch_shapes=[pltpu.VMEM(kept_out.shape, kept_out.dtype), pltpu.SemaphoreType.DMA],
        compiler_params=pltpu.CompilerParams(vmem_limit_bytes=48 << 20),
        cost_estimate=pl.CostEstimate(flops=1_000_000, bytes_accessed=20_000_000, transcendentals=0),
        name="unpack",
    )(kept_out, own_bc, *tokens)
    return state, conv.transpose(1, 0, 2)


def mixer_kernel(*refs):
    sources, refs = refs[:22], refs[22:]
    part_refs = refs[:SIDE]
    decay_ref, scaled_ref, b_ref, in_x_ref, in_bc_ref = refs[SIDE : SIDE + 5]
    held, (mixed_scr, lanes_scr, sems) = refs[SIDE + 5 : -3], refs[-3:]
    member_ref, accepted_ref, lengths_ref, rate_ref, bias_ref, skip_ref = held[:6]
    hidden_ref, gain_ref, w_dt_ref, conv_x_ref, conv_bc_ref, past_x_ref, past_bc_ref = held[6:13]
    w_query, w_kv, prompt, w_x, w_bc, w_z, state, w_out = held[13:]
    tokens = hidden_ref.shape[0]
    requests = tokens // DRAFT
    inner = w_x.shape[1]
    heads = inner // SSM_DIM
    query_width = w_query.shape[1]
    rank = lax.axis_index("mdl")
    group = rank * (query_width // HEAD_DIM) // (Q_HEADS // KV_HEADS)
    query_hbm, kv_hbm, prompt_hbm, x_hbm, bc_hbm, z_hbm, state_hbm, attn_hbm, mamba_hbm = sources[13:]
    moves = [(source, target) for source, target in zip(sources[:13], held[:13], strict=True)]
    moves += [
        (query_hbm, w_query),
        (kv_hbm.at[group], w_kv),
        (prompt_hbm.at[0, group], prompt.at[0]),
        (prompt_hbm.at[1, group], prompt.at[1]),
        (x_hbm, w_x),
        (bc_hbm, w_bc),
        (z_hbm, w_z),
        (state_hbm, state),
        (attn_hbm, w_out.at[pl.ds(0, query_width), :]),
        (mamba_hbm, w_out.at[pl.ds(query_width, inner), :]),
    ]
    started = [
        pltpu.make_async_copy(source, target, sems.at[index])
        for index, (source, target) in enumerate(moves)
    ]
    for copy in started:
        copy.start()
    for copy in started[:13]:
        copy.wait()
    copies = started[13:]

    def head_row(ref):
        lane = lax.broadcasted_iota(jnp.int32, (1, heads), 1)
        values = jnp.zeros((1, heads), jnp.float32)
        for h in range(heads):
            values = jnp.where(lane == h, ref[h], values)
        return values

    row = lax.broadcasted_iota(jnp.int32, (tokens, 1), 0)
    time, request = row % DRAFT, row // DRAFT
    own_prompt = jnp.zeros((tokens, 1), jnp.int32)
    last = jnp.zeros((tokens, 1), jnp.int32)
    for r in range(requests):
        own_prompt = jnp.where(request == r, member_ref[r], own_prompt)
        last = jnp.where(request == r, accepted_ref[r] - 1, last)
    first_prompt = own_prompt == 0

    gain = jnp.concatenate(
        [gain_ref[j : j + 1, :].astype(jnp.float32) for j in range(gain_ref.shape[0])], axis=1
    )
    widened = hidden_ref[...].astype(jnp.float32)
    spread = jnp.mean(widened * widened, axis=-1, keepdims=True)
    normed = (
        widened * lax.rsqrt(spread + eps_norm) * gain
    ).astype(jnp.bfloat16)

    copies[0].wait()
    queries = dot32(normed, w_query[...]).astype(jnp.bfloat16)
    copies[1].wait()
    drafts = dot32(normed, w_kv[...]).astype(jnp.bfloat16)
    local_heads = query_width // HEAD_DIM
    query_rows = jnp.concatenate(
        [queries[:, h * HEAD_DIM : (h + 1) * HEAD_DIM] for h in range(local_heads)], axis=0
    )
    scale = HEAD_DIM**-0.5
    row_first = jnp.concatenate([own_prompt] * local_heads, axis=0) == 0
    draft_scores = dot32(query_rows, drafts[:, :HEAD_DIM], NEXT_TO) * scale
    same = (row // DRAFT == lax.broadcasted_iota(jnp.int32, (tokens, tokens), 1) // DRAFT) & (
        lax.broadcasted_iota(jnp.int32, (tokens, tokens), 1) <= row
    )
    draft_mask = jnp.concatenate([same] * local_heads, axis=0)
    draft_scores = jnp.where(draft_mask, draft_scores, far_below)
    copies[2].wait()
    copies[3].wait()
    scores = jnp.where(
        row_first,
        dot32(query_rows, prompt[0, :, :HEAD_DIM], NEXT_TO),
        dot32(query_rows, prompt[1, :, :HEAD_DIM], NEXT_TO),
    )
    length = jnp.where(row_first, lengths_ref[0], lengths_ref[1])
    position = lax.broadcasted_iota(jnp.int32, scores.shape, 1)
    scores = jnp.where(position < length, scores * scale, far_below)
    top = jnp.maximum(
        jnp.max(scores, axis=1, keepdims=True), jnp.max(draft_scores, axis=1, keepdims=True)
    )
    weights = jnp.exp(scores - top)
    draft_weights = jnp.exp(draft_scores - top)
    total = jnp.sum(weights, axis=1, keepdims=True) + jnp.sum(draft_weights, axis=1, keepdims=True)
    weighted = (
        dot32(jnp.where(row_first, weights, 0.0).astype(jnp.bfloat16), prompt[0, :, HEAD_DIM:])
        + dot32(jnp.where(row_first, 0.0, weights).astype(jnp.bfloat16), prompt[1, :, HEAD_DIM:])
        + dot32(draft_weights.astype(jnp.bfloat16), drafts[:, HEAD_DIM:])
    )
    attended = (weighted / total).astype(jnp.bfloat16)
    for h in range(local_heads):
        mixed_scr[:, h * HEAD_DIM : (h + 1) * HEAD_DIM] = attended[h * tokens : (h + 1) * tokens]

    def convolve_rows(series, past_ref, taps_ref):
        past = [
            jnp.where(
                first_prompt,
                past_ref[j, 0:1, :].astype(jnp.float32),
                past_ref[j, 1:2, :].astype(jnp.float32),
            )
            for j in range(CONV - 1)
        ]
        taps = taps_ref[...].astype(jnp.float32)
        summed = series * taps[CONV - 1 : CONV, :]
        for shift in range(1, CONV):
            window = pltpu.roll(series, shift, 0)
            for t in range(shift):
                window = jnp.where(time == t, past[CONV - 1 - shift + t], window)
            summed = summed + window * taps[CONV - 1 - shift : CONV - shift, :]
        return summed * jax.nn.sigmoid(summed)

    copies[4].wait()
    in_x = dot32(normed, w_x[...]).astype(jnp.bfloat16)
    heads_x = convolve_rows(in_x.astype(jnp.float32), past_x_ref, conv_x_ref)
    copies[5].wait()
    in_bc = dot32(normed, w_bc[...]).astype(jnp.bfloat16)
    conv_bcs = convolve_rows(in_bc.astype(jnp.float32), past_bc_ref, conv_bc_ref)
    b_part = conv_bcs[:, :STATE].astype(jnp.bfloat16)
    c_part = conv_bcs[:, STATE:].astype(jnp.bfloat16)

    def widen(values):
        lanes_scr[...] = jnp.zeros(lanes_scr.shape, jnp.float32)
        lanes_scr[:, :heads] = values
        return lanes_scr[...]

    spread_lanes = lane_spread(tokens, inner)
    dt_in = dot32(normed, w_dt_ref[...], NEXT_TO).astype(jnp.bfloat16).astype(jnp.float32) + head_row(bias_ref)
    step = jnp.maximum(dt_in, 0.0) + jnp.log1p(jnp.exp(-jnp.abs(dt_in)))
    log_decay = exact_dot(same.astype(jnp.float32), widen(-step * head_row(rate_ref)))
    step_x = exact_dot(widen(step), spread_lanes)
    skip_x = exact_dot(widen(jnp.broadcast_to(head_row(skip_ref), (tokens, heads))), spread_lanes)
    decay_x = exact_dot(log_decay, spread_lanes)
    turned = log_decay.T
    intersection = dot32(c_part, b_part, NEXT_TO)
    scaled_x = heads_x * step_x
    low = lax.broadcasted_iota(jnp.int32, (tokens, 2 * SSM_DIM), 1) < SSM_DIM
    groups = []
    for pair in range(heads // 2):
        mixing = []
        for h in (2 * pair, 2 * pair + 1):
            gaps = log_decay[:, h : h + 1] - turned[h : h + 1, :]
            mixing.append(
                (jnp.exp(jnp.where(same, gaps, far_below)) * intersection).astype(jnp.bfloat16)
            )
        lanes = scaled_x[:, pair * 2 * SSM_DIM : (pair + 1) * 2 * SSM_DIM]
        both = jnp.concatenate([jnp.where(low, lanes, 0.0), jnp.where(low, 0.0, lanes)], axis=0)
        groups.append(dot32(jnp.concatenate(mixing, axis=1), both.astype(jnp.bfloat16)))
    copies[7].wait()
    carried = jnp.where(
        first_prompt,
        dot32(c_part, state[0].astype(jnp.bfloat16), NEXT_TO),
        dot32(c_part, state[1].astype(jnp.bfloat16), NEXT_TO),
    )
    ssm_out = jnp.concatenate(groups, axis=1) + carried * jnp.exp(decay_x) + skip_x * heads_x
    copies[6].wait()
    gate_z = dot32(normed, w_z[...]).astype(jnp.bfloat16).astype(jnp.float32)
    mixed_scr[:, query_width:] = (ssm_out * (gate_z * jax.nn.sigmoid(gate_z))).astype(jnp.bfloat16)

    own_rows = tokens // SIDE
    copies[8].wait()
    copies[9].wait()
    rows = jnp.concatenate(
        [
            mixed_scr[pl.ds(pl.multiple_of((rank ^ flip) * own_rows, own_rows), own_rows), :]
            for flip in (0, *DIRECT)
        ],
        axis=0,
    )
    parts = dot32(rows, w_out[...]).astype(jnp.bfloat16)
    for block, part_ref in enumerate(part_refs):
        part_ref[...] = parts[block * own_rows : (block + 1) * own_rows]
    decay_ref[...] = log_decay
    scaled_ref[...] = scaled_x
    b_ref[...] = b_part
    in_x_ref[...] = in_x
    in_bc_ref[...] = in_bc


def mixer(
    hidden, mixer_gain, w_query, w_kv, w_attn_out, prompt_kv, prompt_lengths, member, accepted, w_z, w_x, w_bc,
    w_dt, conv_x, conv_bc, ssm_rate, dt_bias, skip_d, prompt_state, prompt_conv_x, prompt_conv_bc, w_mamba_out,
):
    tokens, width = hidden.shape
    inner = w_x.shape[1]
    query_width = w_query.shape[1]
    bf16 = jnp.bfloat16
    state = prompt_state.reshape(PROMPTS, inner, STATE)
    small = [
        hidden, mixer_gain.reshape(-1, 128), w_dt.T, conv_x, conv_bc,
        prompt_conv_x.transpose(1, 0, 2), prompt_conv_bc.transpose(1, 0, 2),
    ]
    scalars = [member, accepted, prompt_lengths, ssm_rate, dt_bias, skip_d]
    whole = pl.BlockSpec(memory_space=pltpu.VMEM)
    outs = pl.pallas_call(
        mixer_kernel,
        out_shape=[
            *([jax.ShapeDtypeStruct((tokens // SIDE, width), bf16)] * SIDE),
            jax.ShapeDtypeStruct((tokens, 128), jnp.float32),
            jax.ShapeDtypeStruct((tokens, inner), jnp.float32),
            jax.ShapeDtypeStruct((tokens, STATE), bf16),
            jax.ShapeDtypeStruct((tokens, inner), bf16),
            jax.ShapeDtypeStruct((tokens, 2 * STATE), bf16),
        ],
        in_specs=[pl.BlockSpec(memory_space=pltpu.HBM)] * 22,
        out_specs=[whole] * (SIDE + 5),
        scratch_shapes=[
            *(pltpu.SMEM(a.shape, a.dtype) for a in scalars),
            *(pltpu.VMEM(a.shape, a.dtype) for a in small),
            pltpu.VMEM(w_query.shape, bf16),
            pltpu.VMEM(w_kv.shape[1:], bf16),
            pltpu.VMEM((PROMPTS, *prompt_kv.shape[2:]), bf16),
            pltpu.VMEM(w_x.shape, bf16),
            pltpu.VMEM(w_bc.shape, bf16),
            pltpu.VMEM(w_z.shape, bf16),
            pltpu.VMEM(state.shape, jnp.float32),
            pltpu.VMEM((query_width + inner, width), bf16),
            pltpu.VMEM((tokens, query_width + inner), bf16),
            pltpu.VMEM((tokens, 128), jnp.float32),
            pltpu.SemaphoreType.DMA((23,)),
        ],
        compiler_params=pltpu.CompilerParams(vmem_limit_bytes=59 << 20),
        cost_estimate=pl.CostEstimate(
            flops=3_000_000_000, bytes_accessed=20_000_000, transcendentals=1_000_000
        ),
        name="mixer",
    )(
        *scalars, *small, w_query, w_kv, prompt_kv, w_x, w_bc, w_z, state, w_attn_out, w_mamba_out
    )
    return outs[:SIDE], *keeper(member, accepted, *outs[SIDE:], *small[-2:], state)


def feed_kernel(first_ref, second_ref, both_ref, down_ref, first_out, second_out):
    hidden = down_ref.shape[0]
    rows = first_ref.shape[0]
    joined = jnp.concatenate([first_ref[...], second_ref[...]], axis=0)
    pair = dot32(joined, both_ref[...])
    gate, up = pair[:, :hidden], pair[:, hidden:]
    active = (gate * jax.nn.sigmoid(gate) * up).astype(jnp.bfloat16)
    parts = dot32(active, down_ref[...]).astype(jnp.bfloat16)
    first_out[...] = parts[:rows]
    second_out[...] = parts[rows:]


def feed(first, second, w_both, w_down):
    rows, width = first.shape
    whole = pl.BlockSpec(memory_space=pltpu.VMEM)
    return pl.pallas_call(
        feed_kernel,
        out_shape=[jax.ShapeDtypeStruct((rows, width), jnp.bfloat16)] * 2,
        in_specs=[whole] * 4,
        out_specs=[whole] * 2,
        compiler_params=pltpu.CompilerParams(vmem_limit_bytes=16 << 20),
        cost_estimate=pl.CostEstimate(
            flops=20 * 2 * rows * width * 2 * 3 * w_down.shape[0],
            bytes_accessed=4 * rows * width * 2 + 3 * w_down.size * 2,
            transcendentals=2 * rows * w_down.shape[0],
        ),
        name="feed",
    )(first, second, w_both, w_down)


def head_kernel(targets_ref, owners_ref, *refs):
    count = targets_ref.shape[0]
    rows_refs, head_ref, others, out_ref = refs[:count], refs[count], refs[count + 1 : -1], refs[-1]
    vocab = head_ref.shape[0]
    lanes = 2 * rows_refs[0].shape[0]
    slots = out_ref.shape[0]
    base = lax.axis_index("req") * vocab
    lane = lax.broadcasted_iota(jnp.int32, (lanes, 128), 0)
    column = lax.broadcasted_iota(jnp.int32, (lanes, 128), 1)
    place = (column == lane % (2 * DRAFT)).astype(jnp.bfloat16)
    ids = lax.broadcasted_iota(jnp.int32, (vocab, lanes), 0) + base
    slot = lax.broadcasted_iota(jnp.int32, (slots, lanes), 0)
    packed = jnp.zeros(out_ref.shape, jnp.float32)
    for other in others:
        packed = packed + other[...]
    for pair in range(count // 2):
        joined = jnp.concatenate([rows_refs[2 * pair][...], rows_refs[2 * pair + 1][...]], axis=0)
        wanted = jnp.concatenate(
            [targets_ref[2 * pair : 2 * pair + 1, :], targets_ref[2 * pair + 1 : 2 * pair + 2, :]],
            axis=1,
        )
        owner = jnp.concatenate(
            [owners_ref[2 * pair : 2 * pair + 1, :], owners_ref[2 * pair + 1 : 2 * pair + 2, :]],
            axis=1,
        )
        logits = dot32(head_ref[...], joined, NEXT_TO)
        target = jnp.sum(jnp.where(ids == wanted, logits, 0.0), axis=0, keepdims=True)
        top = jnp.max(logits, axis=0, keepdims=True)
        total = jnp.sum(jnp.exp(logits - top), axis=0, keepdims=True)
        stats = jnp.where(slot % 8 == 0, top, jnp.where(slot % 8 == 1, total, target))
        rest = jnp.where((slot // 8 == owner) & (slot % 8 < 3), stats, 0.0)
        for _ in range(3):
            part = rest.astype(jnp.bfloat16)
            packed = packed + dot32(part, place)
            rest = rest - part.astype(jnp.float32)
    out_ref[...] = packed


def head_stats(targets, owners, rows, head_weight, devices, others=()):
    whole = pl.BlockSpec(memory_space=pltpu.VMEM)
    return pl.pallas_call(
        head_kernel,
        out_shape=jax.ShapeDtypeStruct((devices * 8, 128), jnp.float32),
        in_specs=[whole] * (3 + len(rows) + len(others)),
        out_specs=whole,
        compiler_params=pltpu.CompilerParams(vmem_limit_bytes=32 << 20),
        cost_estimate=pl.CostEstimate(
            flops=10 * 2 * len(rows) * rows[0].size * head_weight.shape[0],
            bytes_accessed=2 * len(rows) * rows[0].size + 2 * head_weight.size,
            transcendentals=len(rows) * rows[0].shape[0] * head_weight.shape[0],
        ),
        name="head_stats",
    )(targets, owners, *rows, head_weight, *others)


def shards(
    hidden_in,
    mixer_gain,
    w_query,
    w_kv,
    w_attn_out,
    prompt_kv,
    prompt_lengths,
    member,
    accepted,
    w_z,
    w_x,
    w_bc,
    w_dt,
    conv_x,
    conv_bc,
    ssm_rate,
    dt_bias,
    skip_d,
    prompt_state,
    prompt_conv_x,
    prompt_conv_bc,
    w_mamba_out,
    mlp_gain,
    w_gate,
    w_up,
    w_down,
    final_gain,
    head_weight,
    draft_ids,
):
    row_reqs, draft_len, width = hidden_in.shape
    mdl_count = lax.axis_size("mdl")
    req_count = lax.axis_size("req")
    mdl_rank = lax.axis_index("mdl")
    req_rank = lax.axis_index("req")
    row_tokens = row_reqs * draft_len
    own_reqs = row_reqs // mdl_count
    own_tokens = own_reqs * draft_len
    flat_rows = hidden_in.reshape(row_tokens, width)
    local_inner = w_x.shape[1]
    parts, kept, own_bc = mixer(
        flat_rows, mixer_gain, w_query, w_kv, w_attn_out, prompt_kv, prompt_lengths, member, accepted, w_z, w_x, w_bc,
        w_dt, conv_x, conv_bc, ssm_rate, dt_bias, skip_d, prompt_state, prompt_conv_x, prompt_conv_bc, w_mamba_out,
    )
    came = [
        lax.ppermute(part, "mdl", [(z, z ^ flip) for z in range(SIDE)])
        for part, flip in zip(parts[1:], DIRECT, strict=True)
    ]
    mixed = sum((part.astype(jnp.float32) for part in came), parts[0].astype(jnp.float32))
    own_rows = lax.dynamic_slice_in_dim(flat_rows, mdl_rank * own_tokens, own_tokens, 0)
    after_mixer = (own_rows.astype(jnp.float32) + mixed).astype(jnp.bfloat16)
    prepared = rms_scale(after_mixer, mlp_gain).astype(jnp.bfloat16)
    w_both = jnp.concatenate([w_gate, w_up], axis=1)
    held, late = gather_rows(prepared)
    early = (held, [swap_core(part) for part in held])
    late = (late, [swap_core(part) for part in late])

    core = req_rank % CORES
    chip_x = req_rank // CORES % SIDE
    chip_y = req_rank // (CORES * SIDE)
    table = jnp.where(core == 0, jnp.asarray(block_table()[0]), jnp.asarray(block_table()[1]))
    owner = ((chip_y ^ table[:, 0]) * SIDE + (chip_x ^ table[:, 1])) * CORES + (core ^ table[:, 2])
    request = owner * row_reqs + mdl_rank * own_reqs + table[:, 3]
    next_ids = jnp.concatenate([draft_ids[:, 1:], draft_ids[:, :1]], axis=1)
    picked = (request[:, None] == jnp.arange(draft_ids.shape[0])[None, :]).astype(jnp.float32)
    targets = jnp.dot(picked, next_ids.astype(jnp.float32), precision=HIGHEST).astype(jnp.int32)
    targets = targets.reshape(8, 8 * draft_len)
    owners = jnp.broadcast_to(owner[:, None], (64, draft_len)).reshape(8, 8 * draft_len)

    early_parts = [feed(*rows, w_both, w_down) for rows in early]
    late_parts = [feed(*rows, w_both, w_down) for rows in late]
    summed = scatter_rows(early_parts, late_parts)
    tip = early_parts[0][0][:8, :128]
    kept, tip = lax.optimization_barrier((kept, tip))
    kept_out = lax.all_to_all(
        kept.reshape(mdl_count, own_reqs, local_inner + 16, STATE),
        "mdl",
        split_axis=0,
        concat_axis=0,
        tiled=True,
    )
    final_gain, kept_out, targets, owners = lax.optimization_barrier(
        (final_gain, kept_out, targets, owners)
    )
    after_feed = (after_mixer.astype(jnp.float32) + summed).astype(jnp.bfloat16)
    final_rows = rms_scale(after_feed, final_gain).astype(jnp.bfloat16)
    held, late = gather_rows(final_rows)
    early = held + [swap_core(part) for part in held]
    first_stats = head_stats(targets[:4], owners[:4], early, head_weight, req_count)
    late, first_stats = lax.optimization_barrier((late, first_stats))
    sibling = [swap_core(part) for part in late]
    stats = [first_stats, head_stats(targets[4:6], owners[4:6], late, head_weight, req_count)]
    stats = head_stats(targets[6:], owners[6:], sibling, head_weight, req_count, stats)
    kept_state, kept_conv = unpack(kept_out, own_bc, stats, tip)
    kept_state = kept_state.reshape(own_reqs, -1, SSM_DIM, STATE)
    shared = lax.all_to_all(stats, "req", split_axis=0, concat_axis=0, tiled=True)
    shared = shared.reshape(req_count, 8, 128)[:, :, :own_tokens]
    tops, totals, hits = shared[:, 0], shared[:, 1], shared[:, 2]
    top = jnp.max(tops, axis=0)
    total = jnp.sum(totals * jnp.exp(tops - top[None, :]), axis=0)
    log_total = top + jnp.log(total)
    position = jnp.arange(own_tokens) % draft_len
    verify_scores = jnp.where(
        position < draft_len - 1, jnp.sum(hits, axis=0) - log_total, top - log_total
    ).reshape(own_reqs, draft_len)
    return (
        after_feed.reshape(own_reqs, draft_len, width),
        verify_scores,
        kept_state,
        kept_conv,
    )


def solution(mesh):
    in_specs = (
        P("req", None, None),
        P(),
        P(None, "mdl"),
        P(),
        P("mdl", None),
        P("req", None, None, None),
        P("req"),
        P("req"),
        P("req"),
        P(None, "mdl"),
        P(None, "mdl"),
        P(),
        P(None, "mdl"),
        P(None, "mdl"),
        P(),
        P("mdl"),
        P("mdl"),
        P("mdl"),
        P("req", "mdl", None, None),
        P("req", None, "mdl"),
        P("req", None, None),
        P("mdl", None),
        P(),
        P(None, "req"),
        P(None, "req"),
        P("req", None),
        P(),
        P("req", None),
        P(),
    )
    out_specs = (
        P(("req", "mdl"), None, None),
        P(("req", "mdl"), None),
        P(("req", "mdl"), None, None, None),
        P(("req", "mdl"), None, None),
    )
    return jax.shard_map(shards, mesh=mesh, in_specs=in_specs, out_specs=out_specs, check_vma=False)
```

```python
import functools

import jax
import jax.numpy as jnp
import numpy as np
from jax import lax
from jax.experimental import pallas as pl
from jax.experimental.pallas import tpu as pltpu
from jax.sharding import PartitionSpec as P

Q_HEADS = 8
KV_HEADS = 2
HEAD_DIM = 128
SSM_DIM = 64
STATE = 256
CONV = 4
PROMPTS = 2
P_MAX = 1024
DRAFT = 16
SIDE = 4
CORES = 2

eps_norm = 1e-05
far_below = -1e30

DIRECT = (1, 3, 2)
EDGES = ((1, 3), (3, 1))


def device_at(y, x, core):
    return (y * SIDE + x) * CORES + core


def flip_pairs(ring, flip):
    pairs = []
    for y in range(SIDE):
        for x in range(SIDE):
            for core in range(CORES):
                on_x = ring == core
                target = device_at(y if on_x else y ^ flip, x ^ flip if on_x else x, core)
                pairs.append((device_at(y, x, core), target))
    return pairs


CORE_PAIRS = [(device, device ^ 1) for device in range(SIDE * SIDE * CORES)]


def hop(part, ring, flip):
    return lax.ppermute(part, "req", flip_pairs(ring, flip))


def swap_core(part):
    return lax.ppermute(part, "req", CORE_PAIRS)


def gather_rows(rows):
    came = [hop(rows, 0, flip) for flip in DIRECT]
    held = [jnp.concatenate([rows, came[0]], axis=0), jnp.concatenate(came[1:], axis=0)]
    near = [hop(held[s], 1, EDGES[s][0]) for s in range(2)]
    far = [hop(held[s], 1, EDGES[s][1]) for s in range(2)]
    last = [hop(near[s], 1, EDGES[s][1]) for s in range(2)]
    return held + near + far, last


def added(*parts):
    return sum(part.astype(jnp.float32) for part in parts).astype(jnp.bfloat16)


def scatter_rows(early, late):
    rows = late[0][0].shape[0]

    def stream(joined, s):
        return joined[s * rows : (s + 1) * rows]

    came = swap_core(late[1][0])
    last = [hop(added(late[0][s], stream(came, s)), 1, EDGES[s][1]) for s in range(2)]
    kept, near, far = (swap_core(part) for part in early[1])
    own = early[0]
    far = [hop(added(own[4 + s], stream(far, s)), 1, EDGES[s][1]) for s in range(2)]
    near = [hop(added(own[2 + s], stream(near, s), last[s]), 1, EDGES[s][0]) for s in range(2)]
    held = [added(own[s], stream(kept, s), far[s], near[s]) for s in range(2)]
    half = held[0].shape[0] // 2
    blocks = (held[0][half:], held[1][:half], held[1][half:])
    came = [hop(block, 0, flip) for block, flip in zip(blocks, DIRECT, strict=True)]
    total = held[0][:half].astype(jnp.float32)
    return sum((part.astype(jnp.float32) for part in came), total)


def swap_early(arrays):
    kept = [swap_core(part) for part in arrays[:2]]
    return kept + [swap_core(jnp.concatenate(arrays[k : k + 2], axis=0)) for k in (2, 4)]


def block_table():
    arrays = [(half, kind) for half in range(2) for kind in range(3)] + [(0, 3), (1, 3)]
    table = np.zeros((CORES, len(arrays), 2, 2, 2, 4), np.int32)
    for core, array, stream, block, request in np.ndindex(table.shape[:-1]):
        half, kind = arrays[array]
        first = ((0, 1), (3, 2))[stream][block]
        other = (0, *EDGES[stream], 2)[kind]
        y, x = (other, first) if core == half else (first, other)
        table[core, array, stream, block, request] = (y, x, half, request)
    return table.reshape(CORES, 64, 4)


def rms_scale(values, gain):
    widened = values.astype(jnp.float32)
    spread = jnp.mean(widened * widened, axis=-1, keepdims=True)
    return widened * lax.rsqrt(spread + eps_norm) * gain.astype(jnp.float32)


HIGHEST = lax.Precision.HIGHEST
NEXT_TO = (((1,), (1,)), ((), ()))


def dot32(left, right, dims=None):
    dims = dims or (((1,), (0,)), ((), ()))
    return lax.dot_general(left, right, dims, preferred_element_type=jnp.float32)


def exact_dot(left, right):
    return jnp.dot(left, right, precision=HIGHEST, preferred_element_type=jnp.float32)


def lane_spread(rows, lanes):
    return (
        lax.broadcasted_iota(jnp.int32, (rows, lanes), 0)
        == lax.broadcasted_iota(jnp.int32, (rows, lanes), 1) // SSM_DIM
    ).astype(jnp.float32)


def keeper_kernel(*refs):
    sources, (kept_ref, kept_bc_ref), held, sems = refs[:10], refs[10:12], refs[12:22], refs[22]
    copies = [
        pltpu.make_async_copy(source, target, sems.at[index])
        for index, (source, target) in enumerate(zip(sources, held, strict=True))
    ]
    for copy in copies:
        copy.start()
    for copy in copies:
        copy.wait()
    member_ref, accepted_ref, decay_ref, scaled_ref, b_ref, in_x_ref, in_bc_ref = held[:7]
    past_x_ref, past_bc_ref, state = held[7:]
    tokens, inner = scaled_ref.shape
    requests = tokens // DRAFT
    rank = lax.axis_index("mdl")

    row = lax.broadcasted_iota(jnp.int32, (tokens, 1), 0)
    time, request = row % DRAFT, row // DRAFT
    last = jnp.zeros((tokens, 1), jnp.int32)
    for r in range(requests):
        last = jnp.where(request == r, accepted_ref[r] - 1, last)
    spread_lanes = lane_spread(tokens, inner)
    log_decay, scaled_x, b_part = decay_ref[...], scaled_ref[...], b_ref[...]
    in_x, in_bc = in_x_ref[...], in_bc_ref[...]
    decay_x = exact_dot(log_decay, spread_lanes)
    other = lax.broadcasted_iota(jnp.int32, (tokens, tokens), 1)
    pick = (other == request * DRAFT + last).astype(jnp.float32)
    final_log = exact_dot(pick, log_decay)
    final_x = exact_dot(final_log, spread_lanes)
    carry_x = jnp.exp(jnp.where(time <= last, final_x - decay_x, far_below))
    carried_x = (scaled_x * carry_x).T.astype(jnp.bfloat16)
    shrink = jnp.exp(final_x).T
    for r in range(requests):
        b_here = jnp.where(request == r, b_part, jnp.zeros_like(b_part))
        kept = shrink[:, r * DRAFT : r * DRAFT + 1] * state[member_ref[r]] + dot32(
            carried_x, b_here
        )
        kept_ref[r, :inner, :] = kept.astype(jnp.bfloat16)

    def kept_rows(first_request, count, slots, series, past_of):
        at = lax.broadcasted_iota(jnp.int32, (count * slots, 1), 0)
        here, edge = at // slots, at % slots
        start = jnp.zeros((count * slots, 1), jnp.int32)
        owner = jnp.zeros((count * slots, 1), jnp.int32)
        for r in range(count):
            start = jnp.where(here == r, accepted_ref[first_request + r], start)
            owner = jnp.where(here == r, member_ref[first_request + r], owner)
        index = start + edge
        token = (here + first_request) * DRAFT + index - (CONV - 1)
        chosen = (lax.broadcasted_iota(jnp.int32, (count * slots, tokens), 1) == token) & (
            index >= CONV - 1
        )
        rows = dot32(chosen.astype(jnp.bfloat16), series)
        for p in range(PROMPTS):
            for j in range(CONV - 1):
                rows = jnp.where((owner == p) & (index == j), past_of(j, p), rows)
        return rows.astype(jnp.bfloat16)

    for lanes in range(2):
        cut = slice(lanes * STATE, min((lanes + 1) * STATE, inner))
        rows = kept_rows(
            0, requests, 8, in_x[:, cut], lambda j, p: past_x_ref[j, p : p + 1, cut].astype(jnp.float32)
        )
        for r in range(requests):
            kept_ref[r, inner + 8 * lanes : inner + 8 * (lanes + 1), : rows.shape[1]] = rows[
                r * 8 : (r + 1) * 8
            ]
    kept_ref[:, inner + 8 :, inner - STATE :] = jnp.zeros(
        (requests, 8, 2 * STATE - inner), jnp.bfloat16
    )
    kept_bc_ref[...] = kept_rows(
        rank * (requests // SIDE),
        requests // SIDE,
        8,
        in_bc,
        lambda j, p: past_bc_ref[j, p : p + 1, :].astype(jnp.float32),
    )


def keeper(member, accepted, log_decay, scaled_x, b_part, in_x, in_bc, past_x, past_bc, state):
    tokens, inner = scaled_x.shape
    requests = tokens // DRAFT
    operands = (member, accepted, log_decay, scaled_x, b_part, in_x, in_bc, past_x, past_bc, state)
    whole = pl.BlockSpec(memory_space=pltpu.VMEM)
    return pl.pallas_call(
        keeper_kernel,
        out_shape=[
            jax.ShapeDtypeStruct((requests, inner + 16, STATE), jnp.bfloat16),
            jax.ShapeDtypeStruct((requests // SIDE * 8, 2 * STATE), jnp.bfloat16),
        ],
        in_specs=[pl.BlockSpec(memory_space=pltpu.HBM)] * len(operands),
        out_specs=[whole] * 2,
        scratch_shapes=[
            *(pltpu.SMEM(a.shape, a.dtype) for a in operands[:2]),
            *(pltpu.VMEM(a.shape, a.dtype) for a in operands[2:]),
            pltpu.SemaphoreType.DMA((len(operands),)),
        ],
        compiler_params=pltpu.CompilerParams(vmem_limit_bytes=12 << 20),
        cost_estimate=pl.CostEstimate(
            flops=2_000_000_000, bytes_accessed=5_000_000, transcendentals=200_000
        ),
        name="keeper",
    )(*operands)


def unpack_kernel(kept_hbm, bc_ref, _stats, _tip, state_ref, conv_ref, kept_ref, sem):
    copy = pltpu.make_async_copy(kept_hbm, kept_ref, sem)
    copy.start()
    copy.wait()
    inner = kept_ref.shape[2] - 16
    for r in range(state_ref.shape[0]):
        for z in range(kept_ref.shape[0]):
            state_ref[r, z * inner : (z + 1) * inner, :] = kept_ref[z, r, :inner, :].astype(
                jnp.float32
            )
    for j in range(CONV - 1):
        rows = []
        for r in range(state_ref.shape[0]):
            pieces = []
            for z in range(kept_ref.shape[0]):
                tail = kept_ref[z, r, inner:, :].astype(jnp.float32)
                pieces += [tail[j : j + 1, :], tail[8 + j : 9 + j, : inner - STATE]]
            pieces.append(bc_ref[...].astype(jnp.float32)[r * 8 + j : r * 8 + j + 1, :])
            rows.append(jnp.concatenate(pieces, axis=1))
        conv_ref[j] = jnp.concatenate(rows, axis=0).astype(jnp.bfloat16)


def unpack(kept_out, own_bc, *tokens):
    sources, requests, rows, _ = kept_out.shape
    inner = rows - 16
    whole = pl.BlockSpec(memory_space=pltpu.VMEM)
    state, conv = pl.pallas_call(
        unpack_kernel,
        out_shape=[
            jax.ShapeDtypeStruct((requests, sources * inner, STATE), jnp.float32),
            jax.ShapeDtypeStruct((CONV - 1, requests, sources * inner + 2 * STATE), jnp.bfloat16),
        ],
        in_specs=[pl.BlockSpec(memory_space=pltpu.HBM), whole]
        + [pl.BlockSpec(memory_space=pl.ANY)] * len(tokens),
        out_specs=[whole] * 2,
        scratch_shapes=[pltpu.VMEM(kept_out.shape, kept_out.dtype), pltpu.SemaphoreType.DMA],
        compiler_params=pltpu.CompilerParams(vmem_limit_bytes=10 << 20),
        cost_estimate=pl.CostEstimate(flops=1_000_000, bytes_accessed=20_000_000, transcendentals=0),
        name="unpack",
    )(kept_out, own_bc, *tokens)
    return state, conv.transpose(1, 0, 2)


def mixer_kernel(*refs):
    sources, refs = refs[:22], refs[22:]
    part_refs = refs[:SIDE]
    decay_ref, scaled_ref, b_ref, in_x_ref, in_bc_ref = refs[SIDE : SIDE + 5]
    held, (mixed_scr, lanes_scr, sems) = refs[SIDE + 5 : -3], refs[-3:]
    member_ref, accepted_ref, lengths_ref, rate_ref, bias_ref, skip_ref = held[:6]
    hidden_ref, gain_ref, w_dt_ref, conv_x_ref, conv_bc_ref, past_x_ref, past_bc_ref = held[6:13]
    w_query, w_kv, prompt, w_x, w_bc, w_z, state, w_out = held[13:]
    tokens = hidden_ref.shape[0]
    requests = tokens // DRAFT
    inner = w_x.shape[1]
    heads = inner // SSM_DIM
    query_width = w_query.shape[1]
    rank = lax.axis_index("mdl")
    group = rank * (query_width // HEAD_DIM) // (Q_HEADS // KV_HEADS)
    query_hbm, kv_hbm, prompt_hbm, x_hbm, bc_hbm, z_hbm, state_hbm, attn_hbm, mamba_hbm = sources[13:]
    moves = [(source, target) for source, target in zip(sources[:13], held[:13], strict=True)]
    moves += [
        (query_hbm, w_query),
        (kv_hbm.at[group], w_kv),
        (prompt_hbm.at[0, group], prompt.at[0]),
        (prompt_hbm.at[1, group], prompt.at[1]),
        (x_hbm, w_x),
        (bc_hbm, w_bc),
        (z_hbm, w_z),
        (state_hbm, state),
        (attn_hbm, w_out.at[pl.ds(0, query_width), :]),
        (mamba_hbm, w_out.at[pl.ds(query_width, inner), :]),
    ]
    started = [
        pltpu.make_async_copy(source, target, sems.at[index])
        for index, (source, target) in enumerate(moves)
    ]
    for copy in started:
        copy.start()
    for copy in started[:13]:
        copy.wait()
    copies = started[13:]

    def head_row(ref):
        lane = lax.broadcasted_iota(jnp.int32, (1, heads), 1)
        values = jnp.zeros((1, heads), jnp.float32)
        for h in range(heads):
            values = jnp.where(lane == h, ref[h], values)
        return values

    row = lax.broadcasted_iota(jnp.int32, (tokens, 1), 0)
    time, request = row % DRAFT, row // DRAFT
    own_prompt = jnp.zeros((tokens, 1), jnp.int32)
    last = jnp.zeros((tokens, 1), jnp.int32)
    for r in range(requests):
        own_prompt = jnp.where(request == r, member_ref[r], own_prompt)
        last = jnp.where(request == r, accepted_ref[r] - 1, last)
    first_prompt = own_prompt == 0

    gain = jnp.concatenate(
        [gain_ref[j : j + 1, :].astype(jnp.float32) for j in range(gain_ref.shape[0])], axis=1
    )
    widened = hidden_ref[...].astype(jnp.float32)
    spread = jnp.mean(widened * widened, axis=-1, keepdims=True)
    normed = (
        widened * lax.rsqrt(spread + eps_norm) * gain
    ).astype(jnp.bfloat16)

    copies[0].wait()
    queries = dot32(normed, w_query[...]).astype(jnp.bfloat16)
    copies[1].wait()
    drafts = dot32(normed, w_kv[...]).astype(jnp.bfloat16)
    local_heads = query_width // HEAD_DIM
    query_rows = jnp.concatenate(
        [queries[:, h * HEAD_DIM : (h + 1) * HEAD_DIM] for h in range(local_heads)], axis=0
    )
    scale = HEAD_DIM**-0.5
    row_first = jnp.concatenate([own_prompt] * local_heads, axis=0) == 0
    draft_scores = dot32(query_rows, drafts[:, :HEAD_DIM], NEXT_TO) * scale
    same = (row // DRAFT == lax.broadcasted_iota(jnp.int32, (tokens, tokens), 1) // DRAFT) & (
        lax.broadcasted_iota(jnp.int32, (tokens, tokens), 1) <= row
    )
    draft_mask = jnp.concatenate([same] * local_heads, axis=0)
    draft_scores = jnp.where(draft_mask, draft_scores, far_below)
    copies[2].wait()
    copies[3].wait()
    scores = jnp.where(
        row_first,
        dot32(query_rows, prompt[0, :, :HEAD_DIM], NEXT_TO),
        dot32(query_rows, prompt[1, :, :HEAD_DIM], NEXT_TO),
    )
    length = jnp.where(row_first, lengths_ref[0], lengths_ref[1])
    position = lax.broadcasted_iota(jnp.int32, scores.shape, 1)
    scores = jnp.where(position < length, scores * scale, far_below)
    top = jnp.maximum(
        jnp.max(scores, axis=1, keepdims=True), jnp.max(draft_scores, axis=1, keepdims=True)
    )
    weights = jnp.exp(scores - top)
    draft_weights = jnp.exp(draft_scores - top)
    total = jnp.sum(weights, axis=1, keepdims=True) + jnp.sum(draft_weights, axis=1, keepdims=True)
    weighted = (
        dot32(jnp.where(row_first, weights, 0.0).astype(jnp.bfloat16), prompt[0, :, HEAD_DIM:])
        + dot32(jnp.where(row_first, 0.0, weights).astype(jnp.bfloat16), prompt[1, :, HEAD_DIM:])
        + dot32(draft_weights.astype(jnp.bfloat16), drafts[:, HEAD_DIM:])
    )
    attended = (weighted / total).astype(jnp.bfloat16)
    for h in range(local_heads):
        mixed_scr[:, h * HEAD_DIM : (h + 1) * HEAD_DIM] = attended[h * tokens : (h + 1) * tokens]

    def convolve_rows(series, past_ref, taps_ref):
        past = [
            jnp.where(
                first_prompt,
                past_ref[j, 0:1, :].astype(jnp.float32),
                past_ref[j, 1:2, :].astype(jnp.float32),
            )
            for j in range(CONV - 1)
        ]
        taps = taps_ref[...].astype(jnp.float32)
        summed = series * taps[CONV - 1 : CONV, :]
        for shift in range(1, CONV):
            window = pltpu.roll(series, shift, 0)
            for t in range(shift):
                window = jnp.where(time == t, past[CONV - 1 - shift + t], window)
            summed = summed + window * taps[CONV - 1 - shift : CONV - shift, :]
        return summed * jax.nn.sigmoid(summed)

    copies[4].wait()
    in_x = dot32(normed, w_x[...]).astype(jnp.bfloat16)
    heads_x = convolve_rows(in_x.astype(jnp.float32), past_x_ref, conv_x_ref)
    copies[5].wait()
    in_bc = dot32(normed, w_bc[...]).astype(jnp.bfloat16)
    conv_bcs = convolve_rows(in_bc.astype(jnp.float32), past_bc_ref, conv_bc_ref)
    b_part = conv_bcs[:, :STATE].astype(jnp.bfloat16)
    c_part = conv_bcs[:, STATE:].astype(jnp.bfloat16)

    def widen(values):
        lanes_scr[...] = jnp.zeros(lanes_scr.shape, jnp.float32)
        lanes_scr[:, :heads] = values
        return lanes_scr[...]

    spread_lanes = lane_spread(tokens, inner)
    dt_in = dot32(normed, w_dt_ref[...], NEXT_TO).astype(jnp.bfloat16).astype(jnp.float32) + head_row(bias_ref)
    step = jnp.maximum(dt_in, 0.0) + jnp.log1p(jnp.exp(-jnp.abs(dt_in)))
    log_decay = exact_dot(same.astype(jnp.float32), widen(-step * head_row(rate_ref)))
    step_x = exact_dot(widen(step), spread_lanes)
    skip_x = exact_dot(widen(jnp.broadcast_to(head_row(skip_ref), (tokens, heads))), spread_lanes)
    decay_x = exact_dot(log_decay, spread_lanes)
    turned = log_decay.T
    intersection = dot32(c_part, b_part, NEXT_TO)
    scaled_x = heads_x * step_x
    low = lax.broadcasted_iota(jnp.int32, (tokens, 2 * SSM_DIM), 1) < SSM_DIM
    groups = []
    for pair in range(heads // 2):
        mixing = []
        for h in (2 * pair, 2 * pair + 1):
            gaps = log_decay[:, h : h + 1] - turned[h : h + 1, :]
            mixing.append(
                (jnp.exp(jnp.where(same, gaps, far_below)) * intersection).astype(jnp.bfloat16)
            )
        lanes = scaled_x[:, pair * 2 * SSM_DIM : (pair + 1) * 2 * SSM_DIM]
        both = jnp.concatenate([jnp.where(low, lanes, 0.0), jnp.where(low, 0.0, lanes)], axis=0)
        groups.append(dot32(jnp.concatenate(mixing, axis=1), both.astype(jnp.bfloat16)))
    copies[7].wait()
    carried = jnp.where(
        first_prompt,
        dot32(c_part, state[0].astype(jnp.bfloat16), NEXT_TO),
        dot32(c_part, state[1].astype(jnp.bfloat16), NEXT_TO),
    )
    ssm_out = jnp.concatenate(groups, axis=1) + carried * jnp.exp(decay_x) + skip_x * heads_x
    copies[6].wait()
    gate_z = dot32(normed, w_z[...]).astype(jnp.bfloat16).astype(jnp.float32)
    mixed_scr[:, query_width:] = (ssm_out * (gate_z * jax.nn.sigmoid(gate_z))).astype(jnp.bfloat16)

    own_rows = tokens // SIDE
    copies[8].wait()
    copies[9].wait()
    rows = jnp.concatenate(
        [
            mixed_scr[pl.ds(pl.multiple_of((rank ^ flip) * own_rows, own_rows), own_rows), :]
            for flip in (0, *DIRECT)
        ],
        axis=0,
    )
    parts = dot32(rows, w_out[...]).astype(jnp.bfloat16)
    for block, part_ref in enumerate(part_refs):
        part_ref[...] = parts[block * own_rows : (block + 1) * own_rows]
    decay_ref[...] = log_decay
    scaled_ref[...] = scaled_x
    b_ref[...] = b_part
    in_x_ref[...] = in_x
    in_bc_ref[...] = in_bc


def mixer(
    hidden, mixer_gain, w_query, w_kv, w_attn_out, prompt_kv, prompt_lengths, member, accepted, w_z, w_x, w_bc,
    w_dt, conv_x, conv_bc, ssm_rate, dt_bias, skip_d, prompt_state, prompt_conv_x, prompt_conv_bc, w_mamba_out,
):
    tokens, width = hidden.shape
    inner = w_x.shape[1]
    query_width = w_query.shape[1]
    bf16 = jnp.bfloat16
    state = prompt_state.reshape(PROMPTS, inner, STATE)
    small = [
        hidden, mixer_gain.reshape(-1, 128), w_dt.T, conv_x, conv_bc,
        prompt_conv_x.transpose(1, 0, 2), prompt_conv_bc.transpose(1, 0, 2),
    ]
    scalars = [member, accepted, prompt_lengths, ssm_rate, dt_bias, skip_d]
    whole = pl.BlockSpec(memory_space=pltpu.VMEM)
    outs = pl.pallas_call(
        mixer_kernel,
        out_shape=[
            *([jax.ShapeDtypeStruct((tokens // SIDE, width), bf16)] * SIDE),
            jax.ShapeDtypeStruct((tokens, 128), jnp.float32),
            jax.ShapeDtypeStruct((tokens, inner), jnp.float32),
            jax.ShapeDtypeStruct((tokens, STATE), bf16),
            jax.ShapeDtypeStruct((tokens, inner), bf16),
            jax.ShapeDtypeStruct((tokens, 2 * STATE), bf16),
        ],
        in_specs=[pl.BlockSpec(memory_space=pltpu.HBM)] * 22,
        out_specs=[whole] * (SIDE + 5),
        scratch_shapes=[
            *(pltpu.SMEM(a.shape, a.dtype) for a in scalars),
            *(pltpu.VMEM(a.shape, a.dtype) for a in small),
            pltpu.VMEM(w_query.shape, bf16),
            pltpu.VMEM(w_kv.shape[1:], bf16),
            pltpu.VMEM((PROMPTS, *prompt_kv.shape[2:]), bf16),
            pltpu.VMEM(w_x.shape, bf16),
            pltpu.VMEM(w_bc.shape, bf16),
            pltpu.VMEM(w_z.shape, bf16),
            pltpu.VMEM(state.shape, jnp.float32),
            pltpu.VMEM((query_width + inner, width), bf16),
            pltpu.VMEM((tokens, query_width + inner), bf16),
            pltpu.VMEM((tokens, 128), jnp.float32),
            pltpu.SemaphoreType.DMA((23,)),
        ],
        compiler_params=pltpu.CompilerParams(vmem_limit_bytes=59 << 20),
        cost_estimate=pl.CostEstimate(
            flops=3_000_000_000, bytes_accessed=20_000_000, transcendentals=1_000_000
        ),
        name="mixer",
    )(
        *scalars, *small, w_query, w_kv, prompt_kv, w_x, w_bc, w_z, state, w_attn_out, w_mamba_out
    )
    return outs[:SIDE], *keeper(member, accepted, *outs[SIDE:], *small[-2:], state)


def feed_kernel(count, both_ref, down_ref, _token, *refs):
    hidden = down_ref.shape[0]
    rows_refs, out_refs = refs[:count], refs[count:]
    joined = jnp.concatenate([ref[...] for ref in rows_refs], axis=0)
    pair = dot32(joined, both_ref[...])
    gate, up = pair[:, :hidden], pair[:, hidden:]
    active = (gate * jax.nn.sigmoid(gate) * up).astype(jnp.bfloat16)
    parts = dot32(active, down_ref[...]).astype(jnp.bfloat16)
    first = 0
    for out_ref in out_refs:
        out_ref[...] = parts[first : first + out_ref.shape[0]]
        first += out_ref.shape[0]


def feed(arrays, out_rows, w_both, w_down, token):
    rows, width = sum(a.shape[0] for a in arrays), arrays[0].shape[1]
    whole = pl.BlockSpec(memory_space=pltpu.VMEM)
    return pl.pallas_call(
        functools.partial(feed_kernel, len(arrays)),
        out_shape=[jax.ShapeDtypeStruct((r, width), jnp.bfloat16) for r in out_rows],
        in_specs=[whole] * 2
        + [pl.BlockSpec(memory_space=pl.ANY)]
        + [whole] * len(arrays),
        out_specs=[whole] * len(out_rows),
        compiler_params=pltpu.CompilerParams(vmem_limit_bytes=12 << 20),
        cost_estimate=pl.CostEstimate(
            flops=4 * rows * width * 2 * 3 * w_down.shape[0],
            bytes_accessed=2 * rows * width * 2 + 3 * w_down.size * 2,
            transcendentals=rows * w_down.shape[0],
        ),
        name="feed",
    )(w_both, w_down, token, *arrays)


def head_kernel(count, targets_ref, owners_ref, *refs):
    groups, lanes = targets_ref.shape
    rows_refs, head_ref, others, out_ref = refs[:count], refs[count], refs[count + 1 : -1], refs[-1]
    vocab = head_ref.shape[0]
    devices = out_ref.shape[0]
    base = lax.axis_index("req") * vocab
    ids = lax.broadcasted_iota(jnp.int32, (vocab, lanes), 0) + base
    device = lax.broadcasted_iota(jnp.int32, (devices, lanes), 0)
    source = lax.broadcasted_iota(jnp.int32, (3 * lanes, 128), 0)
    column = lax.broadcasted_iota(jnp.int32, (3 * lanes, 128), 1)
    place = (column == source // lanes * (2 * DRAFT) + source % (2 * DRAFT)).astype(jnp.bfloat16)
    packed = jnp.zeros((devices, 128), jnp.float32)
    for other in others:
        packed = packed + other[:, 0, :]
    for group in range(groups):
        members, first = [], 0
        for ref in rows_refs:
            if group * lanes <= first < (group + 1) * lanes:
                members.append(ref[...])
            first += ref.shape[0]
        joined = jnp.concatenate(members, axis=0)
        logits = dot32(head_ref[...], joined, NEXT_TO)
        wanted = targets_ref[group : group + 1, :]
        target = jnp.sum(jnp.where(ids == wanted, logits, 0.0), axis=0, keepdims=True)
        top = jnp.max(logits, axis=0, keepdims=True)
        total = jnp.sum(jnp.exp(logits - top), axis=0, keepdims=True)
        here = device == owners_ref[group : group + 1, :]
        rest = jnp.concatenate([jnp.where(here, stat, 0.0) for stat in (top, total, target)], axis=1)
        for _ in range(3):
            part = rest.astype(jnp.bfloat16)
            packed = packed + dot32(part, place)
            rest = rest - part.astype(jnp.float32)
    out_ref[:, 0, :] = packed


def head_stats(targets, owners, rows, head_weight, devices, others=()):
    whole = pl.BlockSpec(memory_space=pltpu.VMEM)
    return pl.pallas_call(
        functools.partial(head_kernel, len(rows)),
        out_shape=jax.ShapeDtypeStruct((devices, 1, 128), jnp.float32),
        in_specs=[whole] * (3 + len(rows) + len(others)),
        out_specs=whole,
        compiler_params=pltpu.CompilerParams(vmem_limit_bytes=20 << 20),
        cost_estimate=pl.CostEstimate(
            flops=1 * 2 * targets.size * head_weight.size,
            bytes_accessed=2 * targets.size * head_weight.shape[1] + 2 * head_weight.size,
            transcendentals=targets.size * head_weight.shape[0],
        ),
        name="head_stats",
    )(targets, owners, *rows, head_weight, *others)


def shards(
    hidden_in,
    mixer_gain,
    w_query,
    w_kv,
    w_attn_out,
    prompt_kv,
    prompt_lengths,
    member,
    accepted,
    w_z,
    w_x,
    w_bc,
    w_dt,
    conv_x,
    conv_bc,
    ssm_rate,
    dt_bias,
    skip_d,
    prompt_state,
    prompt_conv_x,
    prompt_conv_bc,
    w_mamba_out,
    mlp_gain,
    w_gate,
    w_up,
    w_down,
    final_gain,
    head_weight,
    draft_ids,
):
    row_reqs, draft_len, width = hidden_in.shape
    mdl_count = lax.axis_size("mdl")
    req_count = lax.axis_size("req")
    mdl_rank = lax.axis_index("mdl")
    req_rank = lax.axis_index("req")
    row_tokens = row_reqs * draft_len
    own_reqs = row_reqs // mdl_count
    own_tokens = own_reqs * draft_len
    flat_rows = hidden_in.reshape(row_tokens, width)
    local_inner = w_x.shape[1]
    parts, kept, own_bc = mixer(
        flat_rows, mixer_gain, w_query, w_kv, w_attn_out, prompt_kv, prompt_lengths, member, accepted, w_z, w_x, w_bc,
        w_dt, conv_x, conv_bc, ssm_rate, dt_bias, skip_d, prompt_state, prompt_conv_x, prompt_conv_bc, w_mamba_out,
    )
    came = [
        lax.ppermute(part, "mdl", [(z, z ^ flip) for z in range(SIDE)])
        for part, flip in zip(parts[1:], DIRECT, strict=True)
    ]
    mixed = sum((part.astype(jnp.float32) for part in came), parts[0].astype(jnp.float32))
    own_rows = lax.dynamic_slice_in_dim(flat_rows, mdl_rank * own_tokens, own_tokens, 0)
    after_mixer = (own_rows.astype(jnp.float32) + mixed).astype(jnp.bfloat16)
    prepared = rms_scale(after_mixer, mlp_gain).astype(jnp.bfloat16)
    w_both = jnp.concatenate([w_gate, w_up], axis=1)
    early, late = gather_rows(prepared)
    early = (early, swap_early(early))
    late = (late, [swap_core(part) for part in late])

    core = req_rank % CORES
    chip_x = req_rank // CORES % SIDE
    chip_y = req_rank // (CORES * SIDE)
    table = jnp.where(core == 0, jnp.asarray(block_table()[0]), jnp.asarray(block_table()[1]))
    owner = ((chip_y ^ table[:, 0]) * SIDE + (chip_x ^ table[:, 1])) * CORES + (core ^ table[:, 2])
    request = owner * row_reqs + mdl_rank * own_reqs + table[:, 3]
    next_ids = jnp.concatenate([draft_ids[:, 1:], draft_ids[:, :1]], axis=1)
    picked = (request[:, None] == jnp.arange(draft_ids.shape[0])[None, :]).astype(jnp.float32)
    targets = jnp.dot(picked, next_ids.astype(jnp.float32), precision=HIGHEST).astype(jnp.int32)
    targets = targets.reshape(4, 16 * draft_len)
    owners = jnp.broadcast_to(owner[:, None], (64, draft_len)).reshape(4, 16 * draft_len)

    half = 2 * own_tokens
    early_parts = [
        feed(rows, out_rows, w_both, w_down, mlp_gain)
        for rows, out_rows in zip(early, ([half] * 6, [2 * half] * 3), strict=True)
    ]
    late_parts = [
        feed(rows, out_rows, w_both, w_down, own_bc)
        for rows, out_rows in zip(late, ([half] * 2, [2 * half]), strict=True)
    ]
    summed = scatter_rows(early_parts, late_parts)
    tip = early_parts[0][0][:8, :128]
    kept, tip = lax.optimization_barrier((kept, tip))
    kept_out = lax.all_to_all(
        kept.reshape(mdl_count, own_reqs, local_inner + 16, STATE),
        "mdl",
        split_axis=0,
        concat_axis=0,
        tiled=True,
    )
    final_gain, kept_out, targets, owners = lax.optimization_barrier(
        (final_gain, kept_out, targets, owners)
    )
    after_feed = (after_mixer.astype(jnp.float32) + summed).astype(jnp.bfloat16)
    final_rows = rms_scale(after_feed, final_gain).astype(jnp.bfloat16)
    early, late = gather_rows(final_rows)
    early = early + swap_early(early)
    first_stats = head_stats(targets[:3], owners[:3], early, head_weight, req_count)
    late, first_stats = lax.optimization_barrier((late, first_stats))
    late = late + [swap_core(part) for part in late]
    stats = head_stats(targets[3:], owners[3:], late, head_weight, req_count, [first_stats])
    kept_state, kept_conv = unpack(kept_out, own_bc, stats, tip)
    kept_state = kept_state.reshape(own_reqs, -1, SSM_DIM, STATE)
    shared = lax.all_to_all(stats, "req", split_axis=0, concat_axis=0, tiled=True)
    tops, totals, hits = (
        shared[:, 0, kind * own_tokens : (kind + 1) * own_tokens] for kind in range(3)
    )
    top = jnp.max(tops, axis=0)
    total = jnp.sum(totals * jnp.exp(tops - top[None, :]), axis=0)
    log_total = top + jnp.log(total)
    position = jnp.arange(own_tokens) % draft_len
    verify_scores = jnp.where(
        position < draft_len - 1, jnp.sum(hits, axis=0) - log_total, top - log_total
    ).reshape(own_reqs, draft_len)
    return (
        after_feed.reshape(own_reqs, draft_len, width),
        verify_scores,
        kept_state,
        kept_conv,
    )


def solution(mesh):
    in_specs = (
        P("req", None, None),
        P(),
        P(None, "mdl"),
        P(),
        P("mdl", None),
        P("req", None, None, None),
        P("req"),
        P("req"),
        P("req"),
        P(None, "mdl"),
        P(None, "mdl"),
        P(),
        P(None, "mdl"),
        P(None, "mdl"),
        P(),
        P("mdl"),
        P("mdl"),
        P("mdl"),
        P("req", "mdl", None, None),
        P("req", None, "mdl"),
        P("req", None, None),
        P("mdl", None),
        P(),
        P(None, "req"),
        P(None, "req"),
        P("req", None),
        P(),
        P("req", None),
        P(),
    )
    out_specs = (
        P(("req", "mdl"), None, None),
        P(("req", "mdl"), None),
        P(("req", "mdl"), None, None, None),
        P(("req", "mdl"), None, None),
    )
    return jax.shard_map(shards, mesh=mesh, in_specs=in_specs, out_specs=out_specs, check_vma=False)
```

```python
import functools

import jax
import jax.numpy as jnp
import numpy as np
from jax import lax
from jax.experimental import pallas as pl
from jax.experimental.pallas import tpu as pltpu
from jax.sharding import PartitionSpec as P

Q_HEADS = 8
KV_HEADS = 2
HEAD_DIM = 128
SSM_DIM = 64
STATE = 256
CONV = 4
PROMPTS = 2
P_MAX = 1024
DRAFT = 16
SIDE = 4
CORES = 2

eps_norm = 1e-05
far_below = -1e30

DIRECT = (1, 3, 2)
EDGES = ((1, 3), (3, 1))


def device_at(y, x, core):
    return (y * SIDE + x) * CORES + core


def flip_pairs(ring, flip):
    pairs = []
    for y in range(SIDE):
        for x in range(SIDE):
            for core in range(CORES):
                on_x = ring == core
                target = device_at(y if on_x else y ^ flip, x ^ flip if on_x else x, core)
                pairs.append((device_at(y, x, core), target))
    return pairs


CORE_PAIRS = [(device, device ^ 1) for device in range(SIDE * SIDE * CORES)]


def hop(part, ring, flip):
    return lax.ppermute(part, "req", flip_pairs(ring, flip))


def swap_core(part):
    return lax.ppermute(part, "req", CORE_PAIRS)


def gather_rows(rows):
    came = [hop(rows, 0, flip) for flip in DIRECT]
    held = [jnp.concatenate([rows, came[0]], axis=0), jnp.concatenate(came[1:], axis=0)]
    near = [hop(held[s], 1, EDGES[s][0]) for s in range(2)]
    far = [hop(held[s], 1, EDGES[s][1]) for s in range(2)]
    last = [hop(near[s], 1, EDGES[s][1]) for s in range(2)]
    return held + near + far, last


def added(*parts):
    return sum(part.astype(jnp.float32) for part in parts).astype(jnp.bfloat16)


def stream(joined, s):
    rows = joined.shape[0] // 2
    return joined[s * rows : (s + 1) * rows]


def late_sum(late):
    came = swap_core(late[1][0])
    return [added(late[0][s], stream(came, s)) for s in range(2)]


def scatter_rows(early, late):
    last = [hop(late[s], 1, EDGES[s][1]) for s in range(2)]
    kept, near, far = (swap_core(part) for part in early[1])
    own = early[0]
    far = [hop(added(own[4 + s], stream(far, s)), 1, EDGES[s][1]) for s in range(2)]
    near = [hop(added(own[2 + s], stream(near, s), last[s]), 1, EDGES[s][0]) for s in range(2)]
    held = [added(own[s], stream(kept, s), far[s], near[s]) for s in range(2)]
    half = held[0].shape[0] // 2
    blocks = (held[0][half:], held[1][:half], held[1][half:])
    came = [hop(block, 0, flip) for block, flip in zip(blocks, DIRECT, strict=True)]
    total = held[0][:half].astype(jnp.float32)
    return sum((part.astype(jnp.float32) for part in came), total)


def swap_early(arrays):
    kept = [swap_core(part) for part in arrays[:2]]
    return kept + [swap_core(jnp.concatenate(arrays[k : k + 2], axis=0)) for k in (2, 4)]


def block_table():
    arrays = [(half, kind) for half in range(2) for kind in range(3)] + [(0, 3), (1, 3)]
    table = np.zeros((CORES, len(arrays), 2, 2, 2, 4), np.int32)
    for core, array, stream, block, request in np.ndindex(table.shape[:-1]):
        half, kind = arrays[array]
        first = ((0, 1), (3, 2))[stream][block]
        other = (0, *EDGES[stream], 2)[kind]
        y, x = (other, first) if core == half else (first, other)
        table[core, array, stream, block, request] = (y, x, half, request)
    return table.reshape(CORES, 64, 4)


def rms_scale(values, gain):
    widened = values.astype(jnp.float32)
    spread = jnp.mean(widened * widened, axis=-1, keepdims=True)
    return widened * lax.rsqrt(spread + eps_norm) * gain.astype(jnp.float32)


HIGHEST = lax.Precision.HIGHEST
NEXT_TO = (((1,), (1,)), ((), ()))


def dot32(left, right, dims=None):
    dims = dims or (((1,), (0,)), ((), ()))
    return lax.dot_general(left, right, dims, preferred_element_type=jnp.float32)


def exact_dot(left, right):
    return jnp.dot(left, right, precision=HIGHEST, preferred_element_type=jnp.float32)


def lane_spread(rows, lanes):
    return (
        lax.broadcasted_iota(jnp.int32, (rows, lanes), 0)
        == lax.broadcasted_iota(jnp.int32, (rows, lanes), 1) // SSM_DIM
    ).astype(jnp.float32)


def keeper_kernel(*refs):
    sources, (kept_ref, kept_bc_ref), held, sems = refs[:10], refs[10:12], refs[12:22], refs[22]
    copies = [
        pltpu.make_async_copy(source, target, sems.at[index])
        for index, (source, target) in enumerate(zip(sources, held, strict=True))
    ]
    for copy in copies:
        copy.start()
    for copy in copies:
        copy.wait()
    member_ref, accepted_ref, decay_ref, scaled_ref, b_ref, in_x_ref, in_bc_ref = held[:7]
    past_x_ref, past_bc_ref, state = held[7:]
    tokens, inner = scaled_ref.shape
    requests = tokens // DRAFT
    rank = lax.axis_index("mdl")

    row = lax.broadcasted_iota(jnp.int32, (tokens, 1), 0)
    time, request = row % DRAFT, row // DRAFT
    last = jnp.zeros((tokens, 1), jnp.int32)
    for r in range(requests):
        last = jnp.where(request == r, accepted_ref[r] - 1, last)
    spread_lanes = lane_spread(tokens, inner)
    log_decay, scaled_x, b_part = decay_ref[...], scaled_ref[...], b_ref[...]
    in_x, in_bc = in_x_ref[...], in_bc_ref[...]
    decay_x = exact_dot(log_decay, spread_lanes)
    other = lax.broadcasted_iota(jnp.int32, (tokens, tokens), 1)
    pick = (other == request * DRAFT + last).astype(jnp.float32)
    final_log = exact_dot(pick, log_decay)
    final_x = exact_dot(final_log, spread_lanes)
    carry_x = jnp.exp(jnp.where(time <= last, final_x - decay_x, far_below))
    carried_x = (scaled_x * carry_x).T.astype(jnp.bfloat16)
    shrink = jnp.exp(final_x).T
    for r in range(requests):
        b_here = jnp.where(request == r, b_part, jnp.zeros_like(b_part))
        kept = shrink[:, r * DRAFT : r * DRAFT + 1] * state[member_ref[r]] + dot32(
            carried_x, b_here
        )
        kept_ref[r, :inner, :] = kept.astype(jnp.bfloat16)

    def kept_rows(first_request, count, slots, series, past_of):
        at = lax.broadcasted_iota(jnp.int32, (count * slots, 1), 0)
        here, edge = at // slots, at % slots
        start = jnp.zeros((count * slots, 1), jnp.int32)
        owner = jnp.zeros((count * slots, 1), jnp.int32)
        for r in range(count):
            start = jnp.where(here == r, accepted_ref[first_request + r], start)
            owner = jnp.where(here == r, member_ref[first_request + r], owner)
        index = start + edge
        token = (here + first_request) * DRAFT + index - (CONV - 1)
        chosen = (lax.broadcasted_iota(jnp.int32, (count * slots, tokens), 1) == token) & (
            index >= CONV - 1
        )
        rows = dot32(chosen.astype(jnp.bfloat16), series)
        for p in range(PROMPTS):
            for j in range(CONV - 1):
                rows = jnp.where((owner == p) & (index == j), past_of(j, p), rows)
        return rows.astype(jnp.bfloat16)

    for lanes in range(2):
        cut = slice(lanes * STATE, min((lanes + 1) * STATE, inner))
        rows = kept_rows(
            0, requests, 8, in_x[:, cut], lambda j, p: past_x_ref[j, p : p + 1, cut].astype(jnp.float32)
        )
        for r in range(requests):
            kept_ref[r, inner + 8 * lanes : inner + 8 * (lanes + 1), : rows.shape[1]] = rows[
                r * 8 : (r + 1) * 8
            ]
    kept_ref[:, inner + 8 :, inner - STATE :] = jnp.zeros(
        (requests, 8, 2 * STATE - inner), jnp.bfloat16
    )
    kept_bc_ref[...] = kept_rows(
        rank * (requests // SIDE),
        requests // SIDE,
        8,
        in_bc,
        lambda j, p: past_bc_ref[j, p : p + 1, :].astype(jnp.float32),
    )


def keeper(member, accepted, log_decay, scaled_x, b_part, in_x, in_bc, past_x, past_bc, state):
    tokens, inner = scaled_x.shape
    requests = tokens // DRAFT
    operands = (member, accepted, log_decay, scaled_x, b_part, in_x, in_bc, past_x, past_bc, state)
    whole = pl.BlockSpec(memory_space=pltpu.VMEM)
    return pl.pallas_call(
        keeper_kernel,
        out_shape=[
            jax.ShapeDtypeStruct((requests, inner + 16, STATE), jnp.bfloat16),
            jax.ShapeDtypeStruct((requests // SIDE * 8, 2 * STATE), jnp.bfloat16),
        ],
        in_specs=[pl.BlockSpec(memory_space=pltpu.HBM)] * len(operands),
        out_specs=[whole] * 2,
        scratch_shapes=[
            *(pltpu.SMEM(a.shape, a.dtype) for a in operands[:2]),
            *(pltpu.VMEM(a.shape, a.dtype) for a in operands[2:]),
            pltpu.SemaphoreType.DMA((len(operands),)),
        ],
        compiler_params=pltpu.CompilerParams(vmem_limit_bytes=12 << 20),
        cost_estimate=pl.CostEstimate(
            flops=2_000_000_000, bytes_accessed=5_000_000, transcendentals=200_000
        ),
        name="keeper",
    )(*operands)


def unpack_kernel(kept_hbm, bc_ref, _stats, _tip, state_ref, conv_ref, kept_ref, sem):
    copy = pltpu.make_async_copy(kept_hbm, kept_ref, sem)
    copy.start()
    copy.wait()
    inner = kept_ref.shape[2] - 16
    for r in range(state_ref.shape[0]):
        for z in range(kept_ref.shape[0]):
            state_ref[r, z * inner : (z + 1) * inner, :] = kept_ref[z, r, :inner, :].astype(
                jnp.float32
            )
    for j in range(CONV - 1):
        rows = []
        for r in range(state_ref.shape[0]):
            pieces = []
            for z in range(kept_ref.shape[0]):
                tail = kept_ref[z, r, inner:, :].astype(jnp.float32)
                pieces += [tail[j : j + 1, :], tail[8 + j : 9 + j, : inner - STATE]]
            pieces.append(bc_ref[...].astype(jnp.float32)[r * 8 + j : r * 8 + j + 1, :])
            rows.append(jnp.concatenate(pieces, axis=1))
        conv_ref[j] = jnp.concatenate(rows, axis=0).astype(jnp.bfloat16)


def unpack(kept_out, own_bc, *tokens):
    sources, requests, rows, _ = kept_out.shape
    inner = rows - 16
    whole = pl.BlockSpec(memory_space=pltpu.VMEM)
    state, conv = pl.pallas_call(
        unpack_kernel,
        out_shape=[
            jax.ShapeDtypeStruct((requests, sources * inner, STATE), jnp.float32),
            jax.ShapeDtypeStruct((CONV - 1, requests, sources * inner + 2 * STATE), jnp.bfloat16),
        ],
        in_specs=[pl.BlockSpec(memory_space=pltpu.HBM), whole]
        + [pl.BlockSpec(memory_space=pl.ANY)] * len(tokens),
        out_specs=[whole] * 2,
        scratch_shapes=[pltpu.VMEM(kept_out.shape, kept_out.dtype), pltpu.SemaphoreType.DMA],
        compiler_params=pltpu.CompilerParams(vmem_limit_bytes=10 << 20),
        cost_estimate=pl.CostEstimate(flops=1_000_000, bytes_accessed=20_000_000, transcendentals=0),
        name="unpack",
    )(kept_out, own_bc, *tokens)
    return state, conv.transpose(1, 0, 2)


def mixer_kernel(*refs):
    sources, refs = refs[:22], refs[22:]
    part_refs = refs[:SIDE]
    decay_ref, scaled_ref, b_ref, in_x_ref, in_bc_ref = refs[SIDE : SIDE + 5]
    held, (mixed_scr, lanes_scr, sems) = refs[SIDE + 5 : -3], refs[-3:]
    member_ref, accepted_ref, lengths_ref, rate_ref, bias_ref, skip_ref = held[:6]
    hidden_ref, gain_ref, w_dt_ref, conv_x_ref, conv_bc_ref, past_x_ref, past_bc_ref = held[6:13]
    w_query, w_kv, prompt, w_x, w_bc, w_z, state, w_out = held[13:]
    tokens = hidden_ref.shape[0]
    requests = tokens // DRAFT
    inner = w_x.shape[1]
    heads = inner // SSM_DIM
    query_width = w_query.shape[1]
    rank = lax.axis_index("mdl")
    group = rank * (query_width // HEAD_DIM) // (Q_HEADS // KV_HEADS)
    query_hbm, kv_hbm, prompt_hbm, x_hbm, bc_hbm, z_hbm, state_hbm, attn_hbm, mamba_hbm = sources[13:]
    moves = [(source, target) for source, target in zip(sources[:13], held[:13], strict=True)]
    moves += [
        (query_hbm, w_query),
        (kv_hbm.at[group], w_kv),
        (prompt_hbm.at[0, group], prompt.at[0]),
        (prompt_hbm.at[1, group], prompt.at[1]),
        (x_hbm, w_x),
        (bc_hbm, w_bc),
        (z_hbm, w_z),
        (state_hbm, state),
        (attn_hbm, w_out.at[pl.ds(0, query_width), :]),
        (mamba_hbm, w_out.at[pl.ds(query_width, inner), :]),
    ]
    started = [
        pltpu.make_async_copy(source, target, sems.at[index])
        for index, (source, target) in enumerate(moves)
    ]
    for copy in started:
        copy.start()
    for copy in started[:13]:
        copy.wait()
    copies = started[13:]

    def head_row(ref):
        lane = lax.broadcasted_iota(jnp.int32, (1, heads), 1)
        values = jnp.zeros((1, heads), jnp.float32)
        for h in range(heads):
            values = jnp.where(lane == h, ref[h], values)
        return values

    row = lax.broadcasted_iota(jnp.int32, (tokens, 1), 0)
    time, request = row % DRAFT, row // DRAFT
    own_prompt = jnp.zeros((tokens, 1), jnp.int32)
    last = jnp.zeros((tokens, 1), jnp.int32)
    for r in range(requests):
        own_prompt = jnp.where(request == r, member_ref[r], own_prompt)
        last = jnp.where(request == r, accepted_ref[r] - 1, last)
    first_prompt = own_prompt == 0

    gain = jnp.concatenate(
        [gain_ref[j : j + 1, :].astype(jnp.float32) for j in range(gain_ref.shape[0])], axis=1
    )
    widened = hidden_ref[...].astype(jnp.float32)
    spread = jnp.mean(widened * widened, axis=-1, keepdims=True)
    normed = (
        widened * lax.rsqrt(spread + eps_norm) * gain
    ).astype(jnp.bfloat16)

    copies[0].wait()
    queries = dot32(normed, w_query[...]).astype(jnp.bfloat16)
    copies[1].wait()
    drafts = dot32(normed, w_kv[...]).astype(jnp.bfloat16)
    local_heads = query_width // HEAD_DIM
    query_rows = jnp.concatenate(
        [queries[:, h * HEAD_DIM : (h + 1) * HEAD_DIM] for h in range(local_heads)], axis=0
    )
    scale = HEAD_DIM**-0.5
    row_first = jnp.concatenate([own_prompt] * local_heads, axis=0) == 0
    draft_scores = dot32(query_rows, drafts[:, :HEAD_DIM], NEXT_TO) * scale
    same = (row // DRAFT == lax.broadcasted_iota(jnp.int32, (tokens, tokens), 1) // DRAFT) & (
        lax.broadcasted_iota(jnp.int32, (tokens, tokens), 1) <= row
    )
    draft_mask = jnp.concatenate([same] * local_heads, axis=0)
    draft_scores = jnp.where(draft_mask, draft_scores, far_below)
    copies[2].wait()
    copies[3].wait()
    scores = jnp.where(
        row_first,
        dot32(query_rows, prompt[0, :, :HEAD_DIM], NEXT_TO),
        dot32(query_rows, prompt[1, :, :HEAD_DIM], NEXT_TO),
    )
    length = jnp.where(row_first, lengths_ref[0], lengths_ref[1])
    position = lax.broadcasted_iota(jnp.int32, scores.shape, 1)
    scores = jnp.where(position < length, scores * scale, far_below)
    top = jnp.maximum(
        jnp.max(scores, axis=1, keepdims=True), jnp.max(draft_scores, axis=1, keepdims=True)
    )
    weights = jnp.exp(scores - top)
    draft_weights = jnp.exp(draft_scores - top)
    total = jnp.sum(weights, axis=1, keepdims=True) + jnp.sum(draft_weights, axis=1, keepdims=True)
    weighted = (
        dot32(jnp.where(row_first, weights, 0.0).astype(jnp.bfloat16), prompt[0, :, HEAD_DIM:])
        + dot32(jnp.where(row_first, 0.0, weights).astype(jnp.bfloat16), prompt[1, :, HEAD_DIM:])
        + dot32(draft_weights.astype(jnp.bfloat16), drafts[:, HEAD_DIM:])
    )
    attended = (weighted / total).astype(jnp.bfloat16)
    for h in range(local_heads):
        mixed_scr[:, h * HEAD_DIM : (h + 1) * HEAD_DIM] = attended[h * tokens : (h + 1) * tokens]

    def convolve_rows(series, past_ref, taps_ref):
        past = [
            jnp.where(
                first_prompt,
                past_ref[j, 0:1, :].astype(jnp.float32),
                past_ref[j, 1:2, :].astype(jnp.float32),
            )
            for j in range(CONV - 1)
        ]
        taps = taps_ref[...].astype(jnp.float32)
        summed = series * taps[CONV - 1 : CONV, :]
        for shift in range(1, CONV):
            window = pltpu.roll(series, shift, 0)
            for t in range(shift):
                window = jnp.where(time == t, past[CONV - 1 - shift + t], window)
            summed = summed + window * taps[CONV - 1 - shift : CONV - shift, :]
        return summed * jax.nn.sigmoid(summed)

    copies[4].wait()
    in_x = dot32(normed, w_x[...]).astype(jnp.bfloat16)
    heads_x = convolve_rows(in_x.astype(jnp.float32), past_x_ref, conv_x_ref)
    copies[5].wait()
    in_bc = dot32(normed, w_bc[...]).astype(jnp.bfloat16)
    conv_bcs = convolve_rows(in_bc.astype(jnp.float32), past_bc_ref, conv_bc_ref)
    b_part = conv_bcs[:, :STATE].astype(jnp.bfloat16)
    c_part = conv_bcs[:, STATE:].astype(jnp.bfloat16)

    def widen(values):
        lanes_scr[...] = jnp.zeros(lanes_scr.shape, jnp.float32)
        lanes_scr[:, :heads] = values
        return lanes_scr[...]

    spread_lanes = lane_spread(tokens, inner)
    dt_in = dot32(normed, w_dt_ref[...], NEXT_TO).astype(jnp.bfloat16).astype(jnp.float32) + head_row(bias_ref)
    step = jnp.maximum(dt_in, 0.0) + jnp.log1p(jnp.exp(-jnp.abs(dt_in)))
    log_decay = exact_dot(same.astype(jnp.float32), widen(-step * head_row(rate_ref)))
    step_x = exact_dot(widen(step), spread_lanes)
    skip_x = exact_dot(widen(jnp.broadcast_to(head_row(skip_ref), (tokens, heads))), spread_lanes)
    decay_x = exact_dot(log_decay, spread_lanes)
    turned = log_decay.T
    intersection = dot32(c_part, b_part, NEXT_TO)
    scaled_x = heads_x * step_x
    low = lax.broadcasted_iota(jnp.int32, (tokens, 2 * SSM_DIM), 1) < SSM_DIM
    groups = []
    for pair in range(heads // 2):
        mixing = []
        for h in (2 * pair, 2 * pair + 1):
            gaps = log_decay[:, h : h + 1] - turned[h : h + 1, :]
            mixing.append(
                (jnp.exp(jnp.where(same, gaps, far_below)) * intersection).astype(jnp.bfloat16)
            )
        lanes = scaled_x[:, pair * 2 * SSM_DIM : (pair + 1) * 2 * SSM_DIM]
        both = jnp.concatenate([jnp.where(low, lanes, 0.0), jnp.where(low, 0.0, lanes)], axis=0)
        groups.append(dot32(jnp.concatenate(mixing, axis=1), both.astype(jnp.bfloat16)))
    copies[7].wait()
    carried = jnp.where(
        first_prompt,
        dot32(c_part, state[0].astype(jnp.bfloat16), NEXT_TO),
        dot32(c_part, state[1].astype(jnp.bfloat16), NEXT_TO),
    )
    ssm_out = jnp.concatenate(groups, axis=1) + carried * jnp.exp(decay_x) + skip_x * heads_x
    copies[6].wait()
    gate_z = dot32(normed, w_z[...]).astype(jnp.bfloat16).astype(jnp.float32)
    mixed_scr[:, query_width:] = (ssm_out * (gate_z * jax.nn.sigmoid(gate_z))).astype(jnp.bfloat16)

    own_rows = tokens // SIDE
    copies[8].wait()
    copies[9].wait()
    rows = jnp.concatenate(
        [
            mixed_scr[pl.ds(pl.multiple_of((rank ^ flip) * own_rows, own_rows), own_rows), :]
            for flip in (0, *DIRECT)
        ],
        axis=0,
    )
    parts = dot32(rows, w_out[...]).astype(jnp.bfloat16)
    for block, part_ref in enumerate(part_refs):
        part_ref[...] = parts[block * own_rows : (block + 1) * own_rows]
    decay_ref[...] = log_decay
    scaled_ref[...] = scaled_x
    b_ref[...] = b_part
    in_x_ref[...] = in_x
    in_bc_ref[...] = in_bc


def mixer(
    hidden, mixer_gain, w_query, w_kv, w_attn_out, prompt_kv, prompt_lengths, member, accepted, w_z, w_x, w_bc,
    w_dt, conv_x, conv_bc, ssm_rate, dt_bias, skip_d, prompt_state, prompt_conv_x, prompt_conv_bc, w_mamba_out,
):
    tokens, width = hidden.shape
    inner = w_x.shape[1]
    query_width = w_query.shape[1]
    bf16 = jnp.bfloat16
    state = prompt_state.reshape(PROMPTS, inner, STATE)
    small = [
        hidden, mixer_gain.reshape(-1, 128), w_dt.T, conv_x, conv_bc,
        prompt_conv_x.transpose(1, 0, 2), prompt_conv_bc.transpose(1, 0, 2),
    ]
    scalars = [member, accepted, prompt_lengths, ssm_rate, dt_bias, skip_d]
    whole = pl.BlockSpec(memory_space=pltpu.VMEM)
    outs = pl.pallas_call(
        mixer_kernel,
        out_shape=[
            *([jax.ShapeDtypeStruct((tokens // SIDE, width), bf16)] * SIDE),
            jax.ShapeDtypeStruct((tokens, 128), jnp.float32),
            jax.ShapeDtypeStruct((tokens, inner), jnp.float32),
            jax.ShapeDtypeStruct((tokens, STATE), bf16),
            jax.ShapeDtypeStruct((tokens, inner), bf16),
            jax.ShapeDtypeStruct((tokens, 2 * STATE), bf16),
        ],
        in_specs=[pl.BlockSpec(memory_space=pltpu.HBM)] * 22,
        out_specs=[whole] * (SIDE + 5),
        scratch_shapes=[
            *(pltpu.SMEM(a.shape, a.dtype) for a in scalars),
            *(pltpu.VMEM(a.shape, a.dtype) for a in small),
            pltpu.VMEM(w_query.shape, bf16),
            pltpu.VMEM(w_kv.shape[1:], bf16),
            pltpu.VMEM((PROMPTS, *prompt_kv.shape[2:]), bf16),
            pltpu.VMEM(w_x.shape, bf16),
            pltpu.VMEM(w_bc.shape, bf16),
            pltpu.VMEM(w_z.shape, bf16),
            pltpu.VMEM(state.shape, jnp.float32),
            pltpu.VMEM((query_width + inner, width), bf16),
            pltpu.VMEM((tokens, query_width + inner), bf16),
            pltpu.VMEM((tokens, 128), jnp.float32),
            pltpu.SemaphoreType.DMA((23,)),
        ],
        compiler_params=pltpu.CompilerParams(vmem_limit_bytes=59 << 20),
        cost_estimate=pl.CostEstimate(
            flops=3_000_000_000, bytes_accessed=20_000_000, transcendentals=1_000_000
        ),
        name="mixer",
    )(
        *scalars, *small, w_query, w_kv, prompt_kv, w_x, w_bc, w_z, state, w_attn_out, w_mamba_out
    )
    return outs[:SIDE], *keeper(member, accepted, *outs[SIDE:], *small[-2:], state)


def feed_kernel(count, both_ref, down_ref, _token, *refs):
    hidden = down_ref.shape[0]
    rows_refs, out_refs = refs[:count], refs[count:]
    joined = jnp.concatenate([ref[...] for ref in rows_refs], axis=0)
    pair = dot32(joined, both_ref[...])
    gate, up = pair[:, :hidden], pair[:, hidden:]
    active = (gate * jax.nn.sigmoid(gate) * up).astype(jnp.bfloat16)
    parts = dot32(active, down_ref[...]).astype(jnp.bfloat16)
    first = 0
    for out_ref in out_refs:
        out_ref[...] = parts[first : first + out_ref.shape[0]]
        first += out_ref.shape[0]


def feed(arrays, out_rows, w_both, w_down, token):
    rows, width = sum(a.shape[0] for a in arrays), arrays[0].shape[1]
    whole = pl.BlockSpec(memory_space=pltpu.VMEM)
    return pl.pallas_call(
        functools.partial(feed_kernel, len(arrays)),
        out_shape=[jax.ShapeDtypeStruct((r, width), jnp.bfloat16) for r in out_rows],
        in_specs=[whole] * 2
        + [pl.BlockSpec(memory_space=pl.ANY)]
        + [whole] * len(arrays),
        out_specs=[whole] * len(out_rows),
        compiler_params=pltpu.CompilerParams(vmem_limit_bytes=12 << 20),
        cost_estimate=pl.CostEstimate(
            flops=4 * rows * width * 2 * 3 * w_down.shape[0],
            bytes_accessed=2 * rows * width * 2 + 3 * w_down.size * 2,
            transcendentals=rows * w_down.shape[0],
        ),
        name="feed",
    )(w_both, w_down, token, *arrays)


def head_kernel(count, targets_ref, owners_ref, *refs):
    groups, lanes = targets_ref.shape
    rows_refs, head_ref, others, out_ref = refs[:count], refs[count], refs[count + 1 : -1], refs[-1]
    vocab = head_ref.shape[0]
    devices = out_ref.shape[0]
    base = lax.axis_index("req") * vocab
    ids = lax.broadcasted_iota(jnp.int32, (vocab, lanes), 0) + base
    device = lax.broadcasted_iota(jnp.int32, (devices, lanes), 0)
    source = lax.broadcasted_iota(jnp.int32, (3 * lanes, 128), 0)
    column = lax.broadcasted_iota(jnp.int32, (3 * lanes, 128), 1)
    place = (column == source // lanes * (2 * DRAFT) + source % (2 * DRAFT)).astype(jnp.bfloat16)
    packed = jnp.zeros((devices, 128), jnp.float32)
    for other in others:
        packed = packed + other[:, 0, :]
    for group in range(groups):
        members, first = [], 0
        for ref in rows_refs:
            if group * lanes <= first < (group + 1) * lanes:
                members.append(ref[...])
            first += ref.shape[0]
        joined = jnp.concatenate(members, axis=0)
        logits = dot32(head_ref[...], joined, NEXT_TO)
        wanted = targets_ref[group : group + 1, :]
        target = jnp.sum(jnp.where(ids == wanted, logits, 0.0), axis=0, keepdims=True)
        top = jnp.max(logits, axis=0, keepdims=True)
        total = jnp.sum(jnp.exp(logits - top), axis=0, keepdims=True)
        here = device == owners_ref[group : group + 1, :]
        rest = jnp.concatenate([jnp.where(here, stat, 0.0) for stat in (top, total, target)], axis=1)
        for _ in range(3):
            part = rest.astype(jnp.bfloat16)
            packed = packed + dot32(part, place)
            rest = rest - part.astype(jnp.float32)
    out_ref[:, 0, :] = packed


def head_stats(targets, owners, rows, head_weight, devices, others=()):
    whole = pl.BlockSpec(memory_space=pltpu.VMEM)
    return pl.pallas_call(
        functools.partial(head_kernel, len(rows)),
        out_shape=jax.ShapeDtypeStruct((devices, 1, 128), jnp.float32),
        in_specs=[whole] * (3 + len(rows) + len(others)),
        out_specs=whole,
        compiler_params=pltpu.CompilerParams(vmem_limit_bytes=20 << 20),
        cost_estimate=pl.CostEstimate(
            flops=1 * 2 * targets.size * head_weight.size,
            bytes_accessed=2 * targets.size * head_weight.shape[1] + 2 * head_weight.size,
            transcendentals=targets.size * head_weight.shape[0],
        ),
        name="head_stats",
    )(targets, owners, *rows, head_weight, *others)


def shards(
    hidden_in,
    mixer_gain,
    w_query,
    w_kv,
    w_attn_out,
    prompt_kv,
    prompt_lengths,
    member,
    accepted,
    w_z,
    w_x,
    w_bc,
    w_dt,
    conv_x,
    conv_bc,
    ssm_rate,
    dt_bias,
    skip_d,
    prompt_state,
    prompt_conv_x,
    prompt_conv_bc,
    w_mamba_out,
    mlp_gain,
    w_gate,
    w_up,
    w_down,
    final_gain,
    head_weight,
    draft_ids,
):
    row_reqs, draft_len, width = hidden_in.shape
    mdl_count = lax.axis_size("mdl")
    req_count = lax.axis_size("req")
    mdl_rank = lax.axis_index("mdl")
    req_rank = lax.axis_index("req")
    row_tokens = row_reqs * draft_len
    own_reqs = row_reqs // mdl_count
    own_tokens = own_reqs * draft_len
    flat_rows = hidden_in.reshape(row_tokens, width)
    local_inner = w_x.shape[1]
    parts, kept, own_bc = mixer(
        flat_rows, mixer_gain, w_query, w_kv, w_attn_out, prompt_kv, prompt_lengths, member, accepted, w_z, w_x, w_bc,
        w_dt, conv_x, conv_bc, ssm_rate, dt_bias, skip_d, prompt_state, prompt_conv_x, prompt_conv_bc, w_mamba_out,
    )
    came = [
        lax.ppermute(part, "mdl", [(z, z ^ flip) for z in range(SIDE)])
        for part, flip in zip(parts[1:], DIRECT, strict=True)
    ]
    mixed = sum((part.astype(jnp.float32) for part in came), parts[0].astype(jnp.float32))
    own_rows = lax.dynamic_slice_in_dim(flat_rows, mdl_rank * own_tokens, own_tokens, 0)
    after_mixer = (own_rows.astype(jnp.float32) + mixed).astype(jnp.bfloat16)
    prepared = rms_scale(after_mixer, mlp_gain).astype(jnp.bfloat16)
    w_both = jnp.concatenate([w_gate, w_up], axis=1)
    early, late = gather_rows(prepared)
    early = (early, swap_early(early))
    late = (late, [swap_core(part) for part in late])

    core = req_rank % CORES
    chip_x = req_rank // CORES % SIDE
    chip_y = req_rank // (CORES * SIDE)
    table = jnp.where(core == 0, jnp.asarray(block_table()[0]), jnp.asarray(block_table()[1]))
    owner = ((chip_y ^ table[:, 0]) * SIDE + (chip_x ^ table[:, 1])) * CORES + (core ^ table[:, 2])
    request = owner * row_reqs + mdl_rank * own_reqs + table[:, 3]
    next_ids = jnp.concatenate([draft_ids[:, 1:], draft_ids[:, :1]], axis=1)
    picked = (request[:, None] == jnp.arange(draft_ids.shape[0])[None, :]).astype(jnp.float32)
    targets = jnp.dot(picked, next_ids.astype(jnp.float32), precision=HIGHEST).astype(jnp.int32)
    targets = targets.reshape(4, 16 * draft_len)
    owners = jnp.broadcast_to(owner[:, None], (64, draft_len)).reshape(4, 16 * draft_len)

    half = 2 * own_tokens
    late_parts = [
        feed(rows, out_rows, w_both, w_down, own_bc)
        for rows, out_rows in zip(late, ([half] * 2, [2 * half]), strict=True)
    ]
    late_parts = late_sum(late_parts)
    early_parts = [
        feed(rows, out_rows, w_both, w_down, late_parts[0])
        for rows, out_rows in zip(early, ([half] * 6, [2 * half] * 3), strict=True)
    ]
    summed = scatter_rows(early_parts, late_parts)
    tip = early_parts[0][0][:8, :128]
    kept, tip = lax.optimization_barrier((kept, tip))
    kept_out = lax.all_to_all(
        kept.reshape(mdl_count, own_reqs, local_inner + 16, STATE),
        "mdl",
        split_axis=0,
        concat_axis=0,
        tiled=True,
    )
    final_gain, targets, owners = lax.optimization_barrier((final_gain, targets, owners))
    after_feed = (after_mixer.astype(jnp.float32) + summed).astype(jnp.bfloat16)
    final_rows = rms_scale(after_feed, final_gain).astype(jnp.bfloat16)
    early, late = gather_rows(final_rows)
    early = early + swap_early(early)
    first_stats = head_stats(targets[:3], owners[:3], early, head_weight, req_count)
    late, first_stats = lax.optimization_barrier((late, first_stats))
    late = late + [swap_core(part) for part in late]
    stats = head_stats(targets[3:], owners[3:], late, head_weight, req_count, [first_stats])
    kept_state, kept_conv = unpack(kept_out, own_bc, stats, tip)
    kept_state = kept_state.reshape(own_reqs, -1, SSM_DIM, STATE)
    shared = lax.all_to_all(stats, "req", split_axis=0, concat_axis=0, tiled=True)
    tops, totals, hits = (
        shared[:, 0, kind * own_tokens : (kind + 1) * own_tokens] for kind in range(3)
    )
    top = jnp.max(tops, axis=0)
    total = jnp.sum(totals * jnp.exp(tops - top[None, :]), axis=0)
    log_total = top + jnp.log(total)
    position = jnp.arange(own_tokens) % draft_len
    verify_scores = jnp.where(
        position < draft_len - 1, jnp.sum(hits, axis=0) - log_total, top - log_total
    ).reshape(own_reqs, draft_len)
    return (
        after_feed.reshape(own_reqs, draft_len, width),
        verify_scores,
        kept_state,
        kept_conv,
    )


def solution(mesh):
    in_specs = (
        P("req", None, None),
        P(),
        P(None, "mdl"),
        P(),
        P("mdl", None),
        P("req", None, None, None),
        P("req"),
        P("req"),
        P("req"),
        P(None, "mdl"),
        P(None, "mdl"),
        P(),
        P(None, "mdl"),
        P(None, "mdl"),
        P(),
        P("mdl"),
        P("mdl"),
        P("mdl"),
        P("req", "mdl", None, None),
        P("req", None, "mdl"),
        P("req", None, None),
        P("mdl", None),
        P(),
        P(None, "req"),
        P(None, "req"),
        P("req", None),
        P(),
        P("req", None),
        P(),
    )
    out_specs = (
        P(("req", "mdl"), None, None),
        P(("req", "mdl"), None),
        P(("req", "mdl"), None, None, None),
        P(("req", "mdl"), None, None),
    )
    return jax.shard_map(shards, mesh=mesh, in_specs=in_specs, out_specs=out_specs, check_vma=False)
```

```python
import functools

import jax
import jax.numpy as jnp
import numpy as np
from jax import lax
from jax.experimental import pallas as pl
from jax.experimental.pallas import tpu as pltpu
from jax.sharding import PartitionSpec as P

Q_HEADS = 8
KV_HEADS = 2
HEAD_DIM = 128
SSM_DIM = 64
STATE = 256
CONV = 4
PROMPTS = 2
P_MAX = 1024
DRAFT = 16
SIDE = 4
CORES = 2

eps_norm = 1e-05
far_below = -1e30

DIRECT = (1, 3, 2)
EDGES = ((1, 3), (3, 1))


def device_at(y, x, core):
    return (y * SIDE + x) * CORES + core


def flip_pairs(ring, flip):
    pairs = []
    for y in range(SIDE):
        for x in range(SIDE):
            for core in range(CORES):
                on_x = ring == core
                target = device_at(y if on_x else y ^ flip, x ^ flip if on_x else x, core)
                pairs.append((device_at(y, x, core), target))
    return pairs


CORE_PAIRS = [(device, device ^ 1) for device in range(SIDE * SIDE * CORES)]


def hop(part, ring, flip):
    return lax.ppermute(part, "req", flip_pairs(ring, flip))


def swap_core(part):
    return lax.ppermute(part, "req", CORE_PAIRS)


def gather_rows(rows):
    came = [hop(rows, 0, flip) for flip in DIRECT]
    held = [jnp.concatenate([rows, came[0]], axis=0), jnp.concatenate(came[1:], axis=0)]
    near = [hop(held[s], 1, EDGES[s][0]) for s in range(2)]
    far = [hop(held[s], 1, EDGES[s][1]) for s in range(2)]
    last = [hop(near[s], 1, EDGES[s][1]) for s in range(2)]
    return held + near + far, last


def added(*parts):
    return sum(part.astype(jnp.float32) for part in parts).astype(jnp.bfloat16)


def stream(joined, s):
    rows = joined.shape[0] // 2
    return joined[s * rows : (s + 1) * rows]


def late_sum(late):
    came = swap_core(late[1][0])
    return [added(late[0][s], stream(came, s)) for s in range(2)]


def scatter_rows(early, late):
    last = [hop(late[s], 1, EDGES[s][1]) for s in range(2)]
    kept, near, far = (swap_core(part) for part in early[1])
    own = early[0]
    far = [hop(added(own[4 + s], stream(far, s)), 1, EDGES[s][1]) for s in range(2)]
    near = [hop(added(own[2 + s], stream(near, s), last[s]), 1, EDGES[s][0]) for s in range(2)]
    held = [added(own[s], stream(kept, s), far[s], near[s]) for s in range(2)]
    half = held[0].shape[0] // 2
    blocks = (held[0][half:], held[1][:half], held[1][half:])
    came = [hop(block, 0, flip) for block, flip in zip(blocks, DIRECT, strict=True)]
    total = held[0][:half].astype(jnp.float32)
    return sum((part.astype(jnp.float32) for part in came), total)


def swap_early(arrays):
    kept = [swap_core(part) for part in arrays[:2]]
    return kept + [swap_core(jnp.concatenate(arrays[k : k + 2], axis=0)) for k in (2, 4)]


def block_table():
    arrays = [(half, kind) for half in range(2) for kind in range(3)] + [(0, 3), (1, 3)]
    table = np.zeros((CORES, len(arrays), 2, 2, 2, 4), np.int32)
    for core, array, stream, block, request in np.ndindex(table.shape[:-1]):
        half, kind = arrays[array]
        first = ((0, 1), (3, 2))[stream][block]
        other = (0, *EDGES[stream], 2)[kind]
        y, x = (other, first) if core == half else (first, other)
        table[core, array, stream, block, request] = (y, x, half, request)
    return table.reshape(CORES, 64, 4)


def rms_scale(values, gain):
    widened = values.astype(jnp.float32)
    spread = jnp.mean(widened * widened, axis=-1, keepdims=True)
    return widened * lax.rsqrt(spread + eps_norm) * gain.astype(jnp.float32)


HIGHEST = lax.Precision.HIGHEST
NEXT_TO = (((1,), (1,)), ((), ()))


def dot32(left, right, dims=None):
    dims = dims or (((1,), (0,)), ((), ()))
    return lax.dot_general(left, right, dims, preferred_element_type=jnp.float32)


def exact_dot(left, right):
    return jnp.dot(left, right, precision=HIGHEST, preferred_element_type=jnp.float32)


def lane_spread(rows, lanes):
    return (
        lax.broadcasted_iota(jnp.int32, (rows, lanes), 0)
        == lax.broadcasted_iota(jnp.int32, (rows, lanes), 1) // SSM_DIM
    ).astype(jnp.float32)


def keeper_kernel(*refs):
    sources, (kept_ref, kept_bc_ref), held, sems = refs[:10], refs[10:12], refs[12:22], refs[22]
    copies = [
        pltpu.make_async_copy(source, target, sems.at[index])
        for index, (source, target) in enumerate(zip(sources, held, strict=True))
    ]
    for copy in copies:
        copy.start()
    for copy in copies:
        copy.wait()
    member_ref, accepted_ref, decay_ref, scaled_ref, b_ref, in_x_ref, in_bc_ref = held[:7]
    past_x_ref, past_bc_ref, state = held[7:]
    tokens, inner = scaled_ref.shape
    requests = tokens // DRAFT
    rank = lax.axis_index("mdl")

    row = lax.broadcasted_iota(jnp.int32, (tokens, 1), 0)
    time, request = row % DRAFT, row // DRAFT
    last = jnp.zeros((tokens, 1), jnp.int32)
    for r in range(requests):
        last = jnp.where(request == r, accepted_ref[r] - 1, last)
    spread_lanes = lane_spread(tokens, inner)
    log_decay, scaled_x, b_part = decay_ref[...], scaled_ref[...], b_ref[...]
    in_x, in_bc = in_x_ref[...], in_bc_ref[...]
    decay_x = exact_dot(log_decay, spread_lanes)
    other = lax.broadcasted_iota(jnp.int32, (tokens, tokens), 1)
    pick = (other == request * DRAFT + last).astype(jnp.float32)
    final_log = exact_dot(pick, log_decay)
    final_x = exact_dot(final_log, spread_lanes)
    carry_x = jnp.exp(jnp.where(time <= last, final_x - decay_x, far_below))
    carried_x = (scaled_x * carry_x).T.astype(jnp.bfloat16)
    shrink = jnp.exp(final_x).T
    for r in range(requests):
        b_here = jnp.where(request == r, b_part, jnp.zeros_like(b_part))
        kept = shrink[:, r * DRAFT : r * DRAFT + 1] * state[member_ref[r]] + dot32(
            carried_x, b_here
        )
        kept_ref[r, :inner, :] = kept.astype(jnp.bfloat16)

    def kept_rows(first_request, count, slots, series, past_of):
        at = lax.broadcasted_iota(jnp.int32, (count * slots, 1), 0)
        here, edge = at // slots, at % slots
        start = jnp.zeros((count * slots, 1), jnp.int32)
        owner = jnp.zeros((count * slots, 1), jnp.int32)
        for r in range(count):
            start = jnp.where(here == r, accepted_ref[first_request + r], start)
            owner = jnp.where(here == r, member_ref[first_request + r], owner)
        index = start + edge
        token = (here + first_request) * DRAFT + index - (CONV - 1)
        chosen = (lax.broadcasted_iota(jnp.int32, (count * slots, tokens), 1) == token) & (
            index >= CONV - 1
        )
        rows = dot32(chosen.astype(jnp.bfloat16), series)
        for p in range(PROMPTS):
            for j in range(CONV - 1):
                rows = jnp.where((owner == p) & (index == j), past_of(j, p), rows)
        return rows.astype(jnp.bfloat16)

    for lanes in range(2):
        cut = slice(lanes * STATE, min((lanes + 1) * STATE, inner))
        rows = kept_rows(
            0, requests, 8, in_x[:, cut], lambda j, p: past_x_ref[j, p : p + 1, cut].astype(jnp.float32)
        )
        for r in range(requests):
            kept_ref[r, inner + 8 * lanes : inner + 8 * (lanes + 1), : rows.shape[1]] = rows[
                r * 8 : (r + 1) * 8
            ]
    kept_ref[:, inner + 8 :, inner - STATE :] = jnp.zeros(
        (requests, 8, 2 * STATE - inner), jnp.bfloat16
    )
    kept_bc_ref[...] = kept_rows(
        rank * (requests // SIDE),
        requests // SIDE,
        8,
        in_bc,
        lambda j, p: past_bc_ref[j, p : p + 1, :].astype(jnp.float32),
    )


def keeper(member, accepted, log_decay, scaled_x, b_part, in_x, in_bc, past_x, past_bc, state):
    tokens, inner = scaled_x.shape
    requests = tokens // DRAFT
    operands = (member, accepted, log_decay, scaled_x, b_part, in_x, in_bc, past_x, past_bc, state)
    whole = pl.BlockSpec(memory_space=pltpu.VMEM)
    return pl.pallas_call(
        keeper_kernel,
        out_shape=[
            jax.ShapeDtypeStruct((requests, inner + 16, STATE), jnp.bfloat16),
            jax.ShapeDtypeStruct((requests // SIDE * 8, 2 * STATE), jnp.bfloat16),
        ],
        in_specs=[pl.BlockSpec(memory_space=pltpu.HBM)] * len(operands),
        out_specs=[whole] * 2,
        scratch_shapes=[
            *(pltpu.SMEM(a.shape, a.dtype) for a in operands[:2]),
            *(pltpu.VMEM(a.shape, a.dtype) for a in operands[2:]),
            pltpu.SemaphoreType.DMA((len(operands),)),
        ],
        compiler_params=pltpu.CompilerParams(vmem_limit_bytes=12 << 20),
        cost_estimate=pl.CostEstimate(
            flops=2_000_000_000, bytes_accessed=5_000_000, transcendentals=200_000
        ),
        name="keeper",
    )(*operands)


def unpack_kernel(kept_hbm, bc_ref, _stats, _tip, state_ref, conv_ref, kept_ref, sem):
    copy = pltpu.make_async_copy(kept_hbm, kept_ref, sem)
    copy.start()
    copy.wait()
    inner = kept_ref.shape[2] - 16
    for r in range(state_ref.shape[0]):
        for z in range(kept_ref.shape[0]):
            state_ref[r, z * inner : (z + 1) * inner, :] = kept_ref[z, r, :inner, :].astype(
                jnp.float32
            )
    for j in range(CONV - 1):
        rows = []
        for r in range(state_ref.shape[0]):
            pieces = []
            for z in range(kept_ref.shape[0]):
                tail = kept_ref[z, r, inner:, :].astype(jnp.float32)
                pieces += [tail[j : j + 1, :], tail[8 + j : 9 + j, : inner - STATE]]
            pieces.append(bc_ref[...].astype(jnp.float32)[r * 8 + j : r * 8 + j + 1, :])
            rows.append(jnp.concatenate(pieces, axis=1))
        conv_ref[j] = jnp.concatenate(rows, axis=0).astype(jnp.bfloat16)


def unpack(kept_out, own_bc, *tokens):
    sources, requests, rows, _ = kept_out.shape
    inner = rows - 16
    whole = pl.BlockSpec(memory_space=pltpu.VMEM)
    state, conv = pl.pallas_call(
        unpack_kernel,
        out_shape=[
            jax.ShapeDtypeStruct((requests, sources * inner, STATE), jnp.float32),
            jax.ShapeDtypeStruct((CONV - 1, requests, sources * inner + 2 * STATE), jnp.bfloat16),
        ],
        in_specs=[pl.BlockSpec(memory_space=pltpu.HBM), whole]
        + [pl.BlockSpec(memory_space=pl.ANY)] * len(tokens),
        out_specs=[whole] * 2,
        scratch_shapes=[pltpu.VMEM(kept_out.shape, kept_out.dtype), pltpu.SemaphoreType.DMA],
        compiler_params=pltpu.CompilerParams(vmem_limit_bytes=10 << 20),
        cost_estimate=pl.CostEstimate(flops=1_000_000, bytes_accessed=20_000_000, transcendentals=0),
        name="unpack",
    )(kept_out, own_bc, *tokens)
    return state, conv.transpose(1, 0, 2)


def mixer_kernel(*refs):
    sources, refs = refs[:22], refs[22:]
    part_refs = refs[:SIDE]
    decay_ref, scaled_ref, b_ref, in_x_ref, in_bc_ref = refs[SIDE : SIDE + 5]
    held, (mixed_scr, lanes_scr, sems) = refs[SIDE + 5 : -3], refs[-3:]
    member_ref, accepted_ref, lengths_ref, rate_ref, bias_ref, skip_ref = held[:6]
    hidden_ref, gain_ref, w_dt_ref, conv_x_ref, conv_bc_ref, past_x_ref, past_bc_ref = held[6:13]
    w_query, w_kv, prompt, w_x, w_bc, w_z, state, w_out = held[13:]
    tokens = hidden_ref.shape[0]
    requests = tokens // DRAFT
    inner = w_x.shape[1]
    heads = inner // SSM_DIM
    query_width = w_query.shape[1]
    rank = lax.axis_index("mdl")
    group = rank * (query_width // HEAD_DIM) // (Q_HEADS // KV_HEADS)
    query_hbm, kv_hbm, prompt_hbm, x_hbm, bc_hbm, z_hbm, state_hbm, attn_hbm, mamba_hbm = sources[13:]
    moves = [(source, target) for source, target in zip(sources[:13], held[:13], strict=True)]
    moves += [
        (query_hbm, w_query),
        (kv_hbm.at[group], w_kv),
        (prompt_hbm.at[0, group], prompt.at[0]),
        (prompt_hbm.at[1, group], prompt.at[1]),
        (x_hbm, w_x),
        (bc_hbm, w_bc),
        (z_hbm, w_z),
        (state_hbm, state),
        (attn_hbm, w_out.at[pl.ds(0, query_width), :]),
        (mamba_hbm, w_out.at[pl.ds(query_width, inner), :]),
    ]
    started = [
        pltpu.make_async_copy(source, target, sems.at[index])
        for index, (source, target) in enumerate(moves)
    ]
    for copy in started:
        copy.start()
    for copy in started[:13]:
        copy.wait()
    copies = started[13:]

    def head_row(ref):
        lane = lax.broadcasted_iota(jnp.int32, (1, heads), 1)
        values = jnp.zeros((1, heads), jnp.float32)
        for h in range(heads):
            values = jnp.where(lane == h, ref[h], values)
        return values

    row = lax.broadcasted_iota(jnp.int32, (tokens, 1), 0)
    time, request = row % DRAFT, row // DRAFT
    own_prompt = jnp.zeros((tokens, 1), jnp.int32)
    last = jnp.zeros((tokens, 1), jnp.int32)
    for r in range(requests):
        own_prompt = jnp.where(request == r, member_ref[r], own_prompt)
        last = jnp.where(request == r, accepted_ref[r] - 1, last)
    first_prompt = own_prompt == 0

    gain = jnp.concatenate(
        [gain_ref[j : j + 1, :].astype(jnp.float32) for j in range(gain_ref.shape[0])], axis=1
    )
    widened = hidden_ref[...].astype(jnp.float32)
    spread = jnp.mean(widened * widened, axis=-1, keepdims=True)
    normed = (
        widened * lax.rsqrt(spread + eps_norm) * gain
    ).astype(jnp.bfloat16)

    copies[0].wait()
    queries = dot32(normed, w_query[...]).astype(jnp.bfloat16)
    copies[1].wait()
    drafts = dot32(normed, w_kv[...]).astype(jnp.bfloat16)
    local_heads = query_width // HEAD_DIM
    query_rows = jnp.concatenate(
        [queries[:, h * HEAD_DIM : (h + 1) * HEAD_DIM] for h in range(local_heads)], axis=0
    )
    scale = HEAD_DIM**-0.5
    row_first = jnp.concatenate([own_prompt] * local_heads, axis=0) == 0
    draft_scores = dot32(query_rows, drafts[:, :HEAD_DIM], NEXT_TO) * scale
    same = (row // DRAFT == lax.broadcasted_iota(jnp.int32, (tokens, tokens), 1) // DRAFT) & (
        lax.broadcasted_iota(jnp.int32, (tokens, tokens), 1) <= row
    )
    draft_mask = jnp.concatenate([same] * local_heads, axis=0)
    draft_scores = jnp.where(draft_mask, draft_scores, far_below)
    copies[2].wait()
    copies[3].wait()
    scores = jnp.where(
        row_first,
        dot32(query_rows, prompt[0, :, :HEAD_DIM], NEXT_TO),
        dot32(query_rows, prompt[1, :, :HEAD_DIM], NEXT_TO),
    )
    length = jnp.where(row_first, lengths_ref[0], lengths_ref[1])
    position = lax.broadcasted_iota(jnp.int32, scores.shape, 1)
    scores = jnp.where(position < length, scores * scale, far_below)
    top = jnp.maximum(
        jnp.max(scores, axis=1, keepdims=True), jnp.max(draft_scores, axis=1, keepdims=True)
    )
    weights = jnp.exp(scores - top)
    draft_weights = jnp.exp(draft_scores - top)
    total = jnp.sum(weights, axis=1, keepdims=True) + jnp.sum(draft_weights, axis=1, keepdims=True)
    weighted = (
        dot32(jnp.where(row_first, weights, 0.0).astype(jnp.bfloat16), prompt[0, :, HEAD_DIM:])
        + dot32(jnp.where(row_first, 0.0, weights).astype(jnp.bfloat16), prompt[1, :, HEAD_DIM:])
        + dot32(draft_weights.astype(jnp.bfloat16), drafts[:, HEAD_DIM:])
    )
    attended = (weighted / total).astype(jnp.bfloat16)
    for h in range(local_heads):
        mixed_scr[:, h * HEAD_DIM : (h + 1) * HEAD_DIM] = attended[h * tokens : (h + 1) * tokens]

    def convolve_rows(series, past_ref, taps_ref):
        past = [
            jnp.where(
                first_prompt,
                past_ref[j, 0:1, :].astype(jnp.float32),
                past_ref[j, 1:2, :].astype(jnp.float32),
            )
            for j in range(CONV - 1)
        ]
        taps = taps_ref[...].astype(jnp.float32)
        summed = series * taps[CONV - 1 : CONV, :]
        for shift in range(1, CONV):
            window = pltpu.roll(series, shift, 0)
            for t in range(shift):
                window = jnp.where(time == t, past[CONV - 1 - shift + t], window)
            summed = summed + window * taps[CONV - 1 - shift : CONV - shift, :]
        return summed * jax.nn.sigmoid(summed)

    copies[4].wait()
    in_x = dot32(normed, w_x[...]).astype(jnp.bfloat16)
    heads_x = convolve_rows(in_x.astype(jnp.float32), past_x_ref, conv_x_ref)
    copies[5].wait()
    in_bc = dot32(normed, w_bc[...]).astype(jnp.bfloat16)
    conv_bcs = convolve_rows(in_bc.astype(jnp.float32), past_bc_ref, conv_bc_ref)
    b_part = conv_bcs[:, :STATE].astype(jnp.bfloat16)
    c_part = conv_bcs[:, STATE:].astype(jnp.bfloat16)

    def widen(values):
        lanes_scr[...] = jnp.zeros(lanes_scr.shape, jnp.float32)
        lanes_scr[:, :heads] = values
        return lanes_scr[...]

    spread_lanes = lane_spread(tokens, inner)
    dt_in = dot32(normed, w_dt_ref[...], NEXT_TO).astype(jnp.bfloat16).astype(jnp.float32) + head_row(bias_ref)
    step = jnp.maximum(dt_in, 0.0) + jnp.log1p(jnp.exp(-jnp.abs(dt_in)))
    log_decay = exact_dot(same.astype(jnp.float32), widen(-step * head_row(rate_ref)))
    step_x = exact_dot(widen(step), spread_lanes)
    skip_x = exact_dot(widen(jnp.broadcast_to(head_row(skip_ref), (tokens, heads))), spread_lanes)
    decay_x = exact_dot(log_decay, spread_lanes)
    turned = log_decay.T
    intersection = dot32(c_part, b_part, NEXT_TO)
    scaled_x = heads_x * step_x
    low = lax.broadcasted_iota(jnp.int32, (tokens, 2 * SSM_DIM), 1) < SSM_DIM
    groups = []
    for pair in range(heads // 2):
        mixing = []
        for h in (2 * pair, 2 * pair + 1):
            gaps = log_decay[:, h : h + 1] - turned[h : h + 1, :]
            mixing.append(
                (jnp.exp(jnp.where(same, gaps, far_below)) * intersection).astype(jnp.bfloat16)
            )
        lanes = scaled_x[:, pair * 2 * SSM_DIM : (pair + 1) * 2 * SSM_DIM]
        both = jnp.concatenate([jnp.where(low, lanes, 0.0), jnp.where(low, 0.0, lanes)], axis=0)
        groups.append(dot32(jnp.concatenate(mixing, axis=1), both.astype(jnp.bfloat16)))
    copies[7].wait()
    carried = jnp.where(
        first_prompt,
        dot32(c_part, state[0].astype(jnp.bfloat16), NEXT_TO),
        dot32(c_part, state[1].astype(jnp.bfloat16), NEXT_TO),
    )
    ssm_out = jnp.concatenate(groups, axis=1) + carried * jnp.exp(decay_x) + skip_x * heads_x
    copies[6].wait()
    gate_z = dot32(normed, w_z[...]).astype(jnp.bfloat16).astype(jnp.float32)
    mixed_scr[:, query_width:] = (ssm_out * (gate_z * jax.nn.sigmoid(gate_z))).astype(jnp.bfloat16)

    own_rows = tokens // SIDE
    copies[8].wait()
    copies[9].wait()
    rows = jnp.concatenate(
        [
            mixed_scr[pl.ds(pl.multiple_of((rank ^ flip) * own_rows, own_rows), own_rows), :]
            for flip in (0, *DIRECT)
        ],
        axis=0,
    )
    parts = dot32(rows, w_out[...]).astype(jnp.bfloat16)
    for block, part_ref in enumerate(part_refs):
        part_ref[...] = parts[block * own_rows : (block + 1) * own_rows]
    decay_ref[...] = log_decay
    scaled_ref[...] = scaled_x
    b_ref[...] = b_part
    in_x_ref[...] = in_x
    in_bc_ref[...] = in_bc


def mixer(
    hidden, mixer_gain, w_query, w_kv, w_attn_out, prompt_kv, prompt_lengths, member, accepted, w_z, w_x, w_bc,
    w_dt, conv_x, conv_bc, ssm_rate, dt_bias, skip_d, prompt_state, prompt_conv_x, prompt_conv_bc, w_mamba_out,
):
    tokens, width = hidden.shape
    inner = w_x.shape[1]
    query_width = w_query.shape[1]
    bf16 = jnp.bfloat16
    state = prompt_state.reshape(PROMPTS, inner, STATE)
    small = [
        hidden, mixer_gain.reshape(-1, 128), w_dt.T, conv_x, conv_bc,
        prompt_conv_x.transpose(1, 0, 2), prompt_conv_bc.transpose(1, 0, 2),
    ]
    scalars = [member, accepted, prompt_lengths, ssm_rate, dt_bias, skip_d]
    whole = pl.BlockSpec(memory_space=pltpu.VMEM)
    outs = pl.pallas_call(
        mixer_kernel,
        out_shape=[
            *([jax.ShapeDtypeStruct((tokens // SIDE, width), bf16)] * SIDE),
            jax.ShapeDtypeStruct((tokens, 128), jnp.float32),
            jax.ShapeDtypeStruct((tokens, inner), jnp.float32),
            jax.ShapeDtypeStruct((tokens, STATE), bf16),
            jax.ShapeDtypeStruct((tokens, inner), bf16),
            jax.ShapeDtypeStruct((tokens, 2 * STATE), bf16),
        ],
        in_specs=[pl.BlockSpec(memory_space=pltpu.HBM)] * 22,
        out_specs=[whole] * (SIDE + 5),
        scratch_shapes=[
            *(pltpu.SMEM(a.shape, a.dtype) for a in scalars),
            *(pltpu.VMEM(a.shape, a.dtype) for a in small),
            pltpu.VMEM(w_query.shape, bf16),
            pltpu.VMEM(w_kv.shape[1:], bf16),
            pltpu.VMEM((PROMPTS, *prompt_kv.shape[2:]), bf16),
            pltpu.VMEM(w_x.shape, bf16),
            pltpu.VMEM(w_bc.shape, bf16),
            pltpu.VMEM(w_z.shape, bf16),
            pltpu.VMEM(state.shape, jnp.float32),
            pltpu.VMEM((query_width + inner, width), bf16),
            pltpu.VMEM((tokens, query_width + inner), bf16),
            pltpu.VMEM((tokens, 128), jnp.float32),
            pltpu.SemaphoreType.DMA((23,)),
        ],
        compiler_params=pltpu.CompilerParams(vmem_limit_bytes=59 << 20),
        cost_estimate=pl.CostEstimate(
            flops=3_000_000_000, bytes_accessed=20_000_000, transcendentals=1_000_000
        ),
        name="mixer",
    )(
        *scalars, *small, w_query, w_kv, prompt_kv, w_x, w_bc, w_z, state, w_attn_out, w_mamba_out
    )
    return outs[:SIDE], *keeper(member, accepted, *outs[SIDE:], *small[-2:], state)


def feed_kernel(count, both_ref, down_ref, _token, *refs):
    hidden = down_ref.shape[0]
    rows_refs, out_refs = refs[:count], refs[count:]
    joined = jnp.concatenate([ref[...] for ref in rows_refs], axis=0)
    pair = dot32(joined, both_ref[...])
    gate, up = pair[:, :hidden], pair[:, hidden:]
    active = (gate * jax.nn.sigmoid(gate) * up).astype(jnp.bfloat16)
    parts = dot32(active, down_ref[...]).astype(jnp.bfloat16)
    first = 0
    for out_ref in out_refs:
        out_ref[...] = parts[first : first + out_ref.shape[0]]
        first += out_ref.shape[0]


def feed(arrays, out_rows, w_both, w_down, token):
    rows, width = sum(a.shape[0] for a in arrays), arrays[0].shape[1]
    whole = pl.BlockSpec(memory_space=pltpu.VMEM)
    return pl.pallas_call(
        functools.partial(feed_kernel, len(arrays)),
        out_shape=[jax.ShapeDtypeStruct((r, width), jnp.bfloat16) for r in out_rows],
        in_specs=[whole] * 2
        + [pl.BlockSpec(memory_space=pl.ANY)]
        + [whole] * len(arrays),
        out_specs=[whole] * len(out_rows),
        compiler_params=pltpu.CompilerParams(vmem_limit_bytes=12 << 20),
        cost_estimate=pl.CostEstimate(
            flops=4 * rows * width * 2 * 3 * w_down.shape[0],
            bytes_accessed=2 * rows * width * 2 + 3 * w_down.size * 2,
            transcendentals=rows * w_down.shape[0],
        ),
        name="feed",
    )(w_both, w_down, token, *arrays)


def head_kernel(count, targets_ref, owners_ref, *refs):
    groups, lanes = targets_ref.shape
    rows_refs, head_ref, others, out_ref = refs[:count], refs[count], refs[count + 1 : -1], refs[-1]
    vocab = head_ref.shape[0]
    devices = out_ref.shape[0]
    base = lax.axis_index("req") * vocab
    ids = lax.broadcasted_iota(jnp.int32, (vocab, lanes), 0) + base
    device = lax.broadcasted_iota(jnp.int32, (devices, lanes), 0)
    source = lax.broadcasted_iota(jnp.int32, (3 * lanes, 128), 0)
    column = lax.broadcasted_iota(jnp.int32, (3 * lanes, 128), 1)
    place = (column == source // lanes * (2 * DRAFT) + source % (2 * DRAFT)).astype(jnp.bfloat16)
    packed = jnp.zeros((devices, 128), jnp.float32)
    for other in others:
        packed = packed + other[:, 0, :]
    for group in range(groups):
        members, first = [], 0
        for ref in rows_refs:
            if group * lanes <= first < (group + 1) * lanes:
                members.append(ref[...])
            first += ref.shape[0]
        joined = jnp.concatenate(members, axis=0)
        logits = dot32(head_ref[...], joined, NEXT_TO)
        wanted = targets_ref[group : group + 1, :]
        target = jnp.sum(jnp.where(ids == wanted, logits, 0.0), axis=0, keepdims=True)
        top = jnp.max(logits, axis=0, keepdims=True)
        total = jnp.sum(jnp.exp(logits - top), axis=0, keepdims=True)
        here = device == owners_ref[group : group + 1, :]
        rest = jnp.concatenate([jnp.where(here, stat, 0.0) for stat in (top, total, target)], axis=1)
        for _ in range(3):
            part = rest.astype(jnp.bfloat16)
            packed = packed + dot32(part, place)
            rest = rest - part.astype(jnp.float32)
    out_ref[:, 0, :] = packed


def head_stats(targets, owners, rows, head_weight, devices, others=()):
    whole = pl.BlockSpec(memory_space=pltpu.VMEM)
    return pl.pallas_call(
        functools.partial(head_kernel, len(rows)),
        out_shape=jax.ShapeDtypeStruct((devices, 1, 128), jnp.float32),
        in_specs=[whole] * (3 + len(rows) + len(others)),
        out_specs=whole,
        compiler_params=pltpu.CompilerParams(vmem_limit_bytes=20 << 20),
        cost_estimate=pl.CostEstimate(
            flops=1 * 2 * targets.size * head_weight.size,
            bytes_accessed=2 * targets.size * head_weight.shape[1] + 2 * head_weight.size,
            transcendentals=targets.size * head_weight.shape[0],
        ),
        name="head_stats",
    )(targets, owners, *rows, head_weight, *others)


def shards(
    hidden_in,
    mixer_gain,
    w_query,
    w_kv,
    w_attn_out,
    prompt_kv,
    prompt_lengths,
    member,
    accepted,
    w_z,
    w_x,
    w_bc,
    w_dt,
    conv_x,
    conv_bc,
    ssm_rate,
    dt_bias,
    skip_d,
    prompt_state,
    prompt_conv_x,
    prompt_conv_bc,
    w_mamba_out,
    mlp_gain,
    w_gate,
    w_up,
    w_down,
    final_gain,
    head_weight,
    draft_ids,
):
    row_reqs, draft_len, width = hidden_in.shape
    mdl_count = lax.axis_size("mdl")
    req_count = lax.axis_size("req")
    mdl_rank = lax.axis_index("mdl")
    req_rank = lax.axis_index("req")
    row_tokens = row_reqs * draft_len
    own_reqs = row_reqs // mdl_count
    own_tokens = own_reqs * draft_len
    flat_rows = hidden_in.reshape(row_tokens, width)
    local_inner = w_x.shape[1]
    parts, kept, own_bc = mixer(
        flat_rows, mixer_gain, w_query, w_kv, w_attn_out, prompt_kv, prompt_lengths, member, accepted, w_z, w_x, w_bc,
        w_dt, conv_x, conv_bc, ssm_rate, dt_bias, skip_d, prompt_state, prompt_conv_x, prompt_conv_bc, w_mamba_out,
    )
    came = [
        lax.ppermute(part, "mdl", [(z, z ^ flip) for z in range(SIDE)])
        for part, flip in zip(parts[1:], DIRECT, strict=True)
    ]
    mixed = sum((part.astype(jnp.float32) for part in came), parts[0].astype(jnp.float32))
    own_rows = lax.dynamic_slice_in_dim(flat_rows, mdl_rank * own_tokens, own_tokens, 0)
    after_mixer = (own_rows.astype(jnp.float32) + mixed).astype(jnp.bfloat16)
    prepared = rms_scale(after_mixer, mlp_gain).astype(jnp.bfloat16)
    w_both = jnp.concatenate([w_gate, w_up], axis=1)
    early, late = gather_rows(prepared)
    early = (early, swap_early(early))
    late, own_bc = lax.optimization_barrier((late, own_bc))
    late = (late, [swap_core(part) for part in late])

    core = req_rank % CORES
    chip_x = req_rank // CORES % SIDE
    chip_y = req_rank // (CORES * SIDE)
    table = jnp.where(core == 0, jnp.asarray(block_table()[0]), jnp.asarray(block_table()[1]))
    owner = ((chip_y ^ table[:, 0]) * SIDE + (chip_x ^ table[:, 1])) * CORES + (core ^ table[:, 2])
    request = owner * row_reqs + mdl_rank * own_reqs + table[:, 3]
    next_ids = jnp.concatenate([draft_ids[:, 1:], draft_ids[:, :1]], axis=1)
    picked = (request[:, None] == jnp.arange(draft_ids.shape[0])[None, :]).astype(jnp.float32)
    targets = jnp.dot(picked, next_ids.astype(jnp.float32), precision=HIGHEST).astype(jnp.int32)
    targets = targets.reshape(1, 64 * draft_len)
    owners = jnp.broadcast_to(owner[:, None], (64, draft_len)).reshape(1, 64 * draft_len)

    half = 2 * own_tokens
    late_parts = [
        feed(rows, out_rows, w_both, w_down, own_bc)
        for rows, out_rows in zip(late, ([half] * 2, [2 * half]), strict=True)
    ]
    late_parts = late_sum(late_parts)
    early_parts = [
        feed(rows, out_rows, w_both, w_down, late_parts[0])
        for rows, out_rows in zip(early, ([half] * 6, [2 * half] * 3), strict=True)
    ]
    summed = scatter_rows(early_parts, late_parts)
    tip = early_parts[0][0][:8, :128]
    kept, tip = lax.optimization_barrier((kept, tip))
    kept_out = lax.all_to_all(
        kept.reshape(mdl_count, own_reqs, local_inner + 16, STATE),
        "mdl",
        split_axis=0,
        concat_axis=0,
        tiled=True,
    )
    final_gain, targets, owners = lax.optimization_barrier((final_gain, targets, owners))
    after_feed = (after_mixer.astype(jnp.float32) + summed).astype(jnp.bfloat16)
    final_rows = rms_scale(after_feed, final_gain).astype(jnp.bfloat16)
    early, late = gather_rows(final_rows)
    sibling = swap_early(early)
    most = 6 * half
    first = head_stats(targets[:, :most], owners[:, :most], early, head_weight, req_count)
    second = head_stats(
        targets[:, most : 2 * most], owners[:, most : 2 * most], sibling, head_weight, req_count
    )
    late, first, second = lax.optimization_barrier((late, first, second))
    late = late + [swap_core(part) for part in late]
    stats = head_stats(
        targets[:, 2 * most :], owners[:, 2 * most :], late, head_weight, req_count, [first, second]
    )
    kept_state, kept_conv = unpack(kept_out, own_bc, stats, tip)
    kept_state = kept_state.reshape(own_reqs, -1, SSM_DIM, STATE)
    shared = lax.all_to_all(stats, "req", split_axis=0, concat_axis=0, tiled=True)
    tops, totals, hits = (
        shared[:, 0, kind * own_tokens : (kind + 1) * own_tokens] for kind in range(3)
    )
    top = jnp.max(tops, axis=0)
    total = jnp.sum(totals * jnp.exp(tops - top[None, :]), axis=0)
    log_total = top + jnp.log(total)
    position = jnp.arange(own_tokens) % draft_len
    verify_scores = jnp.where(
        position < draft_len - 1, jnp.sum(hits, axis=0) - log_total, top - log_total
    ).reshape(own_reqs, draft_len)
    return (
        after_feed.reshape(own_reqs, draft_len, width),
        verify_scores,
        kept_state,
        kept_conv,
    )


def solution(mesh):
    in_specs = (
        P("req", None, None),
        P(),
        P(None, "mdl"),
        P(),
        P("mdl", None),
        P("req", None, None, None),
        P("req"),
        P("req"),
        P("req"),
        P(None, "mdl"),
        P(None, "mdl"),
        P(),
        P(None, "mdl"),
        P(None, "mdl"),
        P(),
        P("mdl"),
        P("mdl"),
        P("mdl"),
        P("req", "mdl", None, None),
        P("req", None, "mdl"),
        P("req", None, None),
        P("mdl", None),
        P(),
        P(None, "req"),
        P(None, "req"),
        P("req", None),
        P(),
        P("req", None),
        P(),
    )
    out_specs = (
        P(("req", "mdl"), None, None),
        P(("req", "mdl"), None),
        P(("req", "mdl"), None, None, None),
        P(("req", "mdl"), None, None),
    )
    return jax.shard_map(shards, mesh=mesh, in_specs=in_specs, out_specs=out_specs, check_vma=False)
```

```python
import functools

import jax
import jax.numpy as jnp
import numpy as np
from jax import lax
from jax.experimental import pallas as pl
from jax.experimental.pallas import tpu as pltpu
from jax.sharding import PartitionSpec as P

Q_HEADS = 8
KV_HEADS = 2
HEAD_DIM = 128
SSM_DIM = 64
STATE = 256
CONV = 4
PROMPTS = 2
P_MAX = 1024
DRAFT = 16
SIDE = 4
CORES = 2

eps_norm = 1e-05
far_below = -1e30

DIRECT = (1, 3, 2)
EDGES = ((1, 3), (3, 1))


def device_at(y, x, core):
    return (y * SIDE + x) * CORES + core


def flip_pairs(ring, flip):
    pairs = []
    for y in range(SIDE):
        for x in range(SIDE):
            for core in range(CORES):
                on_x = ring == core
                target = device_at(y if on_x else y ^ flip, x ^ flip if on_x else x, core)
                pairs.append((device_at(y, x, core), target))
    return pairs


CORE_PAIRS = [(device, device ^ 1) for device in range(SIDE * SIDE * CORES)]


def hop(part, ring, flip):
    return lax.ppermute(part, "req", flip_pairs(ring, flip))


def swap_core(part):
    return lax.ppermute(part, "req", CORE_PAIRS)


def gather_rows(rows):
    came = [hop(rows, 0, flip) for flip in DIRECT]
    held = [jnp.concatenate([rows, came[0]], axis=0), jnp.concatenate(came[1:], axis=0)]
    near = [hop(held[s], 1, EDGES[s][0]) for s in range(2)]
    far = [hop(held[s], 1, EDGES[s][1]) for s in range(2)]
    last = [hop(near[s], 1, EDGES[s][1]) for s in range(2)]
    return held + near + far, last


def added(*parts):
    return sum(part.astype(jnp.float32) for part in parts).astype(jnp.bfloat16)


def scatter_rows(early, late):
    rows = late[0][0].shape[0]

    def stream(joined, s):
        return joined[s * rows : (s + 1) * rows]

    came = swap_core(late[1][0])
    last = [hop(added(late[0][s], stream(came, s)), 1, EDGES[s][1]) for s in range(2)]
    kept, near, far = (swap_core(part) for part in early[1])
    own = early[0]
    far = [hop(added(own[4 + s], stream(far, s)), 1, EDGES[s][1]) for s in range(2)]
    near = [hop(added(own[2 + s], stream(near, s), last[s]), 1, EDGES[s][0]) for s in range(2)]
    held = [added(own[s], stream(kept, s), far[s], near[s]) for s in range(2)]
    half = held[0].shape[0] // 2
    blocks = (held[0][half:], held[1][:half], held[1][half:])
    came = [hop(block, 0, flip) for block, flip in zip(blocks, DIRECT, strict=True)]
    total = held[0][:half].astype(jnp.float32)
    return sum((part.astype(jnp.float32) for part in came), total)


def swap_early(arrays):
    kept = [swap_core(part) for part in arrays[:2]]
    return kept + [swap_core(jnp.concatenate(arrays[k : k + 2], axis=0)) for k in (2, 4)]


def block_table():
    arrays = [(half, kind) for half in range(2) for kind in range(3)] + [(0, 3), (1, 3)]
    table = np.zeros((CORES, len(arrays), 2, 2, 2, 4), np.int32)
    for core, array, stream, block, request in np.ndindex(table.shape[:-1]):
        half, kind = arrays[array]
        first = ((0, 1), (3, 2))[stream][block]
        other = (0, *EDGES[stream], 2)[kind]
        y, x = (other, first) if core == half else (first, other)
        table[core, array, stream, block, request] = (y, x, half, request)
    return table.reshape(CORES, 64, 4)


def rms_scale(values, gain):
    widened = values.astype(jnp.float32)
    spread = jnp.mean(widened * widened, axis=-1, keepdims=True)
    return widened * lax.rsqrt(spread + eps_norm) * gain.astype(jnp.float32)


HIGHEST = lax.Precision.HIGHEST
NEXT_TO = (((1,), (1,)), ((), ()))


def dot32(left, right, dims=None):
    dims = dims or (((1,), (0,)), ((), ()))
    return lax.dot_general(left, right, dims, preferred_element_type=jnp.float32)


def exact_dot(left, right):
    return jnp.dot(left, right, precision=HIGHEST, preferred_element_type=jnp.float32)


def lane_spread(rows, lanes):
    return (
        lax.broadcasted_iota(jnp.int32, (rows, lanes), 0)
        == lax.broadcasted_iota(jnp.int32, (rows, lanes), 1) // SSM_DIM
    ).astype(jnp.float32)


def keeper_kernel(*refs):
    sources, (kept_ref, kept_bc_ref), held, sems = refs[:10], refs[10:12], refs[12:22], refs[22]
    copies = [
        pltpu.make_async_copy(source, target, sems.at[index])
        for index, (source, target) in enumerate(zip(sources, held, strict=True))
    ]
    for copy in copies:
        copy.start()
    for copy in copies:
        copy.wait()
    member_ref, accepted_ref, decay_ref, scaled_ref, b_ref, in_x_ref, in_bc_ref = held[:7]
    past_x_ref, past_bc_ref, state = held[7:]
    tokens, inner = scaled_ref.shape
    requests = tokens // DRAFT
    rank = lax.axis_index("mdl")

    row = lax.broadcasted_iota(jnp.int32, (tokens, 1), 0)
    time, request = row % DRAFT, row // DRAFT
    last = jnp.zeros((tokens, 1), jnp.int32)
    for r in range(requests):
        last = jnp.where(request == r, accepted_ref[r] - 1, last)
    spread_lanes = lane_spread(tokens, inner)
    log_decay, scaled_x, b_part = decay_ref[...], scaled_ref[...], b_ref[...]
    in_x, in_bc = in_x_ref[...], in_bc_ref[...]
    decay_x = exact_dot(log_decay, spread_lanes)
    other = lax.broadcasted_iota(jnp.int32, (tokens, tokens), 1)
    pick = (other == request * DRAFT + last).astype(jnp.float32)
    final_log = exact_dot(pick, log_decay)
    final_x = exact_dot(final_log, spread_lanes)
    carry_x = jnp.exp(jnp.where(time <= last, final_x - decay_x, far_below))
    carried_x = (scaled_x * carry_x).T.astype(jnp.bfloat16)
    shrink = jnp.exp(final_x).T
    for r in range(requests):
        b_here = jnp.where(request == r, b_part, jnp.zeros_like(b_part))
        kept = shrink[:, r * DRAFT : r * DRAFT + 1] * state[member_ref[r]] + dot32(
            carried_x, b_here
        )
        kept_ref[r, :inner, :] = kept.astype(jnp.bfloat16)

    def kept_rows(first_request, count, slots, series, past_of):
        at = lax.broadcasted_iota(jnp.int32, (count * slots, 1), 0)
        here, edge = at // slots, at % slots
        start = jnp.zeros((count * slots, 1), jnp.int32)
        owner = jnp.zeros((count * slots, 1), jnp.int32)
        for r in range(count):
            start = jnp.where(here == r, accepted_ref[first_request + r], start)
            owner = jnp.where(here == r, member_ref[first_request + r], owner)
        index = start + edge
        token = (here + first_request) * DRAFT + index - (CONV - 1)
        chosen = (lax.broadcasted_iota(jnp.int32, (count * slots, tokens), 1) == token) & (
            index >= CONV - 1
        )
        rows = dot32(chosen.astype(jnp.bfloat16), series)
        for p in range(PROMPTS):
            for j in range(CONV - 1):
                rows = jnp.where((owner == p) & (index == j), past_of(j, p), rows)
        return rows.astype(jnp.bfloat16)

    for lanes in range(2):
        cut = slice(lanes * STATE, min((lanes + 1) * STATE, inner))
        rows = kept_rows(
            0, requests, 8, in_x[:, cut], lambda j, p: past_x_ref[j, p : p + 1, cut].astype(jnp.float32)
        )
        for r in range(requests):
            kept_ref[r, inner + 8 * lanes : inner + 8 * (lanes + 1), : rows.shape[1]] = rows[
                r * 8 : (r + 1) * 8
            ]
    kept_ref[:, inner + 8 :, inner - STATE :] = jnp.zeros(
        (requests, 8, 2 * STATE - inner), jnp.bfloat16
    )
    kept_bc_ref[...] = kept_rows(
        rank * (requests // SIDE),
        requests // SIDE,
        8,
        in_bc,
        lambda j, p: past_bc_ref[j, p : p + 1, :].astype(jnp.float32),
    )


def keeper(member, accepted, log_decay, scaled_x, b_part, in_x, in_bc, past_x, past_bc, state):
    tokens, inner = scaled_x.shape
    requests = tokens // DRAFT
    operands = (member, accepted, log_decay, scaled_x, b_part, in_x, in_bc, past_x, past_bc, state)
    whole = pl.BlockSpec(memory_space=pltpu.VMEM)
    return pl.pallas_call(
        keeper_kernel,
        out_shape=[
            jax.ShapeDtypeStruct((requests, inner + 16, STATE), jnp.bfloat16),
            jax.ShapeDtypeStruct((requests // SIDE * 8, 2 * STATE), jnp.bfloat16),
        ],
        in_specs=[pl.BlockSpec(memory_space=pltpu.HBM)] * len(operands),
        out_specs=[whole] * 2,
        scratch_shapes=[
            *(pltpu.SMEM(a.shape, a.dtype) for a in operands[:2]),
            *(pltpu.VMEM(a.shape, a.dtype) for a in operands[2:]),
            pltpu.SemaphoreType.DMA((len(operands),)),
        ],
        compiler_params=pltpu.CompilerParams(vmem_limit_bytes=12 << 20),
        cost_estimate=pl.CostEstimate(
            flops=2_000_000_000, bytes_accessed=5_000_000, transcendentals=200_000
        ),
        name="keeper",
    )(*operands)


def unpack_kernel(kept_hbm, bc_ref, _stats, _tip, state_ref, conv_ref, kept_ref, sem):
    copy = pltpu.make_async_copy(kept_hbm, kept_ref, sem)
    copy.start()
    copy.wait()
    inner = kept_ref.shape[2] - 16
    for r in range(state_ref.shape[0]):
        for z in range(kept_ref.shape[0]):
            state_ref[r, z * inner : (z + 1) * inner, :] = kept_ref[z, r, :inner, :].astype(
                jnp.float32
            )
    for j in range(CONV - 1):
        rows = []
        for r in range(state_ref.shape[0]):
            pieces = []
            for z in range(kept_ref.shape[0]):
                tail = kept_ref[z, r, inner:, :].astype(jnp.float32)
                pieces += [tail[j : j + 1, :], tail[8 + j : 9 + j, : inner - STATE]]
            pieces.append(bc_ref[...].astype(jnp.float32)[r * 8 + j : r * 8 + j + 1, :])
            rows.append(jnp.concatenate(pieces, axis=1))
        conv_ref[j] = jnp.concatenate(rows, axis=0).astype(jnp.bfloat16)


def unpack(kept_out, own_bc, *tokens):
    sources, requests, rows, _ = kept_out.shape
    inner = rows - 16
    whole = pl.BlockSpec(memory_space=pltpu.VMEM)
    state, conv = pl.pallas_call(
        unpack_kernel,
        out_shape=[
            jax.ShapeDtypeStruct((requests, sources * inner, STATE), jnp.float32),
            jax.ShapeDtypeStruct((CONV - 1, requests, sources * inner + 2 * STATE), jnp.bfloat16),
        ],
        in_specs=[pl.BlockSpec(memory_space=pltpu.HBM), whole]
        + [pl.BlockSpec(memory_space=pl.ANY)] * len(tokens),
        out_specs=[whole] * 2,
        scratch_shapes=[pltpu.VMEM(kept_out.shape, kept_out.dtype), pltpu.SemaphoreType.DMA],
        compiler_params=pltpu.CompilerParams(vmem_limit_bytes=10 << 20),
        cost_estimate=pl.CostEstimate(flops=1_000_000, bytes_accessed=20_000_000, transcendentals=0),
        name="unpack",
    )(kept_out, own_bc, *tokens)
    return state, conv.transpose(1, 0, 2)


def mixer_kernel(*refs):
    sources, refs = refs[:22], refs[22:]
    part_refs = refs[:SIDE]
    decay_ref, scaled_ref, b_ref, in_x_ref, in_bc_ref = refs[SIDE : SIDE + 5]
    held, (mixed_scr, lanes_scr, sems) = refs[SIDE + 5 : -3], refs[-3:]
    member_ref, accepted_ref, lengths_ref, rate_ref, bias_ref, skip_ref = held[:6]
    hidden_ref, gain_ref, w_dt_ref, conv_x_ref, conv_bc_ref, past_x_ref, past_bc_ref = held[6:13]
    w_query, w_kv, prompt, w_x, w_bc, w_z, state, w_out = held[13:]
    tokens = hidden_ref.shape[0]
    requests = tokens // DRAFT
    inner = w_x.shape[1]
    heads = inner // SSM_DIM
    query_width = w_query.shape[1]
    rank = lax.axis_index("mdl")
    group = rank * (query_width // HEAD_DIM) // (Q_HEADS // KV_HEADS)
    query_hbm, kv_hbm, prompt_hbm, x_hbm, bc_hbm, z_hbm, state_hbm, attn_hbm, mamba_hbm = sources[13:]
    moves = [(source, target) for source, target in zip(sources[:13], held[:13], strict=True)]
    moves += [
        (query_hbm, w_query),
        (kv_hbm.at[group], w_kv),
        (prompt_hbm.at[0, group], prompt.at[0]),
        (prompt_hbm.at[1, group], prompt.at[1]),
        (x_hbm, w_x),
        (bc_hbm, w_bc),
        (z_hbm, w_z),
        (state_hbm, state),
        (attn_hbm, w_out.at[pl.ds(0, query_width), :]),
        (mamba_hbm, w_out.at[pl.ds(query_width, inner), :]),
    ]
    started = [
        pltpu.make_async_copy(source, target, sems.at[index])
        for index, (source, target) in enumerate(moves)
    ]
    for copy in started:
        copy.start()
    for copy in started[:13]:
        copy.wait()
    copies = started[13:]

    def head_row(ref):
        lane = lax.broadcasted_iota(jnp.int32, (1, heads), 1)
        values = jnp.zeros((1, heads), jnp.float32)
        for h in range(heads):
            values = jnp.where(lane == h, ref[h], values)
        return values

    row = lax.broadcasted_iota(jnp.int32, (tokens, 1), 0)
    time, request = row % DRAFT, row // DRAFT
    own_prompt = jnp.zeros((tokens, 1), jnp.int32)
    last = jnp.zeros((tokens, 1), jnp.int32)
    for r in range(requests):
        own_prompt = jnp.where(request == r, member_ref[r], own_prompt)
        last = jnp.where(request == r, accepted_ref[r] - 1, last)
    first_prompt = own_prompt == 0

    gain = jnp.concatenate(
        [gain_ref[j : j + 1, :].astype(jnp.float32) for j in range(gain_ref.shape[0])], axis=1
    )
    widened = hidden_ref[...].astype(jnp.float32)
    spread = jnp.mean(widened * widened, axis=-1, keepdims=True)
    normed = (
        widened * lax.rsqrt(spread + eps_norm) * gain
    ).astype(jnp.bfloat16)

    copies[0].wait()
    queries = dot32(normed, w_query[...]).astype(jnp.bfloat16)
    copies[1].wait()
    drafts = dot32(normed, w_kv[...]).astype(jnp.bfloat16)
    local_heads = query_width // HEAD_DIM
    query_rows = jnp.concatenate(
        [queries[:, h * HEAD_DIM : (h + 1) * HEAD_DIM] for h in range(local_heads)], axis=0
    )
    scale = HEAD_DIM**-0.5
    row_first = jnp.concatenate([own_prompt] * local_heads, axis=0) == 0
    draft_scores = dot32(query_rows, drafts[:, :HEAD_DIM], NEXT_TO) * scale
    same = (row // DRAFT == lax.broadcasted_iota(jnp.int32, (tokens, tokens), 1) // DRAFT) & (
        lax.broadcasted_iota(jnp.int32, (tokens, tokens), 1) <= row
    )
    draft_mask = jnp.concatenate([same] * local_heads, axis=0)
    draft_scores = jnp.where(draft_mask, draft_scores, far_below)
    copies[2].wait()
    copies[3].wait()
    scores = jnp.where(
        row_first,
        dot32(query_rows, prompt[0, :, :HEAD_DIM], NEXT_TO),
        dot32(query_rows, prompt[1, :, :HEAD_DIM], NEXT_TO),
    )
    length = jnp.where(row_first, lengths_ref[0], lengths_ref[1])
    position = lax.broadcasted_iota(jnp.int32, scores.shape, 1)
    scores = jnp.where(position < length, scores * scale, far_below)
    top = jnp.maximum(
        jnp.max(scores, axis=1, keepdims=True), jnp.max(draft_scores, axis=1, keepdims=True)
    )
    weights = jnp.exp(scores - top)
    draft_weights = jnp.exp(draft_scores - top)
    total = jnp.sum(weights, axis=1, keepdims=True) + jnp.sum(draft_weights, axis=1, keepdims=True)
    weighted = (
        dot32(jnp.where(row_first, weights, 0.0).astype(jnp.bfloat16), prompt[0, :, HEAD_DIM:])
        + dot32(jnp.where(row_first, 0.0, weights).astype(jnp.bfloat16), prompt[1, :, HEAD_DIM:])
        + dot32(draft_weights.astype(jnp.bfloat16), drafts[:, HEAD_DIM:])
    )
    attended = (weighted / total).astype(jnp.bfloat16)
    for h in range(local_heads):
        mixed_scr[:, h * HEAD_DIM : (h + 1) * HEAD_DIM] = attended[h * tokens : (h + 1) * tokens]

    def convolve_rows(series, past_ref, taps_ref):
        past = [
            jnp.where(
                first_prompt,
                past_ref[j, 0:1, :].astype(jnp.float32),
                past_ref[j, 1:2, :].astype(jnp.float32),
            )
            for j in range(CONV - 1)
        ]
        taps = taps_ref[...].astype(jnp.float32)
        summed = series * taps[CONV - 1 : CONV, :]
        for shift in range(1, CONV):
            window = pltpu.roll(series, shift, 0)
            for t in range(shift):
                window = jnp.where(time == t, past[CONV - 1 - shift + t], window)
            summed = summed + window * taps[CONV - 1 - shift : CONV - shift, :]
        return summed * jax.nn.sigmoid(summed)

    copies[4].wait()
    in_x = dot32(normed, w_x[...]).astype(jnp.bfloat16)
    heads_x = convolve_rows(in_x.astype(jnp.float32), past_x_ref, conv_x_ref)
    copies[5].wait()
    in_bc = dot32(normed, w_bc[...]).astype(jnp.bfloat16)
    conv_bcs = convolve_rows(in_bc.astype(jnp.float32), past_bc_ref, conv_bc_ref)
    b_part = conv_bcs[:, :STATE].astype(jnp.bfloat16)
    c_part = conv_bcs[:, STATE:].astype(jnp.bfloat16)

    def widen(values):
        lanes_scr[...] = jnp.zeros(lanes_scr.shape, jnp.float32)
        lanes_scr[:, :heads] = values
        return lanes_scr[...]

    spread_lanes = lane_spread(tokens, inner)
    dt_in = dot32(normed, w_dt_ref[...], NEXT_TO).astype(jnp.bfloat16).astype(jnp.float32) + head_row(bias_ref)
    step = jnp.maximum(dt_in, 0.0) + jnp.log1p(jnp.exp(-jnp.abs(dt_in)))
    log_decay = exact_dot(same.astype(jnp.float32), widen(-step * head_row(rate_ref)))
    step_x = exact_dot(widen(step), spread_lanes)
    skip_x = exact_dot(widen(jnp.broadcast_to(head_row(skip_ref), (tokens, heads))), spread_lanes)
    decay_x = exact_dot(log_decay, spread_lanes)
    turned = log_decay.T
    intersection = dot32(c_part, b_part, NEXT_TO)
    scaled_x = heads_x * step_x
    low = lax.broadcasted_iota(jnp.int32, (tokens, 2 * SSM_DIM), 1) < SSM_DIM
    groups = []
    for pair in range(heads // 2):
        mixing = []
        for h in (2 * pair, 2 * pair + 1):
            gaps = log_decay[:, h : h + 1] - turned[h : h + 1, :]
            mixing.append(
                (jnp.exp(jnp.where(same, gaps, far_below)) * intersection).astype(jnp.bfloat16)
            )
        lanes = scaled_x[:, pair * 2 * SSM_DIM : (pair + 1) * 2 * SSM_DIM]
        both = jnp.concatenate([jnp.where(low, lanes, 0.0), jnp.where(low, 0.0, lanes)], axis=0)
        groups.append(dot32(jnp.concatenate(mixing, axis=1), both.astype(jnp.bfloat16)))
    copies[7].wait()
    carried = jnp.where(
        first_prompt,
        dot32(c_part, state[0].astype(jnp.bfloat16), NEXT_TO),
        dot32(c_part, state[1].astype(jnp.bfloat16), NEXT_TO),
    )
    ssm_out = jnp.concatenate(groups, axis=1) + carried * jnp.exp(decay_x) + skip_x * heads_x
    copies[6].wait()
    gate_z = dot32(normed, w_z[...]).astype(jnp.bfloat16).astype(jnp.float32)
    mixed_scr[:, query_width:] = (ssm_out * (gate_z * jax.nn.sigmoid(gate_z))).astype(jnp.bfloat16)

    own_rows = tokens // SIDE
    copies[8].wait()
    copies[9].wait()
    rows = jnp.concatenate(
        [
            mixed_scr[pl.ds(pl.multiple_of((rank ^ flip) * own_rows, own_rows), own_rows), :]
            for flip in (0, *DIRECT)
        ],
        axis=0,
    )
    parts = dot32(rows, w_out[...]).astype(jnp.bfloat16)
    for block, part_ref in enumerate(part_refs):
        part_ref[...] = parts[block * own_rows : (block + 1) * own_rows]
    decay_ref[...] = log_decay
    scaled_ref[...] = scaled_x
    b_ref[...] = b_part
    in_x_ref[...] = in_x
    in_bc_ref[...] = in_bc


def mixer(
    hidden, mixer_gain, w_query, w_kv, w_attn_out, prompt_kv, prompt_lengths, member, accepted, w_z, w_x, w_bc,
    w_dt, conv_x, conv_bc, ssm_rate, dt_bias, skip_d, prompt_state, prompt_conv_x, prompt_conv_bc, w_mamba_out,
):
    tokens, width = hidden.shape
    inner = w_x.shape[1]
    query_width = w_query.shape[1]
    bf16 = jnp.bfloat16
    state = prompt_state.reshape(PROMPTS, inner, STATE)
    small = [
        hidden, mixer_gain.reshape(-1, 128), w_dt.T, conv_x, conv_bc,
        prompt_conv_x.transpose(1, 0, 2), prompt_conv_bc.transpose(1, 0, 2),
    ]
    scalars = [member, accepted, prompt_lengths, ssm_rate, dt_bias, skip_d]
    whole = pl.BlockSpec(memory_space=pltpu.VMEM)
    outs = pl.pallas_call(
        mixer_kernel,
        out_shape=[
            *([jax.ShapeDtypeStruct((tokens // SIDE, width), bf16)] * SIDE),
            jax.ShapeDtypeStruct((tokens, 128), jnp.float32),
            jax.ShapeDtypeStruct((tokens, inner), jnp.float32),
            jax.ShapeDtypeStruct((tokens, STATE), bf16),
            jax.ShapeDtypeStruct((tokens, inner), bf16),
            jax.ShapeDtypeStruct((tokens, 2 * STATE), bf16),
        ],
        in_specs=[pl.BlockSpec(memory_space=pltpu.HBM)] * 22,
        out_specs=[whole] * (SIDE + 5),
        scratch_shapes=[
            *(pltpu.SMEM(a.shape, a.dtype) for a in scalars),
            *(pltpu.VMEM(a.shape, a.dtype) for a in small),
            pltpu.VMEM(w_query.shape, bf16),
            pltpu.VMEM(w_kv.shape[1:], bf16),
            pltpu.VMEM((PROMPTS, *prompt_kv.shape[2:]), bf16),
            pltpu.VMEM(w_x.shape, bf16),
            pltpu.VMEM(w_bc.shape, bf16),
            pltpu.VMEM(w_z.shape, bf16),
            pltpu.VMEM(state.shape, jnp.float32),
            pltpu.VMEM((query_width + inner, width), bf16),
            pltpu.VMEM((tokens, query_width + inner), bf16),
            pltpu.VMEM((tokens, 128), jnp.float32),
            pltpu.SemaphoreType.DMA((23,)),
        ],
        compiler_params=pltpu.CompilerParams(vmem_limit_bytes=59 << 20),
        cost_estimate=pl.CostEstimate(
            flops=3_000_000_000, bytes_accessed=20_000_000, transcendentals=1_000_000
        ),
        name="mixer",
    )(
        *scalars, *small, w_query, w_kv, prompt_kv, w_x, w_bc, w_z, state, w_attn_out, w_mamba_out
    )
    return outs[:SIDE], *keeper(member, accepted, *outs[SIDE:], *small[-2:], state)


def feed_kernel(count, both_ref, down_ref, _token, *refs):
    hidden = down_ref.shape[0]
    rows_refs, out_refs = refs[:count], refs[count:]
    joined = jnp.concatenate([ref[...] for ref in rows_refs], axis=0)
    pair = dot32(joined, both_ref[...])
    gate, up = pair[:, :hidden], pair[:, hidden:]
    active = (gate * jax.nn.sigmoid(gate) * up).astype(jnp.bfloat16)
    parts = dot32(active, down_ref[...]).astype(jnp.bfloat16)
    first = 0
    for out_ref in out_refs:
        out_ref[...] = parts[first : first + out_ref.shape[0]]
        first += out_ref.shape[0]


def feed(arrays, out_rows, w_both, w_down, token):
    rows, width = sum(a.shape[0] for a in arrays), arrays[0].shape[1]
    whole = pl.BlockSpec(memory_space=pltpu.VMEM)
    return pl.pallas_call(
        functools.partial(feed_kernel, len(arrays)),
        out_shape=[jax.ShapeDtypeStruct((r, width), jnp.bfloat16) for r in out_rows],
        in_specs=[whole] * 2
        + [pl.BlockSpec(memory_space=pl.ANY)]
        + [whole] * len(arrays),
        out_specs=[whole] * len(out_rows),
        compiler_params=pltpu.CompilerParams(vmem_limit_bytes=12 << 20),
        cost_estimate=pl.CostEstimate(
            flops=4 * rows * width * 2 * 3 * w_down.shape[0],
            bytes_accessed=2 * rows * width * 2 + 3 * w_down.size * 2,
            transcendentals=rows * w_down.shape[0],
        ),
        name="feed",
    )(w_both, w_down, token, *arrays)


def head_kernel(count, targets_ref, owners_ref, *refs):
    groups, lanes = targets_ref.shape
    rows_refs, head_ref, others, out_ref = refs[:count], refs[count], refs[count + 1 : -1], refs[-1]
    vocab = head_ref.shape[0]
    devices = out_ref.shape[0]
    base = lax.axis_index("req") * vocab
    ids = lax.broadcasted_iota(jnp.int32, (vocab, lanes), 0) + base
    device = lax.broadcasted_iota(jnp.int32, (devices, lanes), 0)
    source = lax.broadcasted_iota(jnp.int32, (3 * lanes, 128), 0)
    column = lax.broadcasted_iota(jnp.int32, (3 * lanes, 128), 1)
    place = (column == source // lanes * (2 * DRAFT) + source % (2 * DRAFT)).astype(jnp.bfloat16)
    packed = jnp.zeros((devices, 128), jnp.float32)
    for other in others:
        packed = packed + other[:, 0, :]
    for group in range(groups):
        members, first = [], 0
        for ref in rows_refs:
            if group * lanes <= first < (group + 1) * lanes:
                members.append(ref[...])
            first += ref.shape[0]
        joined = jnp.concatenate(members, axis=0)
        logits = dot32(head_ref[...], joined, NEXT_TO)
        wanted = targets_ref[group : group + 1, :]
        target = jnp.sum(jnp.where(ids == wanted, logits, 0.0), axis=0, keepdims=True)
        top = jnp.max(logits, axis=0, keepdims=True)
        total = jnp.sum(jnp.exp(logits - top), axis=0, keepdims=True)
        here = device == owners_ref[group : group + 1, :]
        rest = jnp.concatenate([jnp.where(here, stat, 0.0) for stat in (top, total, target)], axis=1)
        for _ in range(3):
            part = rest.astype(jnp.bfloat16)
            packed = packed + dot32(part, place)
            rest = rest - part.astype(jnp.float32)
    out_ref[:, 0, :] = packed


def head_stats(targets, owners, rows, head_weight, devices, others=()):
    whole = pl.BlockSpec(memory_space=pltpu.VMEM)
    return pl.pallas_call(
        functools.partial(head_kernel, len(rows)),
        out_shape=jax.ShapeDtypeStruct((devices, 1, 128), jnp.float32),
        in_specs=[whole] * (3 + len(rows) + len(others)),
        out_specs=whole,
        compiler_params=pltpu.CompilerParams(vmem_limit_bytes=20 << 20),
        cost_estimate=pl.CostEstimate(
            flops=1 * 2 * targets.size * head_weight.size,
            bytes_accessed=2 * targets.size * head_weight.shape[1] + 2 * head_weight.size,
            transcendentals=targets.size * head_weight.shape[0],
        ),
        name="head_stats",
    )(targets, owners, *rows, head_weight, *others)


def shards(
    hidden_in,
    mixer_gain,
    w_query,
    w_kv,
    w_attn_out,
    prompt_kv,
    prompt_lengths,
    member,
    accepted,
    w_z,
    w_x,
    w_bc,
    w_dt,
    conv_x,
    conv_bc,
    ssm_rate,
    dt_bias,
    skip_d,
    prompt_state,
    prompt_conv_x,
    prompt_conv_bc,
    w_mamba_out,
    mlp_gain,
    w_gate,
    w_up,
    w_down,
    final_gain,
    head_weight,
    draft_ids,
):
    row_reqs, draft_len, width = hidden_in.shape
    mdl_count = lax.axis_size("mdl")
    req_count = lax.axis_size("req")
    mdl_rank = lax.axis_index("mdl")
    req_rank = lax.axis_index("req")
    row_tokens = row_reqs * draft_len
    own_reqs = row_reqs // mdl_count
    own_tokens = own_reqs * draft_len
    flat_rows = hidden_in.reshape(row_tokens, width)
    local_inner = w_x.shape[1]
    parts, kept, own_bc = mixer(
        flat_rows, mixer_gain, w_query, w_kv, w_attn_out, prompt_kv, prompt_lengths, member, accepted, w_z, w_x, w_bc,
        w_dt, conv_x, conv_bc, ssm_rate, dt_bias, skip_d, prompt_state, prompt_conv_x, prompt_conv_bc, w_mamba_out,
    )
    came = [
        lax.ppermute(part, "mdl", [(z, z ^ flip) for z in range(SIDE)])
        for part, flip in zip(parts[1:], DIRECT, strict=True)
    ]
    mixed = sum((part.astype(jnp.float32) for part in came), parts[0].astype(jnp.float32))
    own_rows = lax.dynamic_slice_in_dim(flat_rows, mdl_rank * own_tokens, own_tokens, 0)
    after_mixer = (own_rows.astype(jnp.float32) + mixed).astype(jnp.bfloat16)
    prepared = rms_scale(after_mixer, mlp_gain).astype(jnp.bfloat16)
    w_both = jnp.concatenate([w_gate, w_up], axis=1)
    early, late = gather_rows(prepared)
    early = (early, swap_early(early))
    late = (late, [swap_core(part) for part in late])

    core = req_rank % CORES
    chip_x = req_rank // CORES % SIDE
    chip_y = req_rank // (CORES * SIDE)
    table = jnp.where(core == 0, jnp.asarray(block_table()[0]), jnp.asarray(block_table()[1]))
    owner = ((chip_y ^ table[:, 0]) * SIDE + (chip_x ^ table[:, 1])) * CORES + (core ^ table[:, 2])
    request = owner * row_reqs + mdl_rank * own_reqs + table[:, 3]
    next_ids = jnp.concatenate([draft_ids[:, 1:], draft_ids[:, :1]], axis=1)
    picked = (request[:, None] == jnp.arange(draft_ids.shape[0])[None, :]).astype(jnp.float32)
    targets = jnp.dot(picked, next_ids.astype(jnp.float32), precision=HIGHEST).astype(jnp.int32)
    targets = targets.reshape(1, 64 * draft_len)
    owners = jnp.broadcast_to(owner[:, None], (64, draft_len)).reshape(1, 64 * draft_len)

    half = 2 * own_tokens
    early_parts = [
        feed(rows, out_rows, w_both, w_down, mlp_gain)
        for rows, out_rows in zip(early, ([half] * 6, [2 * half] * 3), strict=True)
    ]
    late_parts = [
        feed(rows, out_rows, w_both, w_down, own_bc)
        for rows, out_rows in zip(late, ([half] * 2, [2 * half]), strict=True)
    ]
    summed = scatter_rows(early_parts, late_parts)
    tip = early_parts[0][0][:8, :128]
    kept, tip = lax.optimization_barrier((kept, tip))
    kept_out = lax.all_to_all(
        kept.reshape(mdl_count, own_reqs, local_inner + 16, STATE),
        "mdl",
        split_axis=0,
        concat_axis=0,
        tiled=True,
    )
    final_gain, targets, owners = lax.optimization_barrier((final_gain, targets, owners))
    after_feed = (after_mixer.astype(jnp.float32) + summed).astype(jnp.bfloat16)
    final_rows = rms_scale(after_feed, final_gain).astype(jnp.bfloat16)
    early, late = gather_rows(final_rows)
    sibling = swap_early(early)
    most = 6 * half
    first = head_stats(targets[:, :most], owners[:, :most], early, head_weight, req_count)
    second = head_stats(
        targets[:, most : 2 * most], owners[:, most : 2 * most], sibling, head_weight, req_count
    )
    late, first, second = lax.optimization_barrier((late, first, second))
    late = late + [swap_core(part) for part in late]
    stats = head_stats(
        targets[:, 2 * most :], owners[:, 2 * most :], late, head_weight, req_count, [first, second]
    )
    kept_state, kept_conv = unpack(kept_out, own_bc, stats, tip)
    kept_state = kept_state.reshape(own_reqs, -1, SSM_DIM, STATE)
    shared = lax.all_to_all(stats, "req", split_axis=0, concat_axis=0, tiled=True)
    tops, totals, hits = (
        shared[:, 0, kind * own_tokens : (kind + 1) * own_tokens] for kind in range(3)
    )
    top = jnp.max(tops, axis=0)
    total = jnp.sum(totals * jnp.exp(tops - top[None, :]), axis=0)
    log_total = top + jnp.log(total)
    position = jnp.arange(own_tokens) % draft_len
    verify_scores = jnp.where(
        position < draft_len - 1, jnp.sum(hits, axis=0) - log_total, top - log_total
    ).reshape(own_reqs, draft_len)
    return (
        after_feed.reshape(own_reqs, draft_len, width),
        verify_scores,
        kept_state,
        kept_conv,
    )


def solution(mesh):
    in_specs = (
        P("req", None, None),
        P(),
        P(None, "mdl"),
        P(),
        P("mdl", None),
        P("req", None, None, None),
        P("req"),
        P("req"),
        P("req"),
        P(None, "mdl"),
        P(None, "mdl"),
        P(),
        P(None, "mdl"),
        P(None, "mdl"),
        P(),
        P("mdl"),
        P("mdl"),
        P("mdl"),
        P("req", "mdl", None, None),
        P("req", None, "mdl"),
        P("req", None, None),
        P("mdl", None),
        P(),
        P(None, "req"),
        P(None, "req"),
        P("req", None),
        P(),
        P("req", None),
        P(),
    )
    out_specs = (
        P(("req", "mdl"), None, None),
        P(("req", "mdl"), None),
        P(("req", "mdl"), None, None, None),
        P(("req", "mdl"), None, None),
    )
    return jax.shard_map(shards, mesh=mesh, in_specs=in_specs, out_specs=out_specs, check_vma=False)
```

```python
import functools

import jax
import jax.numpy as jnp
import numpy as np
from jax import lax
from jax.experimental import pallas as pl
from jax.experimental.pallas import tpu as pltpu
from jax.sharding import PartitionSpec as P

Q_HEADS = 8
KV_HEADS = 2
HEAD_DIM = 128
SSM_DIM = 64
STATE = 256
CONV = 4
PROMPTS = 2
P_MAX = 1024
DRAFT = 16
SIDE = 4
CORES = 2

eps_norm = 1e-05
far_below = -1e30

DIRECT = (1, 3, 2)
EDGES = ((1, 3), (3, 1))


def device_at(y, x, core):
    return (y * SIDE + x) * CORES + core


def flip_pairs(ring, flip):
    pairs = []
    for y in range(SIDE):
        for x in range(SIDE):
            for core in range(CORES):
                on_x = ring == core
                target = device_at(y if on_x else y ^ flip, x ^ flip if on_x else x, core)
                pairs.append((device_at(y, x, core), target))
    return pairs


CORE_PAIRS = [(device, device ^ 1) for device in range(SIDE * SIDE * CORES)]


def hop(part, ring, flip):
    return lax.ppermute(part, "req", flip_pairs(ring, flip))


def swap_core(part):
    return lax.ppermute(part, "req", CORE_PAIRS)


def gather_rows(rows):
    came = [hop(rows, 0, flip) for flip in DIRECT]
    held = [jnp.concatenate([rows, came[0]], axis=0), jnp.concatenate(came[1:], axis=0)]
    near = [hop(held[s], 1, EDGES[s][0]) for s in range(2)]
    far = [hop(held[s], 1, EDGES[s][1]) for s in range(2)]
    last = [hop(near[s], 1, EDGES[s][1]) for s in range(2)]
    return held + near + far, last


def added(*parts):
    return sum(part.astype(jnp.float32) for part in parts).astype(jnp.bfloat16)


def stream(joined, s):
    rows = joined.shape[0] // 2
    return joined[s * rows : (s + 1) * rows]


def late_sum(late):
    came = swap_core(late[1][0])
    return [added(late[0][s], stream(came, s)) for s in range(2)]


def scatter_rows(early, late):
    last = [hop(late[s], 1, EDGES[s][1]) for s in range(2)]
    kept, near, far = (swap_core(part) for part in early[1])
    own = early[0]
    far = [hop(added(own[4 + s], stream(far, s)), 1, EDGES[s][1]) for s in range(2)]
    near = [hop(added(own[2 + s], stream(near, s), last[s]), 1, EDGES[s][0]) for s in range(2)]
    held = [added(own[s], stream(kept, s), far[s], near[s]) for s in range(2)]
    half = held[0].shape[0] // 2
    blocks = (held[0][half:], held[1][:half], held[1][half:])
    came = [hop(block, 0, flip) for block, flip in zip(blocks, DIRECT, strict=True)]
    total = held[0][:half].astype(jnp.float32)
    return sum((part.astype(jnp.float32) for part in came), total)


def swap_early(arrays):
    kept = [swap_core(part) for part in arrays[:2]]
    return kept + [swap_core(jnp.concatenate(arrays[k : k + 2], axis=0)) for k in (2, 4)]


def block_table():
    arrays = [(half, kind) for half in range(2) for kind in range(3)] + [(0, 3), (1, 3)]
    table = np.zeros((CORES, len(arrays), 2, 2, 2, 4), np.int32)
    for core, array, stream, block, request in np.ndindex(table.shape[:-1]):
        half, kind = arrays[array]
        first = ((0, 1), (3, 2))[stream][block]
        other = (0, *EDGES[stream], 2)[kind]
        y, x = (other, first) if core == half else (first, other)
        table[core, array, stream, block, request] = (y, x, half, request)
    return table.reshape(CORES, 64, 4)


def rms_scale(values, gain):
    widened = values.astype(jnp.float32)
    spread = jnp.mean(widened * widened, axis=-1, keepdims=True)
    return widened * lax.rsqrt(spread + eps_norm) * gain.astype(jnp.float32)


HIGHEST = lax.Precision.HIGHEST
NEXT_TO = (((1,), (1,)), ((), ()))


def dot32(left, right, dims=None):
    dims = dims or (((1,), (0,)), ((), ()))
    return lax.dot_general(left, right, dims, preferred_element_type=jnp.float32)


def exact_dot(left, right):
    return jnp.dot(left, right, precision=HIGHEST, preferred_element_type=jnp.float32)


def lane_spread(rows, lanes):
    return (
        lax.broadcasted_iota(jnp.int32, (rows, lanes), 0)
        == lax.broadcasted_iota(jnp.int32, (rows, lanes), 1) // SSM_DIM
    ).astype(jnp.float32)


def keeper_kernel(*refs):
    sources, (kept_ref, kept_bc_ref), held, sems = refs[:10], refs[10:12], refs[12:22], refs[22]
    copies = [
        pltpu.make_async_copy(source, target, sems.at[index])
        for index, (source, target) in enumerate(zip(sources, held, strict=True))
    ]
    for copy in copies:
        copy.start()
    for copy in copies:
        copy.wait()
    member_ref, accepted_ref, decay_ref, scaled_ref, b_ref, in_x_ref, in_bc_ref = held[:7]
    past_x_ref, past_bc_ref, state = held[7:]
    tokens, inner = scaled_ref.shape
    requests = tokens // DRAFT
    rank = lax.axis_index("mdl")

    row = lax.broadcasted_iota(jnp.int32, (tokens, 1), 0)
    time, request = row % DRAFT, row // DRAFT
    last = jnp.zeros((tokens, 1), jnp.int32)
    for r in range(requests):
        last = jnp.where(request == r, accepted_ref[r] - 1, last)
    spread_lanes = lane_spread(tokens, inner)
    log_decay, scaled_x, b_part = decay_ref[...], scaled_ref[...], b_ref[...]
    in_x, in_bc = in_x_ref[...], in_bc_ref[...]
    decay_x = exact_dot(log_decay, spread_lanes)
    other = lax.broadcasted_iota(jnp.int32, (tokens, tokens), 1)
    pick = (other == request * DRAFT + last).astype(jnp.float32)
    final_log = exact_dot(pick, log_decay)
    final_x = exact_dot(final_log, spread_lanes)
    carry_x = jnp.exp(jnp.where(time <= last, final_x - decay_x, far_below))
    carried_x = (scaled_x * carry_x).T.astype(jnp.bfloat16)
    shrink = jnp.exp(final_x).T
    for r in range(requests):
        b_here = jnp.where(request == r, b_part, jnp.zeros_like(b_part))
        kept = shrink[:, r * DRAFT : r * DRAFT + 1] * state[member_ref[r]] + dot32(
            carried_x, b_here
        )
        kept_ref[r, :inner, :] = kept.astype(jnp.bfloat16)

    def kept_rows(first_request, count, slots, series, past_of):
        at = lax.broadcasted_iota(jnp.int32, (count * slots, 1), 0)
        here, edge = at // slots, at % slots
        start = jnp.zeros((count * slots, 1), jnp.int32)
        owner = jnp.zeros((count * slots, 1), jnp.int32)
        for r in range(count):
            start = jnp.where(here == r, accepted_ref[first_request + r], start)
            owner = jnp.where(here == r, member_ref[first_request + r], owner)
        index = start + edge
        token = (here + first_request) * DRAFT + index - (CONV - 1)
        chosen = (lax.broadcasted_iota(jnp.int32, (count * slots, tokens), 1) == token) & (
            index >= CONV - 1
        )
        rows = dot32(chosen.astype(jnp.bfloat16), series)
        for p in range(PROMPTS):
            for j in range(CONV - 1):
                rows = jnp.where((owner == p) & (index == j), past_of(j, p), rows)
        return rows.astype(jnp.bfloat16)

    for lanes in range(2):
        cut = slice(lanes * STATE, min((lanes + 1) * STATE, inner))
        rows = kept_rows(
            0, requests, 8, in_x[:, cut], lambda j, p: past_x_ref[j, p : p + 1, cut].astype(jnp.float32)
        )
        for r in range(requests):
            kept_ref[r, inner + 8 * lanes : inner + 8 * (lanes + 1), : rows.shape[1]] = rows[
                r * 8 : (r + 1) * 8
            ]
    kept_ref[:, inner + 8 :, inner - STATE :] = jnp.zeros(
        (requests, 8, 2 * STATE - inner), jnp.bfloat16
    )
    kept_bc_ref[...] = kept_rows(
        rank * (requests // SIDE),
        requests // SIDE,
        8,
        in_bc,
        lambda j, p: past_bc_ref[j, p : p + 1, :].astype(jnp.float32),
    )


def keeper(member, accepted, log_decay, scaled_x, b_part, in_x, in_bc, past_x, past_bc, state):
    tokens, inner = scaled_x.shape
    requests = tokens // DRAFT
    operands = (member, accepted, log_decay, scaled_x, b_part, in_x, in_bc, past_x, past_bc, state)
    whole = pl.BlockSpec(memory_space=pltpu.VMEM)
    return pl.pallas_call(
        keeper_kernel,
        out_shape=[
            jax.ShapeDtypeStruct((requests, inner + 16, STATE), jnp.bfloat16),
            jax.ShapeDtypeStruct((requests // SIDE * 8, 2 * STATE), jnp.bfloat16),
        ],
        in_specs=[pl.BlockSpec(memory_space=pltpu.HBM)] * len(operands),
        out_specs=[whole] * 2,
        scratch_shapes=[
            *(pltpu.SMEM(a.shape, a.dtype) for a in operands[:2]),
            *(pltpu.VMEM(a.shape, a.dtype) for a in operands[2:]),
            pltpu.SemaphoreType.DMA((len(operands),)),
        ],
        compiler_params=pltpu.CompilerParams(vmem_limit_bytes=12 << 20),
        cost_estimate=pl.CostEstimate(
            flops=2_000_000_000, bytes_accessed=5_000_000, transcendentals=200_000
        ),
        name="keeper",
    )(*operands)


def unpack_kernel(kept_hbm, bc_ref, _stats, _tip, state_ref, conv_ref, kept_ref, sem):
    copy = pltpu.make_async_copy(kept_hbm, kept_ref, sem)
    copy.start()
    copy.wait()
    inner = kept_ref.shape[2] - 16
    for r in range(state_ref.shape[0]):
        for z in range(kept_ref.shape[0]):
            state_ref[r, z * inner : (z + 1) * inner, :] = kept_ref[z, r, :inner, :].astype(
                jnp.float32
            )
    for j in range(CONV - 1):
        rows = []
        for r in range(state_ref.shape[0]):
            pieces = []
            for z in range(kept_ref.shape[0]):
                tail = kept_ref[z, r, inner:, :].astype(jnp.float32)
                pieces += [tail[j : j + 1, :], tail[8 + j : 9 + j, : inner - STATE]]
            pieces.append(bc_ref[...].astype(jnp.float32)[r * 8 + j : r * 8 + j + 1, :])
            rows.append(jnp.concatenate(pieces, axis=1))
        conv_ref[j] = jnp.concatenate(rows, axis=0).astype(jnp.bfloat16)


def unpack(kept_out, own_bc, *tokens):
    sources, requests, rows, _ = kept_out.shape
    inner = rows - 16
    whole = pl.BlockSpec(memory_space=pltpu.VMEM)
    state, conv = pl.pallas_call(
        unpack_kernel,
        out_shape=[
            jax.ShapeDtypeStruct((requests, sources * inner, STATE), jnp.float32),
            jax.ShapeDtypeStruct((CONV - 1, requests, sources * inner + 2 * STATE), jnp.bfloat16),
        ],
        in_specs=[pl.BlockSpec(memory_space=pltpu.HBM), whole]
        + [pl.BlockSpec(memory_space=pl.ANY)] * len(tokens),
        out_specs=[whole] * 2,
        scratch_shapes=[pltpu.VMEM(kept_out.shape, kept_out.dtype), pltpu.SemaphoreType.DMA],
        compiler_params=pltpu.CompilerParams(vmem_limit_bytes=10 << 20),
        cost_estimate=pl.CostEstimate(flops=1_000_000, bytes_accessed=20_000_000, transcendentals=0),
        name="unpack",
    )(kept_out, own_bc, *tokens)
    return state, conv.transpose(1, 0, 2)


def mixer_kernel(*refs):
    sources, refs = refs[:22], refs[22:]
    part_refs = refs[:SIDE]
    decay_ref, scaled_ref, b_ref, in_x_ref, in_bc_ref = refs[SIDE : SIDE + 5]
    held, (mixed_scr, lanes_scr, sems) = refs[SIDE + 5 : -3], refs[-3:]
    member_ref, accepted_ref, lengths_ref, rate_ref, bias_ref, skip_ref = held[:6]
    hidden_ref, gain_ref, w_dt_ref, conv_x_ref, conv_bc_ref, past_x_ref, past_bc_ref = held[6:13]
    w_query, w_kv, prompt, w_x, w_bc, w_z, state, w_out = held[13:]
    tokens = hidden_ref.shape[0]
    requests = tokens // DRAFT
    inner = w_x.shape[1]
    heads = inner // SSM_DIM
    query_width = w_query.shape[1]
    rank = lax.axis_index("mdl")
    group = rank * (query_width // HEAD_DIM) // (Q_HEADS // KV_HEADS)
    query_hbm, kv_hbm, prompt_hbm, x_hbm, bc_hbm, z_hbm, state_hbm, attn_hbm, mamba_hbm = sources[13:]
    moves = [(source, target) for source, target in zip(sources[:13], held[:13], strict=True)]
    moves += [
        (query_hbm, w_query),
        (kv_hbm.at[group], w_kv),
        (prompt_hbm.at[0, group], prompt.at[0]),
        (prompt_hbm.at[1, group], prompt.at[1]),
        (x_hbm, w_x),
        (bc_hbm, w_bc),
        (z_hbm, w_z),
        (state_hbm, state),
        (attn_hbm, w_out.at[pl.ds(0, query_width), :]),
        (mamba_hbm, w_out.at[pl.ds(query_width, inner), :]),
    ]
    started = [
        pltpu.make_async_copy(source, target, sems.at[index])
        for index, (source, target) in enumerate(moves)
    ]
    for copy in started:
        copy.start()
    for copy in started[:13]:
        copy.wait()
    copies = started[13:]

    def head_row(ref):
        lane = lax.broadcasted_iota(jnp.int32, (1, heads), 1)
        values = jnp.zeros((1, heads), jnp.float32)
        for h in range(heads):
            values = jnp.where(lane == h, ref[h], values)
        return values

    row = lax.broadcasted_iota(jnp.int32, (tokens, 1), 0)
    time, request = row % DRAFT, row // DRAFT
    own_prompt = jnp.zeros((tokens, 1), jnp.int32)
    last = jnp.zeros((tokens, 1), jnp.int32)
    for r in range(requests):
        own_prompt = jnp.where(request == r, member_ref[r], own_prompt)
        last = jnp.where(request == r, accepted_ref[r] - 1, last)
    first_prompt = own_prompt == 0

    gain = jnp.concatenate(
        [gain_ref[j : j + 1, :].astype(jnp.float32) for j in range(gain_ref.shape[0])], axis=1
    )
    widened = hidden_ref[...].astype(jnp.float32)
    spread = jnp.mean(widened * widened, axis=-1, keepdims=True)
    normed = (
        widened * lax.rsqrt(spread + eps_norm) * gain
    ).astype(jnp.bfloat16)

    copies[0].wait()
    queries = dot32(normed, w_query[...]).astype(jnp.bfloat16)
    copies[1].wait()
    drafts = dot32(normed, w_kv[...]).astype(jnp.bfloat16)
    local_heads = query_width // HEAD_DIM
    query_rows = jnp.concatenate(
        [queries[:, h * HEAD_DIM : (h + 1) * HEAD_DIM] for h in range(local_heads)], axis=0
    )
    scale = HEAD_DIM**-0.5
    row_first = jnp.concatenate([own_prompt] * local_heads, axis=0) == 0
    draft_scores = dot32(query_rows, drafts[:, :HEAD_DIM], NEXT_TO) * scale
    same = (row // DRAFT == lax.broadcasted_iota(jnp.int32, (tokens, tokens), 1) // DRAFT) & (
        lax.broadcasted_iota(jnp.int32, (tokens, tokens), 1) <= row
    )
    draft_mask = jnp.concatenate([same] * local_heads, axis=0)
    draft_scores = jnp.where(draft_mask, draft_scores, far_below)
    copies[2].wait()
    copies[3].wait()
    scores = jnp.where(
        row_first,
        dot32(query_rows, prompt[0, :, :HEAD_DIM], NEXT_TO),
        dot32(query_rows, prompt[1, :, :HEAD_DIM], NEXT_TO),
    )
    length = jnp.where(row_first, lengths_ref[0], lengths_ref[1])
    position = lax.broadcasted_iota(jnp.int32, scores.shape, 1)
    scores = jnp.where(position < length, scores * scale, far_below)
    top = jnp.maximum(
        jnp.max(scores, axis=1, keepdims=True), jnp.max(draft_scores, axis=1, keepdims=True)
    )
    weights = jnp.exp(scores - top)
    draft_weights = jnp.exp(draft_scores - top)
    total = jnp.sum(weights, axis=1, keepdims=True) + jnp.sum(draft_weights, axis=1, keepdims=True)
    weighted = (
        dot32(jnp.where(row_first, weights, 0.0).astype(jnp.bfloat16), prompt[0, :, HEAD_DIM:])
        + dot32(jnp.where(row_first, 0.0, weights).astype(jnp.bfloat16), prompt[1, :, HEAD_DIM:])
        + dot32(draft_weights.astype(jnp.bfloat16), drafts[:, HEAD_DIM:])
    )
    attended = (weighted / total).astype(jnp.bfloat16)
    for h in range(local_heads):
        mixed_scr[:, h * HEAD_DIM : (h + 1) * HEAD_DIM] = attended[h * tokens : (h + 1) * tokens]

    def convolve_rows(series, past_ref, taps_ref):
        past = [
            jnp.where(
                first_prompt,
                past_ref[j, 0:1, :].astype(jnp.float32),
                past_ref[j, 1:2, :].astype(jnp.float32),
            )
            for j in range(CONV - 1)
        ]
        taps = taps_ref[...].astype(jnp.float32)
        summed = series * taps[CONV - 1 : CONV, :]
        for shift in range(1, CONV):
            window = pltpu.roll(series, shift, 0)
            for t in range(shift):
                window = jnp.where(time == t, past[CONV - 1 - shift + t], window)
            summed = summed + window * taps[CONV - 1 - shift : CONV - shift, :]
        return summed * jax.nn.sigmoid(summed)

    copies[4].wait()
    in_x = dot32(normed, w_x[...]).astype(jnp.bfloat16)
    heads_x = convolve_rows(in_x.astype(jnp.float32), past_x_ref, conv_x_ref)
    copies[5].wait()
    in_bc = dot32(normed, w_bc[...]).astype(jnp.bfloat16)
    conv_bcs = convolve_rows(in_bc.astype(jnp.float32), past_bc_ref, conv_bc_ref)
    b_part = conv_bcs[:, :STATE].astype(jnp.bfloat16)
    c_part = conv_bcs[:, STATE:].astype(jnp.bfloat16)

    def widen(values):
        lanes_scr[...] = jnp.zeros(lanes_scr.shape, jnp.float32)
        lanes_scr[:, :heads] = values
        return lanes_scr[...]

    spread_lanes = lane_spread(tokens, inner)
    dt_in = dot32(normed, w_dt_ref[...], NEXT_TO).astype(jnp.bfloat16).astype(jnp.float32) + head_row(bias_ref)
    step = jnp.maximum(dt_in, 0.0) + jnp.log1p(jnp.exp(-jnp.abs(dt_in)))
    log_decay = exact_dot(same.astype(jnp.float32), widen(-step * head_row(rate_ref)))
    step_x = exact_dot(widen(step), spread_lanes)
    skip_x = exact_dot(widen(jnp.broadcast_to(head_row(skip_ref), (tokens, heads))), spread_lanes)
    decay_x = exact_dot(log_decay, spread_lanes)
    turned = log_decay.T
    intersection = dot32(c_part, b_part, NEXT_TO)
    scaled_x = heads_x * step_x
    low = lax.broadcasted_iota(jnp.int32, (tokens, 2 * SSM_DIM), 1) < SSM_DIM
    groups = []
    for pair in range(heads // 2):
        mixing = []
        for h in (2 * pair, 2 * pair + 1):
            gaps = log_decay[:, h : h + 1] - turned[h : h + 1, :]
            mixing.append(
                (jnp.exp(jnp.where(same, gaps, far_below)) * intersection).astype(jnp.bfloat16)
            )
        lanes = scaled_x[:, pair * 2 * SSM_DIM : (pair + 1) * 2 * SSM_DIM]
        both = jnp.concatenate([jnp.where(low, lanes, 0.0), jnp.where(low, 0.0, lanes)], axis=0)
        groups.append(dot32(jnp.concatenate(mixing, axis=1), both.astype(jnp.bfloat16)))
    copies[7].wait()
    carried = jnp.where(
        first_prompt,
        dot32(c_part, state[0].astype(jnp.bfloat16), NEXT_TO),
        dot32(c_part, state[1].astype(jnp.bfloat16), NEXT_TO),
    )
    ssm_out = jnp.concatenate(groups, axis=1) + carried * jnp.exp(decay_x) + skip_x * heads_x
    copies[6].wait()
    gate_z = dot32(normed, w_z[...]).astype(jnp.bfloat16).astype(jnp.float32)
    mixed_scr[:, query_width:] = (ssm_out * (gate_z * jax.nn.sigmoid(gate_z))).astype(jnp.bfloat16)

    own_rows = tokens // SIDE
    copies[8].wait()
    copies[9].wait()
    rows = jnp.concatenate(
        [
            mixed_scr[pl.ds(pl.multiple_of((rank ^ flip) * own_rows, own_rows), own_rows), :]
            for flip in (0, *DIRECT)
        ],
        axis=0,
    )
    parts = dot32(rows, w_out[...]).astype(jnp.bfloat16)
    for block, part_ref in enumerate(part_refs):
        part_ref[...] = parts[block * own_rows : (block + 1) * own_rows]
    decay_ref[...] = log_decay
    scaled_ref[...] = scaled_x
    b_ref[...] = b_part
    in_x_ref[...] = in_x
    in_bc_ref[...] = in_bc


def mixer(
    hidden, mixer_gain, w_query, w_kv, w_attn_out, prompt_kv, prompt_lengths, member, accepted, w_z, w_x, w_bc,
    w_dt, conv_x, conv_bc, ssm_rate, dt_bias, skip_d, prompt_state, prompt_conv_x, prompt_conv_bc, w_mamba_out,
):
    tokens, width = hidden.shape
    inner = w_x.shape[1]
    query_width = w_query.shape[1]
    bf16 = jnp.bfloat16
    state = prompt_state.reshape(PROMPTS, inner, STATE)
    small = [
        hidden, mixer_gain.reshape(-1, 128), w_dt.T, conv_x, conv_bc,
        prompt_conv_x.transpose(1, 0, 2), prompt_conv_bc.transpose(1, 0, 2),
    ]
    scalars = [member, accepted, prompt_lengths, ssm_rate, dt_bias, skip_d]
    whole = pl.BlockSpec(memory_space=pltpu.VMEM)
    outs = pl.pallas_call(
        mixer_kernel,
        out_shape=[
            *([jax.ShapeDtypeStruct((tokens // SIDE, width), bf16)] * SIDE),
            jax.ShapeDtypeStruct((tokens, 128), jnp.float32),
            jax.ShapeDtypeStruct((tokens, inner), jnp.float32),
            jax.ShapeDtypeStruct((tokens, STATE), bf16),
            jax.ShapeDtypeStruct((tokens, inner), bf16),
            jax.ShapeDtypeStruct((tokens, 2 * STATE), bf16),
        ],
        in_specs=[pl.BlockSpec(memory_space=pltpu.HBM)] * 22,
        out_specs=[whole] * (SIDE + 5),
        scratch_shapes=[
            *(pltpu.SMEM(a.shape, a.dtype) for a in scalars),
            *(pltpu.VMEM(a.shape, a.dtype) for a in small),
            pltpu.VMEM(w_query.shape, bf16),
            pltpu.VMEM(w_kv.shape[1:], bf16),
            pltpu.VMEM((PROMPTS, *prompt_kv.shape[2:]), bf16),
            pltpu.VMEM(w_x.shape, bf16),
            pltpu.VMEM(w_bc.shape, bf16),
            pltpu.VMEM(w_z.shape, bf16),
            pltpu.VMEM(state.shape, jnp.float32),
            pltpu.VMEM((query_width + inner, width), bf16),
            pltpu.VMEM((tokens, query_width + inner), bf16),
            pltpu.VMEM((tokens, 128), jnp.float32),
            pltpu.SemaphoreType.DMA((23,)),
        ],
        compiler_params=pltpu.CompilerParams(vmem_limit_bytes=59 << 20),
        cost_estimate=pl.CostEstimate(
            flops=3_000_000_000, bytes_accessed=20_000_000, transcendentals=1_000_000
        ),
        name="mixer",
    )(
        *scalars, *small, w_query, w_kv, prompt_kv, w_x, w_bc, w_z, state, w_attn_out, w_mamba_out
    )
    return outs[:SIDE], *keeper(member, accepted, *outs[SIDE:], *small[-2:], state)


def feed_kernel(count, both_ref, down_ref, _token, *refs):
    hidden = down_ref.shape[0]
    rows_refs, out_refs = refs[:count], refs[count:]
    joined = jnp.concatenate([ref[...] for ref in rows_refs], axis=0)
    pair = dot32(joined, both_ref[...])
    gate, up = pair[:, :hidden], pair[:, hidden:]
    active = (gate * jax.nn.sigmoid(gate) * up).astype(jnp.bfloat16)
    parts = dot32(active, down_ref[...]).astype(jnp.bfloat16)
    first = 0
    for out_ref in out_refs:
        out_ref[...] = parts[first : first + out_ref.shape[0]]
        first += out_ref.shape[0]


def feed(arrays, out_rows, w_both, w_down, token):
    rows, width = sum(a.shape[0] for a in arrays), arrays[0].shape[1]
    whole = pl.BlockSpec(memory_space=pltpu.VMEM)
    return pl.pallas_call(
        functools.partial(feed_kernel, len(arrays)),
        out_shape=[jax.ShapeDtypeStruct((r, width), jnp.bfloat16) for r in out_rows],
        in_specs=[whole] * 2
        + [pl.BlockSpec(memory_space=pl.ANY)]
        + [whole] * len(arrays),
        out_specs=[whole] * len(out_rows),
        compiler_params=pltpu.CompilerParams(vmem_limit_bytes=12 << 20),
        cost_estimate=pl.CostEstimate(
            flops=4 * rows * width * 2 * 3 * w_down.shape[0],
            bytes_accessed=2 * rows * width * 2 + 3 * w_down.size * 2,
            transcendentals=rows * w_down.shape[0],
        ),
        name="feed",
    )(w_both, w_down, token, *arrays)


def head_kernel(count, targets_ref, owners_ref, *refs):
    groups, lanes = targets_ref.shape
    rows_refs, head_ref, others, out_ref = refs[:count], refs[count], refs[count + 1 : -1], refs[-1]
    vocab = head_ref.shape[0]
    devices = out_ref.shape[0]
    base = lax.axis_index("req") * vocab
    ids = lax.broadcasted_iota(jnp.int32, (vocab, lanes), 0) + base
    device = lax.broadcasted_iota(jnp.int32, (devices, lanes), 0)
    source = lax.broadcasted_iota(jnp.int32, (3 * lanes, 128), 0)
    column = lax.broadcasted_iota(jnp.int32, (3 * lanes, 128), 1)
    place = (column == source // lanes * (2 * DRAFT) + source % (2 * DRAFT)).astype(jnp.bfloat16)
    packed = jnp.zeros((devices, 128), jnp.float32)
    for other in others:
        packed = packed + other[:, 0, :]
    for group in range(groups):
        members, first = [], 0
        for ref in rows_refs:
            if group * lanes <= first < (group + 1) * lanes:
                members.append(ref[...])
            first += ref.shape[0]
        joined = jnp.concatenate(members, axis=0)
        logits = dot32(head_ref[...], joined, NEXT_TO)
        wanted = targets_ref[group : group + 1, :]
        target = jnp.sum(jnp.where(ids == wanted, logits, 0.0), axis=0, keepdims=True)
        top = jnp.max(logits, axis=0, keepdims=True)
        total = jnp.sum(jnp.exp(logits - top), axis=0, keepdims=True)
        here = device == owners_ref[group : group + 1, :]
        rest = jnp.concatenate([jnp.where(here, stat, 0.0) for stat in (top, total, target)], axis=1)
        for _ in range(3):
            part = rest.astype(jnp.bfloat16)
            packed = packed + dot32(part, place)
            rest = rest - part.astype(jnp.float32)
    out_ref[:, 0, :] = packed


def head_stats(targets, owners, rows, head_weight, devices, others=()):
    whole = pl.BlockSpec(memory_space=pltpu.VMEM)
    return pl.pallas_call(
        functools.partial(head_kernel, len(rows)),
        out_shape=jax.ShapeDtypeStruct((devices, 1, 128), jnp.float32),
        in_specs=[whole] * (3 + len(rows) + len(others)),
        out_specs=whole,
        compiler_params=pltpu.CompilerParams(vmem_limit_bytes=20 << 20),
        cost_estimate=pl.CostEstimate(
            flops=1 * 2 * targets.size * head_weight.size,
            bytes_accessed=2 * targets.size * head_weight.shape[1] + 2 * head_weight.size,
            transcendentals=targets.size * head_weight.shape[0],
        ),
        name="head_stats",
    )(targets, owners, *rows, head_weight, *others)


def shards(
    hidden_in,
    mixer_gain,
    w_query,
    w_kv,
    w_attn_out,
    prompt_kv,
    prompt_lengths,
    member,
    accepted,
    w_z,
    w_x,
    w_bc,
    w_dt,
    conv_x,
    conv_bc,
    ssm_rate,
    dt_bias,
    skip_d,
    prompt_state,
    prompt_conv_x,
    prompt_conv_bc,
    w_mamba_out,
    mlp_gain,
    w_gate,
    w_up,
    w_down,
    final_gain,
    head_weight,
    draft_ids,
):
    row_reqs, draft_len, width = hidden_in.shape
    mdl_count = lax.axis_size("mdl")
    req_count = lax.axis_size("req")
    mdl_rank = lax.axis_index("mdl")
    req_rank = lax.axis_index("req")
    row_tokens = row_reqs * draft_len
    own_reqs = row_reqs // mdl_count
    own_tokens = own_reqs * draft_len
    flat_rows = hidden_in.reshape(row_tokens, width)
    local_inner = w_x.shape[1]
    parts, kept, own_bc = mixer(
        flat_rows, mixer_gain, w_query, w_kv, w_attn_out, prompt_kv, prompt_lengths, member, accepted, w_z, w_x, w_bc,
        w_dt, conv_x, conv_bc, ssm_rate, dt_bias, skip_d, prompt_state, prompt_conv_x, prompt_conv_bc, w_mamba_out,
    )
    came = [
        lax.ppermute(part, "mdl", [(z, z ^ flip) for z in range(SIDE)])
        for part, flip in zip(parts[1:], DIRECT, strict=True)
    ]
    mixed = sum((part.astype(jnp.float32) for part in came), parts[0].astype(jnp.float32))
    own_rows = lax.dynamic_slice_in_dim(flat_rows, mdl_rank * own_tokens, own_tokens, 0)
    after_mixer = (own_rows.astype(jnp.float32) + mixed).astype(jnp.bfloat16)
    prepared = rms_scale(after_mixer, mlp_gain).astype(jnp.bfloat16)
    w_both = jnp.concatenate([w_gate, w_up], axis=1)
    early, late = gather_rows(prepared)
    early = (early, swap_early(early))
    late, own_bc = lax.optimization_barrier((late, own_bc))
    late = (late, [swap_core(part) for part in late])

    core = req_rank % CORES
    chip_x = req_rank // CORES % SIDE
    chip_y = req_rank // (CORES * SIDE)
    table = jnp.where(core == 0, jnp.asarray(block_table()[0]), jnp.asarray(block_table()[1]))
    owner = ((chip_y ^ table[:, 0]) * SIDE + (chip_x ^ table[:, 1])) * CORES + (core ^ table[:, 2])
    request = owner * row_reqs + mdl_rank * own_reqs + table[:, 3]
    next_ids = jnp.concatenate([draft_ids[:, 1:], draft_ids[:, :1]], axis=1)
    picked = (request[:, None] == jnp.arange(draft_ids.shape[0])[None, :]).astype(jnp.float32)
    targets = jnp.dot(picked, next_ids.astype(jnp.float32), precision=HIGHEST).astype(jnp.int32)
    targets = targets.reshape(1, 64 * draft_len)
    owners = jnp.broadcast_to(owner[:, None], (64, draft_len)).reshape(1, 64 * draft_len)

    half = 2 * own_tokens
    sibling_parts = feed(early[1], [2 * half] * 3, w_both, w_down, mlp_gain)
    late_parts = [
        feed(rows, out_rows, w_both, w_down, own_bc)
        for rows, out_rows in zip(late, ([half] * 2, [2 * half]), strict=True)
    ]
    late_parts = late_sum(late_parts)
    early_parts = [feed(early[0], [half] * 6, w_both, w_down, late_parts[0]), sibling_parts]
    summed = scatter_rows(early_parts, late_parts)
    tip = early_parts[0][0][:8, :128]
    kept, tip = lax.optimization_barrier((kept, tip))
    kept_out = lax.all_to_all(
        kept.reshape(mdl_count, own_reqs, local_inner + 16, STATE),
        "mdl",
        split_axis=0,
        concat_axis=0,
        tiled=True,
    )
    final_gain, targets, owners = lax.optimization_barrier((final_gain, targets, owners))
    after_feed = (after_mixer.astype(jnp.float32) + summed).astype(jnp.bfloat16)
    final_rows = rms_scale(after_feed, final_gain).astype(jnp.bfloat16)
    early, late = gather_rows(final_rows)
    sibling = swap_early(early)
    most = 6 * half
    first = head_stats(targets[:, :most], owners[:, :most], early, head_weight, req_count)
    second = head_stats(
        targets[:, most : 2 * most], owners[:, most : 2 * most], sibling, head_weight, req_count
    )
    late, first, second = lax.optimization_barrier((late, first, second))
    late = late + [swap_core(part) for part in late]
    stats = head_stats(
        targets[:, 2 * most :], owners[:, 2 * most :], late, head_weight, req_count, [first, second]
    )
    kept_state, kept_conv = unpack(kept_out, own_bc, stats, tip)
    kept_state = kept_state.reshape(own_reqs, -1, SSM_DIM, STATE)
    shared = lax.all_to_all(stats, "req", split_axis=0, concat_axis=0, tiled=True)
    tops, totals, hits = (
        shared[:, 0, kind * own_tokens : (kind + 1) * own_tokens] for kind in range(3)
    )
    top = jnp.max(tops, axis=0)
    total = jnp.sum(totals * jnp.exp(tops - top[None, :]), axis=0)
    log_total = top + jnp.log(total)
    position = jnp.arange(own_tokens) % draft_len
    verify_scores = jnp.where(
        position < draft_len - 1, jnp.sum(hits, axis=0) - log_total, top - log_total
    ).reshape(own_reqs, draft_len)
    return (
        after_feed.reshape(own_reqs, draft_len, width),
        verify_scores,
        kept_state,
        kept_conv,
    )


def solution(mesh):
    in_specs = (
        P("req", None, None),
        P(),
        P(None, "mdl"),
        P(),
        P("mdl", None),
        P("req", None, None, None),
        P("req"),
        P("req"),
        P("req"),
        P(None, "mdl"),
        P(None, "mdl"),
        P(),
        P(None, "mdl"),
        P(None, "mdl"),
        P(),
        P("mdl"),
        P("mdl"),
        P("mdl"),
        P("req", "mdl", None, None),
        P("req", None, "mdl"),
        P("req", None, None),
        P("mdl", None),
        P(),
        P(None, "req"),
        P(None, "req"),
        P("req", None),
        P(),
        P("req", None),
        P(),
    )
    out_specs = (
        P(("req", "mdl"), None, None),
        P(("req", "mdl"), None),
        P(("req", "mdl"), None, None, None),
        P(("req", "mdl"), None, None),
    )
    return jax.shard_map(shards, mesh=mesh, in_specs=in_specs, out_specs=out_specs, check_vma=False)
```
